32 devices in a mesh: dp: 16 (over z, x, core), seq: 2 (over y).
Axes of the slice: x: 2, y: 2, z: 4, core: 2. Of those that a mesh axis runs over, the one named last changes fastest.
Arguments:
- tokens: bfloat16 [32, 512, 768], P('dp', 'seq'), may hold values from -6 to 6
- cotangent: bfloat16 [32, 512, 768], P('dp', 'seq'), may hold values from -6 to 6
- lengths: int32 [32], P('dp'), may hold values from 1 to 512, 12288 in all
- query_weight: bfloat16 [768, 768], replicated, may hold values from -0.21875 to 0.21875
- query_bias: float32 [768], replicated, may hold values from -1.2 to 1.2
- key_weight: bfloat16 [768, 768], replicated, may hold values from -0.21875 to 0.21875
- value_weight: bfloat16 [768, 768], replicated, may hold values from -0.21875 to 0.21875
- value_bias: float32 [768], replicated, may hold values from -0.3 to 0.3
- mixer_weight: bfloat16 [768, 768], replicated, may hold values from -3.5 to 3.5
- mixer_bias: float32 [768], replicated, may hold values from -1.2 to 1.2
- first_gain: float32 [768], replicated, may hold values from 0.25 to 1.75
- first_bias: float32 [768], replicated, may hold values from -1.2 to 1.2
- inner_weight: bfloat16 [768, 3072], replicated, may hold values from -0.21875 to 0.21875
- inner_bias: float32 [3072], replicated, may hold values from -1.2 to 1.2
- outer_weight: bfloat16 [3072, 768], replicated, may hold values from -0.109375 to 0.109375
- outer_bias: float32 [768], replicated, may hold values from -1.2 to 1.2
- second_gain: float32 [768], replicated, may hold values from 0.25 to 1.75
- second_bias: float32 [768], replicated, may hold values from -1.2 to 1.2
Outputs:
- layer_output: float32 [32, 512, 768], P('dp', 'seq')
- input_gradient: float32 [32, 512, 768], P('dp', 'seq')
- weight_query: float32 [768, 768], P('dp', 'seq')
- weight_key: float32 [768, 768], P('dp', 'seq')
- weight_value: float32 [768, 768], P('dp', 'seq')
- weight_mixer: float32 [768, 768], P('dp', 'seq')
- weight_inner: float32 [768, 3072], P('dp', 'seq')
- weight_outer: float32 [3072, 768], P('dp', 'seq')
- bias_query: float32 [768], replicated
- bias_value: float32 [768], replicated
- bias_mixer: float32 [768], replicated
- bias_inner: float32 [3072], replicated
- bias_outer: float32 [768], replicated
- gain_first: float32 [768], replicated
- bias_first: float32 [768], replicated
- gain_second: float32 [768], replicated
- bias_second: float32 [768], replicated
The draws below stay inside these ranges and needn't reach their ends.
Inputs may be any that keep to these rules, and one draw needn't show every extreme that they name: `lengths`: positions from a slot's length to 511 are padding; some slot has exactly 512 tokens.
All inputs are finite; a program needn't handle non-finite values. No bound on the sum of `lengths` on one device may be relied on, other than what follows from the above.
Results may differ from the reference program's by a relative error of at most 0.017.
Values may be sent and summed in bfloat16 or wider, within the bound.
No kernel may reach another device: no remote copies, remote signals or barrier semaphores. Data moves between devices by JAX's collectives and lax.ppermute only.
A program may use at most 192 MiB of HBM per device.

```python
import math
import jax
import jax.numpy as jnp
import numpy as np
from jax import lax

D = 768
FF = 3072
HEADS = 12
L = 512
SEQS = 2
SEQUENCES = 32
N_DP = 16


def levels(key, shape, shards, smallest, high):
    loudness, own = 1.0, jax.random.fold_in(key, 6)
    for axis_at, shards_of in shards:
        heights = jnp.exp(jax.random.uniform(jax.random.fold_in(own, axis_at), (shards_of,), jnp.float32, smallest / len(shards), high / len(shards)))
        loudness = loudness * jnp.repeat(heights, shape[axis_at] // shards_of).reshape([-1 if axis == axis_at else 1 for axis in range(len(shape))])
    return loudness


def length_profile(amount, total, bound, slope):
    portions = [(1 << 20) // math.isqrt(standing ** slope) + 1 for standing in range(2, amount + 1)]
    surplus, given = total - bound - (amount - 1), [1] * (amount - 1)
    while surplus > 0:
        movable = [i for i in range(amount - 1) if given[i] < bound]
        pool, budget = sum([portions[i] for i in movable]), surplus
        for i in movable:
            more = min(bound - given[i], max(1, budget * portions[i] // pool), surplus)
            given[i] = given[i] + more
            surplus = surplus - more
    return np.array([bound] + given)


def uneven_parts(rng, number_of, total, reach, skew):
    if number_of == 2:
        one = jax.random.randint(rng, (), max(1, total - reach), min(reach, total - 1) + 1)
        return jnp.stack([one, total - one])
    sizes = jnp.asarray(length_profile(number_of, total, reach, skew), jnp.int32)
    twos = (number_of - 1) // 2
    giver, receiver = sizes[1:1 + 2 * twos:2], sizes[2:2 + 2 * twos:2]
    room = jnp.minimum(giver - 1, reach - receiver)
    moved = jax.random.randint(jax.random.fold_in(rng, 1), (twos,), 0, 1 << 20) % (room + 1)
    sizes = sizes.at[1:1 + 2 * twos:2].set(giver - moved).at[2:2 + 2 * twos:2].set(receiver + moved)
    return sizes[jax.random.permutation(jax.random.fold_in(rng, 2), number_of)]


def scatter_about(stream_key, extent, deviation, bound, pieces=(), kind=jnp.bfloat16):
    loudness = levels(stream_key, extent, pieces, -0.22, 0.18) if pieces else 1.0
    drawn = jax.random.normal(stream_key, extent, jnp.float32) * deviation * loudness
    return jnp.minimum(jnp.maximum(drawn, -bound), bound).astype(kind)


def setup_inputs(seed: int = 0) -> dict:
    splits = jax.random.split(jax.random.key(seed), 19)
    return {
        "tokens": scatter_about(splits[0], (SEQUENCES, L, D), 1.0, 6.0, ((0, 16), (1, 2))),
        "cotangent": scatter_about(splits[1], (SEQUENCES, L, D), 1.0, 6.0, ((0, 16), (1, 2))),
        "lengths": uneven_parts(splits[2], SEQUENCES, SEQUENCES * L * 3 // 4, L, 2).astype(jnp.int32),
        "query_weight": scatter_about(splits[3], (D, D), D ** -0.5, 0.21875),
        "query_bias": scatter_about(splits[4], (D,), 0.2, 1.2, (), jnp.float32),
        "key_weight": scatter_about(splits[5], (D, D), D ** -0.5, 0.21875),
        "value_weight": scatter_about(splits[6], (D, D), D ** -0.5, 0.21875),
        "value_bias": scatter_about(splits[7], (D,), 0.05, 0.3, (), jnp.float32),
        "mixer_weight": scatter_about(splits[8], (D, D), 3 ** -0.5, 3.5),
        "mixer_bias": scatter_about(splits[9], (D,), 0.2, 1.2, (), jnp.float32),
        "first_gain": jnp.clip(1.0 + 0.15 * jax.random.normal(splits[10], (D,), jnp.float32), 0.25, 1.75),
        "first_bias": scatter_about(splits[11], (D,), 0.2, 1.2, (), jnp.float32),
        "inner_weight": scatter_about(splits[12], (D, FF), D ** -0.5, 0.21875),
        "inner_bias": scatter_about(splits[13], (FF,), 0.2, 1.2, (), jnp.float32),
        "outer_weight": scatter_about(splits[14], (FF, D), FF ** -0.5, 0.109375),
        "outer_bias": scatter_about(splits[15], (D,), 0.2, 1.2, (), jnp.float32),
        "second_gain": jnp.clip(1.0 + 0.15 * jax.random.normal(splits[16], (D,), jnp.float32), 0.25, 1.75),
        "second_bias": scatter_about(splits[17], (D,), 0.2, 1.2, (), jnp.float32),
    }


@jax.custom_vjp
def low(v):
    return lax.optimization_barrier(v.astype(jnp.bfloat16)).astype(jnp.float32)

@jax.custom_vjp
def low_back(v):
    return v

def low_keep(v):
    return (low(v), None)

def low_pass(kept, grad):
    return (grad,)

def back_keep(v):
    return (v, None)

def back_low(kept, grad):
    return (low(grad),)
low.defvjp(low_keep, low_pass)
low_back.defvjp(back_keep, back_low)
highest = lax.Precision.HIGHEST
gelu_scale = math.sqrt(2.0 / math.pi)

def matmul(left, right):
    return jnp.dot(left, right, precision=highest)

def normalize(residue, gain, shift):
    average = lax.optimization_barrier(jnp.mean(residue, -1, keepdims=True))
    centred = residue - average
    variance = lax.optimization_barrier(jnp.mean(centred * centred, -1, keepdims=True))
    return centred * lax.rsqrt(variance + 1e-05) * gain + shift

def smooth(pre_act):
    return 0.5 * pre_act * (1.0 + jnp.tanh(gelu_scale * (pre_act + 0.044715 * pre_act * pre_act * pre_act)))

def forward(group_rows, usable, params):
    query_weight, query_bias, key_weight, value_weight, value_bias, mixer_weight, mixer_bias, first_gain, first_bias, inner_weight, inner_bias, outer_weight, outer_bias, second_gain, second_bias = params
    slots, length, breadth = group_rows.shape
    flat_rows = group_rows.reshape(slots * length, breadth)
    queries = low_back(low(matmul(flat_rows, query_weight) + query_bias))
    all_keys = low_back(low(matmul(flat_rows, key_weight)))
    all_values = low_back(low(matmul(flat_rows, value_weight) + value_bias))

    def heads_of(tensor):
        return tensor.reshape(slots, length, HEADS, breadth // HEADS)
    raw_scores = jnp.einsum('sqhd,skhd->shqk', heads_of(queries), heads_of(all_keys), precision=highest) * 0.125
    raw_scores = low_back(raw_scores)
    masked = jnp.where(usable[:, None, None, :], raw_scores, -1000000000.0)
    row_top = lax.optimization_barrier(jnp.max(masked, -1, keepdims=True))
    raised = jnp.exp(masked - row_top)
    shares = raised / lax.optimization_barrier(jnp.sum(raised, -1, keepdims=True))
    context = jnp.einsum('shqk,skhd->sqhd', low(shares), heads_of(all_values), precision=highest)
    context = low_back(low(context.reshape(slots * length, breadth)))
    mixed = low_back(matmul(context, mixer_weight) + mixer_bias)
    normed_one = normalize(flat_rows + mixed, first_gain, first_bias)
    inner_pre = low_back(matmul(low(normed_one), inner_weight) + inner_bias)
    active = low(smooth(inner_pre))
    outer_out = low_back(matmul(active, outer_weight) + outer_bias)
    result = normalize(normed_one + outer_out, second_gain, second_bias)
    return result.reshape(slots, length, breadth)

def add_up(left, right):
    return left + right

def reference(tokens, cotangent, lengths, query_weight, query_bias, key_weight, value_weight, value_bias, mixer_weight, mixer_bias, first_gain, first_bias, inner_weight, inner_bias, outer_weight, outer_bias, second_gain, second_bias):
    params = (query_weight.astype(jnp.float32), query_bias, key_weight.astype(jnp.float32), value_weight.astype(jnp.float32), value_bias, mixer_weight.astype(jnp.float32), mixer_bias, first_gain, first_bias, inner_weight.astype(jnp.float32), inner_bias, outer_weight.astype(jnp.float32), outer_bias, second_gain, second_bias)
    groups = tokens.astype(jnp.float32).reshape(N_DP, SEQS, L, D)
    tangents = cotangent.astype(jnp.float32).reshape(N_DP, SEQS, L, D)
    span_rows = lengths.astype(jnp.int32).reshape(N_DP, SEQS)

    def one_group(totals, inputs):
        group_rows, tangent, span_row = inputs
        usable = jnp.arange(L).astype(jnp.int32)[None, :] < span_row[:, None]

        def local_forward(rows_in, params_in):
            return forward(rows_in, usable, params_in)
        result, pullback = jax.vjp(local_forward, group_rows, params)
        slope_rows, slope_params = pullback(tangent)
        totals = jax.tree.map(add_up, totals, slope_params)
        return (totals, (result, slope_rows))
    zeroed = jax.tree.map(jnp.zeros_like, params)
    totals, (results, slopes) = lax.scan(one_group, zeroed, (groups, tangents, span_rows))
    return (results.reshape(SEQUENCES, L, D), slopes.reshape(SEQUENCES, L, D), totals[0], totals[2], totals[3], totals[5], totals[9], totals[11], totals[1], totals[4], totals[6], totals[10], totals[12], totals[7], totals[8], totals[13], totals[14])
```

```python
import math

import jax
import jax.numpy as jnp
from jax import lax
from jax.experimental import pallas as pl
from jax.experimental.pallas import tpu as pltpu
from jax.sharding import PartitionSpec as P

HEADS = 12
F32, BF = jnp.float32, jnp.bfloat16
NEG = -1000000000.0
GELU = math.sqrt(2.0 / math.pi)
VMEM_LIMIT = 40 << 20


def nn(a, b):
    return lax.dot_general(a, b, (((1,), (0,)), ((), ())), preferred_element_type=F32)


def nt(a, b):
    return lax.dot_general(a, b, (((1,), (1,)), ((), ())), preferred_element_type=F32)


def tn(a, b):
    return lax.dot_general(a, b, (((0,), (0,)), ((), ())), preferred_element_type=F32)


def shape(dims, dtype):
    return jax.ShapeDtypeStruct(dims, dtype)


def full(dims):
    return pl.BlockSpec(dims, lambda g, s: (0,) * len(dims))


def cols(rows, width):
    return pl.BlockSpec((rows, width), lambda g, s: (0, g))


def rows_of(height, width):
    return pl.BlockSpec((height, width), lambda g, s: (g, 0))


def own_slot(rows, width):
    return pl.BlockSpec((1, rows, width), lambda g, s: (s[0], 0, 0))


def call(body, grid, in_specs, out_specs, out_shape, scratch, name, flops, nbytes, trans=0, aliases=None):
    return pl.pallas_call(
        body,
        grid_spec=pltpu.PrefetchScalarGridSpec(
            num_scalar_prefetch=1,
            grid=grid,
            in_specs=in_specs,
            out_specs=out_specs,
            scratch_shapes=scratch,
        ),
        out_shape=out_shape,
        input_output_aliases=aliases or {},
        compiler_params=pltpu.CompilerParams(vmem_limit_bytes=VMEM_LIMIT),
        cost_estimate=pl.CostEstimate(flops=flops, bytes_accessed=nbytes, transcendentals=trans),
        name=name,
    )


def attn_fwd_body(s, own, rem, wq, wk, wv, bq, bv, wm, mb, g1, b1,
                  q_o, kt_o, v_o, e_o, il_o, ctx_o, n1_o, rs_o, nl_o, xs, mask, acc):
    g = pl.program_id(0)
    half = own.shape[1]
    length = 2 * half

    @pl.when(g == 0)
    def _():
        xs[:half] = own[0]
        xs[half:] = rem[...]
        at = lax.broadcasted_iota(jnp.int32, (length, 128), 0) + s[0] * half
        at = jnp.where(at >= length, at - length, at)
        mask[...] = jnp.where(at < s[1], 0.0, NEG)

    x = xs[...]
    q = (nn(x, wq[...]) + bq[...]).astype(BF) * BF(0.125)
    k = nn(x, wk[...]).astype(BF)
    v = (nn(x, wv[...]) + bv[...]).astype(BF)
    q_o[...] = q
    v_o[...] = v
    qt = q.T
    kt_o[...] = k.T
    vt = v.T
    zero = jnp.zeros((64, length), BF)
    outs = []
    for h in range(4):
        pair = (h // 2) * 128
        qh = qt[h * 64 : h * 64 + 64]
        qa = jnp.concatenate([qh, zero] if h % 2 == 0 else [zero, qh], 0)
        sc = nn(k[:, pair : pair + 128], qa) + mask[:, :1]
        e = jnp.exp(sc - jnp.max(sc, 0, keepdims=True))
        il = 1.0 / jnp.sum(e, 0, keepdims=True)
        low = e.astype(BF)
        e_o[h] = low
        il_o[h] = il
        outs.append(nn(vt[h * 64 : h * 64 + 64], low) * il)
    ctx = jnp.concatenate(outs, 0).astype(BF).T
    ctx_o[...] = ctx
    part = nn(ctx, wm[...])

    @pl.when(g == 0)
    def _():
        acc[...] = part

    @pl.when(g > 0)
    def _():
        acc[...] += part

    @pl.when(g == pl.num_programs(0) - 1)
    def _():
        for i in range(4):
            at = pl.ds(i * 128, 128)
            r = acc[at] + mb[...] + xs[at].astype(F32)
            c = r - jnp.mean(r, -1, keepdims=True)
            rs = lax.rsqrt(jnp.mean(c * c, -1, keepdims=True) + 1e-05)
            n = c * rs
            n1_o[at] = n
            rs_o[at] = rs
            nl_o[at] = (n * g1[...] + b1[...]).astype(BF)


def attn_fwd(s, tokens, rem, wq, wk, wv, bq, bv, wm, mb, g1, b1):
    half, d = rem.shape
    t = 2 * half
    return call(
        attn_fwd_body,
        (d // 256,),
        [own_slot(half, d), full((half, d))]
        + [cols(d, 256)] * 3
        + [cols(1, 256)] * 2
        + [rows_of(256, d)]
        + [full((1, d))] * 3,
        [
            cols(t, 256),
            rows_of(256, t),
            cols(t, 256),
            pl.BlockSpec((4, t, t), lambda g, s: (g, 0, 0)),
            pl.BlockSpec((4, 1, t), lambda g, s: (g, 0, 0)),
            cols(t, 256),
            full((t, d)),
            full((t, 1)),
            full((t, d)),
        ],
        [
            shape((t, d), BF),
            shape((d, t), BF),
            shape((t, d), BF),
            shape((HEADS, t, t), BF),
            shape((HEADS, 1, t), F32),
            shape((t, d), BF),
            shape((t, d), F32),
            shape((t, 1), F32),
            shape((t, d), BF),
        ],
        [pltpu.VMEM((t, d), BF), pltpu.VMEM((t, 128), F32), pltpu.VMEM((t, d), F32)],
        "attn_fwd",
        3_200_000_000,
        18 << 20,
        3 << 20,
    )(s, tokens, rem, wq, wk, wv, bq, bv, wm, mb, g1, b1)


def gelu_both(u):
    u2 = u * u
    a = 0.5 + 0.5 * jnp.tanh(u * (GELU + (GELU * 0.044715) * u2))
    return u * a, a + (2.0 * u) * (a * (1.0 - a)) * (GELU + (3.0 * GELU * 0.044715) * u2)


def norm_back(c, n, rs):
    return rs * (c - jnp.mean(c, -1, keepdims=True) - n * jnp.mean(c * n, -1, keepdims=True))


def mlp_fwd_body(s, nl, wi, bi, wo, bo, n1, g1, b1, g2, b2, cot_own, cot_rem,
                 act_o, dg_o, out_own, out_rem, ss_o, sl_o, vec_o, acc):
    j = pl.program_id(0)
    half = cot_rem.shape[0]
    u = nn(nl[...], wi[...]) + bi[...]
    act, slope = gelu_both(u)
    act = act.astype(BF)
    act_o[...] = act
    dg_o[...] = slope.astype(BF)
    part = nn(act, wo[...])

    @pl.when(j == 0)
    def _():
        acc[...] = part

    @pl.when(j > 0)
    def _():
        acc[...] += part

    @pl.when(j == pl.num_programs(0) - 1)
    def _():
        gain = jnp.zeros((1, nl.shape[1]), F32)
        bias, outer = gain, gain
        for i in range(4):
            at = pl.ds(i * 128, 128)
            r = acc[at] + bo[...] + (n1[at] * g1[...] + b1[...])
            c = r - jnp.mean(r, -1, keepdims=True)
            rs = lax.rsqrt(jnp.mean(c * c, -1, keepdims=True) + 1e-05)
            n = c * rs
            o = n * g2[...] + b2[...]
            if i * 128 < half:
                out_own[0, at] = o
                ct = cot_own[0, at].astype(F32)
            else:
                back = pl.ds(i * 128 - half, 128)
                out_rem[back] = o.astype(BF)
                ct = cot_rem[back].astype(F32)
            gain += jnp.sum(ct * n, 0, keepdims=True)
            bias += jnp.sum(ct, 0, keepdims=True)
            slope2 = norm_back(ct * g2[...], n, rs)
            ss_o[at] = slope2
            low = slope2.astype(BF)
            sl_o[at] = low
            outer += jnp.sum(low.astype(F32), 0, keepdims=True)
        vec_o[0:1] = gain
        vec_o[1:2] = bias
        vec_o[2:3] = outer


def mlp_fwd(s, nl, wi, bi, wo, bo, n1, g1, b1, g2, b2, cot, cot_rem):
    t, d = nl.shape
    ff = wi.shape[1]
    half = t // 2
    w = 512
    return call(
        mlp_fwd_body,
        (ff // w,),
        [full((t, d)), cols(d, w), cols(1, w), rows_of(w, d), full((1, d)), full((t, d))]
        + [full((1, d))] * 4
        + [own_slot(half, d), full((half, d))],
        [cols(t, w), cols(t, w), own_slot(half, d), full((half, d)), full((t, d)), full((t, d)), full((3, d))],
        [
            shape((t, ff), BF),
            shape((t, ff), BF),
            shape((2, half, d), F32),
            shape((half, d), BF),
            shape((t, d), F32),
            shape((t, d), BF),
            shape((3, d), F32),
        ],
        [pltpu.VMEM((t, d), F32)],
        "mlp_fwd",
        4_800_000_000,
        24 << 20,
        2 << 20,
    )(s, nl, wi, bi, wo, bo, n1, g1, b1, g2, b2, cot, cot_rem)


def mlp_bwd_body(s, sl, wo, dg, wi, ss, n1, rs, g1, si_o, sm_o, ml_o, vec_o, bi_o, acc):
    j = pl.program_id(0)
    si = (nt(sl[...], wo[...]) * dg[...].astype(F32)).astype(BF)
    si_o[...] = si
    bi_o[...] = jnp.sum(si.astype(F32), 0, keepdims=True)
    part = nt(si, wi[...])

    @pl.when(j == 0)
    def _():
        acc[...] = part

    @pl.when(j > 0)
    def _():
        acc[...] += part

    @pl.when(j == pl.num_programs(0) - 1)
    def _():
        gain = jnp.zeros((1, sl.shape[1]), F32)
        bias, mixer = gain, gain
        for i in range(4):
            at = pl.ds(i * 128, 128)
            sf = acc[at] + ss[at]
            n = n1[at]
            gain += jnp.sum(sf * n, 0, keepdims=True)
            bias += jnp.sum(sf, 0, keepdims=True)
            sm = norm_back(sf * g1[...], n, rs[at])
            sm_o[at] = sm
            low = sm.astype(BF)
            ml_o[at] = low
            mixer += jnp.sum(low.astype(F32), 0, keepdims=True)
        vec_o[0:1] = gain
        vec_o[1:2] = bias
        vec_o[2:3] = mixer


def mlp_bwd(s, sl, wo, dg, wi, ss, n1, rs, g1):
    t, d = sl.shape
    ff = wi.shape[1]
    w = 512
    return call(
        mlp_bwd_body,
        (ff // w,),
        [full((t, d)), rows_of(w, d), cols(t, w), cols(d, w), full((t, d)), full((t, d)), full((t, 1)), full((1, d))],
        [cols(t, w), full((t, d)), full((t, d)), full((3, d)), cols(1, w)],
        [shape((t, ff), BF), shape((t, d), F32), shape((t, d), BF), shape((3, d), F32), shape((1, ff), F32)],
        [pltpu.VMEM((t, d), F32)],
        "mlp_bwd",
        4_800_000_000,
        20 << 20,
    )(s, sl, wo, dg, wi, ss, n1, rs, g1)


def attn_bwd_body(s, ml, wm, q, kt, v, e, il, ctx, wq, wk, wv, sm, v2, v1, bi,
                  dq_o, dk_o, dv_o, vec_o, own_o, rem_o, acc):
    g = pl.program_id(0)
    t, d = ml.shape
    half = t // 2
    dct = nt(wm[...], ml[...]).astype(BF)
    ctxt = ctx[...].T
    zero = jnp.zeros((64, t), BF)
    lane = lax.broadcasted_iota(jnp.int32, (t, 128), 1)
    dqs, dks, dvs = [], [], []
    for pair in range(2):
        dkp = jnp.zeros((t, 128), F32)
        dvp = dkp
        at = slice(pair * 128, pair * 128 + 128)
        vp, qp = v[:, at], q[:, at]
        for one in range(2):
            h = pair * 2 + one
            sub = slice(h * 64, h * 64 + 64)
            dc = (dct[sub].astype(F32) * il[h]).astype(BF)
            da = jnp.concatenate([dc, zero] if one == 0 else [zero, dc], 0)
            delta = jnp.sum(dc.astype(F32) * ctxt[sub].astype(F32), 0, keepdims=True)
            low = e[h]
            ds = (low.astype(F32) * (nn(vp, da) - delta)).astype(BF)
            keep = (lane < 64) if one == 0 else (lane >= 64)
            dkp += nn(ds, jnp.where(keep, qp, BF(0)))
            dvp += nn(low, da.T)
            dqs.append(nn(kt[sub], ds) * 0.125)
        dks.append(dkp)
        dvs.append(dvp)
    dq = jnp.concatenate(dqs, 0).astype(BF).T
    dk = jnp.concatenate(dks, 1).astype(BF)
    dv = jnp.concatenate(dvs, 1).astype(BF)
    dq_o[...] = dq
    dk_o[...] = dk
    dv_o[...] = dv
    here = pl.ds(pl.multiple_of(g * 256, 256), 256)
    vec_o[0:1, here] = jnp.sum(dq.astype(F32), 0, keepdims=True)
    vec_o[1:2, here] = jnp.sum(dv.astype(F32), 0, keepdims=True)
    part = nt(dq, wq[...]) + nt(dk, wk[...]) + nt(dv, wv[...])

    @pl.when(g == 0)
    def _():
        acc[...] = part + sm[...]
        vec_o[2:5] = v2[...]
        vec_o[5:8] = v1[...]
        for i in range(4):
            vec_o[8 + i : 9 + i] = bi[:, i * d : i * d + d]

    @pl.when(g == 1)
    def _():
        acc[...] += part

    @pl.when(g == 2)
    def _():
        own_o[0] = acc[:half] + part[:half]
        rem_o[...] = (acc[half:] + part[half:]).astype(BF)


def attn_bwd(s, ml, wm, q, kt, v, e, il, ctx, wq, wk, wv, sm, v2, v1, bi):
    t, d = ml.shape
    half = t // 2
    return call(
        attn_bwd_body,
        (d // 256,),
        [
            full((t, d)),
            rows_of(256, d),
            cols(t, 256),
            rows_of(256, t),
            cols(t, 256),
            pl.BlockSpec((4, t, t), lambda g, s: (g, 0, 0)),
            pl.BlockSpec((4, 1, t), lambda g, s: (g, 0, 0)),
            cols(t, 256),
        ]
        + [cols(d, 256)] * 3
        + [full((t, d)), full((3, d)), full((3, d)), full((1, 4 * d))],
        [cols(t, 256)] * 3 + [full((12, d)), own_slot(half, d), full((half, d))],
        [shape((t, d), BF)] * 3 + [shape((12, d), F32), shape((2, half, d), F32), shape((half, d), BF)],
        [pltpu.VMEM((t, d), F32)],
        "attn_bwd",
        5_400_000_000,
        20 << 20,
    )(s, ml, wm, q, kt, v, e, il, ctx, wq, wk, wv, sm, v2, v1, bi)


def place(s, core, rx, ry, z1, z2):
    first = jnp.where(core == 0, rx, ry)
    second = jnp.where(core == 0, ry, rx)
    return first, second, z1 ^ s[4], z2 ^ s[5]


def flush(s, j, tile, outs, sems, jobs):
    copies = []
    for rc, out in enumerate(outs):
        core = s[2] ^ rc
        for n, (row_of, height, col, x, y, z1, z2, at) in enumerate(jobs):
            a, b, c, e = place(s, core, x ^ s[3], y ^ s[0], z1, z2)
            copies.append(
                pltpu.make_async_copy(
                    tile.at[pl.ds(pl.multiple_of(row_of(core), 16), height), pl.ds(col, 384)],
                    out.at[a, b, c, e, pl.ds(at, height)],
                    sems.at[rc * len(jobs) + n],
                )
            )
    return copies


def outer_jobs(j):
    return [
        ((lambda core, x=x: (2 * x + core) * 192), 192, 384 * y, x, y, j & 1, j >> 1, 0)
        for x in range(2)
        for y in range(2)
    ]


def thin_jobs(ys, ats):
    return [
        ((lambda core, r=r: (2 * r + core) * 48), 48, 384 * p, r & 1, ys[p], (r >> 1) & 1, r >> 2, ats[p])
        for r in range(8)
        for p in range(2)
    ]


def run_tiles(s, steps, tiles, sems, outs, compute, jobs_of):
    j = pl.program_id(0)

    def go(step, slot, wait):
        for copy in flush(s, step, tiles.at[slot], outs, sems.at[slot], jobs_of(step)):
            copy.wait() if wait else copy.start()

    slot = lax.rem(j, 2)

    @pl.when(j >= 2)
    def _():
        go(j - 2, slot, True)

    tiles[slot] = compute(j).astype(BF)
    go(j, slot, False)

    @pl.when(j == steps - 1)
    def _():
        if steps > 1:
            go(j - 1, 1 - slot, True)
        go(j, slot, True)


def outer_body(s, act, sl, keep, send, tiles, sems):
    run_tiles(s, 4, tiles, sems, (keep, send), lambda j: tn(act[...], sl[...]), outer_jobs)


def inner_body(s, nl, si, ctx, ml, keep, send, tiles, sems):
    j = pl.program_id(0)

    def jobs_of(step):
        mixer = step == 4
        base = jnp.where(mixer, 4, (step & 1) * 2) * 48
        ys = (jnp.where(mixer, 0, step >> 1), jnp.where(mixer, 1, step >> 1))
        return thin_jobs(ys, (pl.multiple_of(base, 16), pl.multiple_of(jnp.where(mixer, base, base + 48), 16)))

    def compute(_):
        return lax.cond(j == 4, lambda: tn(ctx[...], ml[...]), lambda: tn(nl[...], si[...]))

    run_tiles(s, 5, tiles, sems, (keep, send), compute, jobs_of)


def qkv_body(s, own, rem, dq, dk, dv, keep, send, tiles, sems, xs):
    j = pl.program_id(0)
    half = rem.shape[0]

    @pl.when(j == 0)
    def _():
        xs[:half] = own[0]
        xs[half:] = rem[...]

    def jobs_of(step):
        at = pl.multiple_of(step * 48, 16)
        return thin_jobs((0, 1), (at, at))

    def compute(_):
        b = jnp.where(j == 0, dq[...], jnp.where(j == 1, dk[...], dv[...]))
        return tn(xs[...], b)

    run_tiles(s, 3, tiles, sems, (keep, send), compute, jobs_of)


def weight_call(body, steps, in_specs, height, jobs, name, flops, scratch=()):
    block = (2, 2, 2, 2, height, 384)
    hbm = pl.BlockSpec(memory_space=pl.ANY)
    return call(
        body,
        (steps,),
        in_specs,
        [hbm, hbm],
        [shape(block, BF)] * 2,
        [pltpu.VMEM((2, 768, 768), BF), pltpu.SemaphoreType.DMA((2, 2 * jobs))] + list(scratch),
        name,
        flops,
        10 << 20,
    )


def finish_body(s, recv, whole, out):
    out[0] = recv[...].astype(F32)


def finish(s, recv, whole):
    half, d = recv.shape
    return call(
        finish_body,
        (1,),
        [full((half, d)), pl.BlockSpec(memory_space=pl.ANY)],
        pl.BlockSpec((1, half, d), lambda g, s: (1 - s[0], 0, 0)),
        shape(whole.shape, F32),
        [],
        "finish",
        0,
        1 << 20,
        aliases={2: 0},
    )(s, recv, whole)


def local(n, tokens, cotangent, lengths, query_weight, query_bias, key_weight, value_weight, value_bias,
          mixer_weight, mixer_bias, first_gain, first_bias, inner_weight, inner_bias, outer_weight,
          outer_bias, second_gain, second_bias):
    d = tokens.shape[2]
    low_n = n // 16
    y = lax.axis_index("seq")
    dp = lax.axis_index("dp")
    hi = dp // low_n
    mine = lax.dynamic_index_in_dim(lengths, y, 0, keepdims=False)
    s = jnp.stack([y, mine, hi & 1, (hi >> 1) & 1, (hi >> 2) & 1, (hi >> 3) & 1]).astype(jnp.int32)

    def trade(value, bit):
        if bit == "y":
            return lax.ppermute(value, "seq", [(0, 1), (1, 0)])
        return lax.ppermute(value, "dp", [(i, i ^ (bit * low_n)) for i in range(n)])

    def trade_mixed(value, first):
        pairs = []
        for i in range(n):
            for r in range(2):
                over_x = ((i // low_n) % 2 == 0) == first
                pairs.append((2 * i + r, 2 * (i ^ (2 * low_n)) + r if over_x else 2 * i + 1 - r))
        return lax.ppermute(value, ("dp", "seq"), pairs)

    rem = trade(lax.dynamic_index_in_dim(tokens, 1 - y, 0, keepdims=False), "y")
    cot_rem = trade(lax.dynamic_index_in_dim(cotangent, 1 - y, 0, keepdims=False), "y")

    def row(v):
        return v.reshape(1, -1)

    g1, b1, g2, b2 = row(first_gain), row(first_bias), row(second_gain), row(second_bias)
    q, kt, v, e, il, ctx, n1, rs, nl = attn_fwd(
        s, tokens, rem, query_weight, key_weight, value_weight, row(query_bias), row(value_bias),
        mixer_weight, row(mixer_bias), g1, b1)
    act, dg, out, out_rem, ss, sl, v2 = mlp_fwd(
        s, nl, inner_weight, row(inner_bias), outer_weight, row(outer_bias), n1, g1, b1, g2, b2,
        cotangent, cot_rem)
    t = sl.shape[0]
    half = t // 2
    piece = cols(t, 768)
    hold = full((t, d))

    def reduce(pair, height):
        keep, send = pair
        got = [keep, trade(send, 1)]

        def total(index):
            return sum(a[index[i:]].astype(F32) for a, i in zip(got, (0, 0, 1, 2, 3, 4)))

        for stage in range(4):
            out_going = total((0,) * stage + (1,)).astype(BF)
            got.append((
                lambda u: trade_mixed(u, True),
                lambda u: trade_mixed(u, False),
                lambda u: trade(u, 4),
                lambda u: trade(u, 8),
            )[stage](out_going))
        return total((0, 0, 0, 0))

    outer = reduce(
        weight_call(outer_body, 4, [piece, hold], 192, 4, "weight_outer", 2_400_000_000)(s, act, sl), 192)
    out = finish(s, trade(out_rem, "y"), out)
    si, sm, ml, v1, bi = mlp_bwd(s, sl, outer_weight, dg, inner_weight, ss, n1, rs, g1)
    inner_piece = pl.BlockSpec((t, 768), lambda g, s: (0, jnp.minimum(g, 3)))
    inner = reduce(
        weight_call(inner_body, 5, [hold, inner_piece, hold, hold], 240, 16, "weight_inner", 3_000_000_000)(
            s, nl, si, ctx, ml), 240)
    dq, dk, dv, vec, grad, grad_rem = attn_bwd(
        s, ml, mixer_weight, q, kt, v, e, il, ctx, query_weight, key_weight, value_weight, sm, v2, v1, bi)
    qkv = reduce(
        weight_call(qkv_body, 3, [own_slot(half, d), full((half, d)), hold, hold, hold], 144, 16,
                    "weight_qkv", 1_800_000_000, [pltpu.VMEM((t, d), BF)])(s, tokens, rem, dq, dk, dv), 144)
    grad = finish(s, trade(grad_rem, "y"), grad)
    for swap in (
        lambda u: trade(u, 1),
        lambda u: trade_mixed(u, True),
        lambda u: trade_mixed(u, False),
        lambda u: trade(u, 4),
        lambda u: trade(u, 8),
    ):
        vec = vec + swap(vec)

    inner_own = jnp.concatenate([inner[i * 48 : i * 48 + 48] for i in range(4)], 1)
    weights = [qkv[:48], qkv[48:96], qkv[96:], inner[192:], inner_own, outer]
    step = low_n // 2
    while step >= 1:
        bit = (dp // step) % 2
        rest = []
        for w in weights:
            two = w.reshape(2, w.shape[0] // 2, w.shape[1])
            away = lax.dynamic_index_in_dim(two, 1 - bit, 0, keepdims=False)
            near = lax.dynamic_index_in_dim(two, bit, 0, keepdims=False)
            rest.append(near + lax.ppermute(away, "dp", [(i, i ^ step) for i in range(n)]))
        weights = rest
        vec = vec + lax.ppermute(vec, "dp", [(i, i ^ step) for i in range(n)])
        step //= 2
    return (out, grad, *weights, vec[0], vec[1], vec[7], vec[8:].reshape(-1), vec[4], vec[5], vec[6], vec[2], vec[3])


def solution(mesh):
    split = P("dp", "seq", None)
    block = P("dp", "seq")
    n = mesh.shape["dp"]

    def run(*args):
        return local(n, *args)

    return jax.shard_map(
        run,
        mesh=mesh,
        in_specs=(split, split, P("dp")) + (P(),) * 15,
        out_specs=(split, split) + (block,) * 6 + (P(),) * 9,
        check_vma=False,
    )
```

```python
import functools
import math

import jax
import jax.numpy as jnp
from jax import lax
from jax.experimental import pallas as pl
from jax.experimental.pallas import tpu as pltpu
from jax.sharding import PartitionSpec as P

HEADS = 12
F32, BF = jnp.float32, jnp.bfloat16
NEG = -1000000000.0
GELU = math.sqrt(2.0 / math.pi)
VMEM_LIMIT = 20 << 20


def nn(a, b):
    return lax.dot_general(a, b, (((1,), (0,)), ((), ())), preferred_element_type=F32)


def nt(a, b):
    return lax.dot_general(a, b, (((1,), (1,)), ((), ())), preferred_element_type=F32)


def tn(a, b):
    return lax.dot_general(a, b, (((0,), (0,)), ((), ())), preferred_element_type=F32)


def shape(dims, dtype):
    return jax.ShapeDtypeStruct(dims, dtype)


def full(dims):
    return pl.BlockSpec(dims, lambda g, s: (0,) * len(dims))


def cols(rows, width):
    return pl.BlockSpec((rows, width), lambda g, s: (0, g))


def vec(width):
    return pl.BlockSpec((width,), lambda g, s: (g,))


def whole_vec(width):
    return pl.BlockSpec((width,), lambda g, s: (0,))


def lane(ref):
    return ref[...].reshape(1, -1)


def rows_of(height, width):
    return pl.BlockSpec((height, width), lambda g, s: (g, 0))


def own_slot(rows, width):
    return pl.BlockSpec((1, rows, width), lambda g, s: (s[0], 0, 0))


def call(body, grid, in_specs, out_specs, out_shape, scratch, name, flops, nbytes, trans=0, aliases=None):
    return pl.pallas_call(
        body,
        grid_spec=pltpu.PrefetchScalarGridSpec(
            num_scalar_prefetch=1,
            grid=grid,
            in_specs=in_specs,
            out_specs=out_specs,
            scratch_shapes=scratch,
        ),
        out_shape=out_shape,
        input_output_aliases=aliases or {},
        compiler_params=pltpu.CompilerParams(vmem_limit_bytes=VMEM_LIMIT),
        cost_estimate=pl.CostEstimate(flops=flops // 1000, bytes_accessed=nbytes // 1000, transcendentals=0),
        name=name,
    )


def attn_fwd_body(s, own, rem, wq, wk, wv, bq, bv, wm, mb, g1, b1,
                  q_o, kt_o, v_o, e_o, il_o, ctx_o, n1_o, rs_o, nl_o, xs, mask, acc):
    g = pl.program_id(0)
    half = own.shape[1]
    length = 2 * half

    @pl.when(g == 0)
    def _():
        xs[:half] = own[0]
        xs[half:] = rem[...]
        at = lax.broadcasted_iota(jnp.int32, (length, 128), 0) + s[0] * half
        at = jnp.where(at >= length, at - length, at)
        mask[...] = jnp.where(at < s[1], 0.0, NEG)

    x = xs[...]
    q = (nn(x, wq[...]) + lane(bq)).astype(BF) * BF(0.125)
    k = nn(x, wk[...]).astype(BF)
    v = (nn(x, wv[...]) + lane(bv)).astype(BF)
    q_o[...] = q
    v_o[...] = v
    qt = q.T
    kt_o[...] = k.T
    vt = v.T
    zero = jnp.zeros((64, length), BF)
    outs = []
    for h in range(4):
        pair = (h // 2) * 128
        qh = qt[h * 64 : h * 64 + 64]
        qa = jnp.concatenate([qh, zero] if h % 2 == 0 else [zero, qh], 0)
        sc = nn(k[:, pair : pair + 128], qa) + mask[:, :1]
        e = jnp.exp(sc - jnp.max(sc, 0, keepdims=True))
        il = 1.0 / jnp.sum(e, 0, keepdims=True)
        low = e.astype(BF)
        e_o[h] = low
        il_o[h] = il
        outs.append(nn(vt[h * 64 : h * 64 + 64], low) * il)
    ctx = jnp.concatenate(outs, 0).astype(BF).T
    ctx_o[...] = ctx
    part = nn(ctx, wm[...])

    @pl.when(g == 0)
    def _():
        acc[...] = part

    @pl.when(g > 0)
    def _():
        acc[...] += part

    @pl.when(g == pl.num_programs(0) - 1)
    def _():
        for i in range(4):
            at = pl.ds(i * 128, 128)
            r = acc[at] + lane(mb) + xs[at].astype(F32)
            c = r - jnp.mean(r, -1, keepdims=True)
            rs = lax.rsqrt(jnp.mean(c * c, -1, keepdims=True) + 1e-05)
            n = c * rs
            n1_o[at] = n
            rs_o[at] = rs
            nl_o[at] = (n * lane(g1) + lane(b1)).astype(BF)


def attn_fwd(s, tokens, rem, wq, wk, wv, bq, bv, wm, mb, g1, b1):
    half, d = rem.shape
    t = 2 * half
    return call(
        attn_fwd_body,
        (d // 256,),
        [own_slot(half, d), full((half, d))]
        + [cols(d, 256)] * 3
        + [vec(256)] * 2
        + [rows_of(256, d)]
        + [whole_vec(d)] * 3,
        [
            cols(t, 256),
            rows_of(256, t),
            cols(t, 256),
            pl.BlockSpec((4, t, t), lambda g, s: (g, 0, 0)),
            pl.BlockSpec((4, 1, t), lambda g, s: (g, 0, 0)),
            cols(t, 256),
            full((t, d)),
            full((t, 1)),
            full((t, d)),
        ],
        [
            shape((t, d), BF),
            shape((d, t), BF),
            shape((t, d), BF),
            shape((HEADS, t, t), BF),
            shape((HEADS, 1, t), F32),
            shape((t, d), BF),
            shape((t, d), F32),
            shape((t, 1), F32),
            shape((t, d), BF),
        ],
        [pltpu.VMEM((t, d), BF), pltpu.VMEM((t, 128), F32), pltpu.VMEM((t, d), F32)],
        "attn_fwd",
        3_200_000_000,
        18 << 20,
        3 << 20,
    )(s, tokens, rem, wq, wk, wv, bq, bv, wm, mb, g1, b1)


def gelu_both(u):
    u2 = u * u
    a = 0.5 + 0.5 * jnp.tanh(u * (GELU + (GELU * 0.044715) * u2))
    return u * a, a + (2.0 * u) * (a * (1.0 - a)) * (GELU + (3.0 * GELU * 0.044715) * u2)


def norm_back(c, n, rs):
    return rs * (c - jnp.mean(c, -1, keepdims=True) - n * jnp.mean(c * n, -1, keepdims=True))


def mlp_fwd_body(s, nl, wi, bi, wo, bo, n1, g1, b1, g2, b2, cot_own, cot_rem,
                 act_o, dg_o, out_own, rem0, rem1, ss_o, sl_o, vec_o, acc):
    j = pl.program_id(0)
    half = cot_rem.shape[0]
    u = nn(nl[...], wi[...]) + lane(bi)
    act, slope = gelu_both(u)
    act = act.astype(BF)
    act_o[...] = act
    dg_o[...] = slope.astype(BF)
    part = nn(act, wo[...])

    @pl.when(j == 0)
    def _():
        acc[...] = part

    @pl.when(j > 0)
    def _():
        acc[...] += part

    @pl.when(j == pl.num_programs(0) - 1)
    def _():
        gain = jnp.zeros((1, nl.shape[1]), F32)
        bias, outer = gain, gain
        for i in range(4):
            at = pl.ds(i * 128, 128)
            r = acc[at] + lane(bo) + (n1[at] * lane(g1) + lane(b1))
            c = r - jnp.mean(r, -1, keepdims=True)
            rs = lax.rsqrt(jnp.mean(c * c, -1, keepdims=True) + 1e-05)
            n = c * rs
            o = n * lane(g2) + lane(b2)
            if i * 128 < half:
                out_own[0, at] = o
                ct = cot_own[0, at].astype(F32)
            else:
                back = pl.ds(i * 128 - half, 128)
                (rem1 if i * 128 - half >= half // 2 else rem0)[...] = o.astype(BF)
                ct = cot_rem[back].astype(F32)
            gain += jnp.sum(ct * n, 0, keepdims=True)
            bias += jnp.sum(ct, 0, keepdims=True)
            slope2 = norm_back(ct * lane(g2), n, rs)
            ss_o[at] = slope2
            low = slope2.astype(BF)
            sl_o[at] = low
            outer += jnp.sum(low.astype(F32), 0, keepdims=True)
        vec_o[0:1] = gain
        vec_o[1:2] = bias
        vec_o[2:3] = outer


def mlp_fwd(s, nl, wi, bi, wo, bo, n1, g1, b1, g2, b2, cot, cot_rem):
    t, d = nl.shape
    ff = wi.shape[1]
    half = t // 2
    w = 512
    return call(
        mlp_fwd_body,
        (ff // w,),
        [full((t, d)), cols(d, w), vec(w), rows_of(w, d), whole_vec(d), full((t, d))]
        + [whole_vec(d)] * 4
        + [own_slot(half, d), full((half, d))],
        [cols(t, w), cols(t, w), own_slot(half, d)] + [full((half // 2, d))] * 2 + [full((t, d)), full((t, d)), full((3, d))],
        [
            shape((t, ff), BF),
            shape((t, ff), BF),
            shape((2, half, d), F32),
            shape((half // 2, d), BF),
            shape((half // 2, d), BF),
            shape((t, d), F32),
            shape((t, d), BF),
            shape((3, d), F32),
        ],
        [pltpu.VMEM((t, d), F32)],
        "mlp_fwd",
        4_800_000_000,
        24 << 20,
        2 << 20,
    )(s, nl, wi, bi, wo, bo, n1, g1, b1, g2, b2, cot, cot_rem)


def slope_inner_body(s, sl, wo, dg, si_o, bi_o):
    si = (nt(sl[...], wo[...]) * dg[...].astype(F32)).astype(BF)
    si_o[...] = si
    bi_o[...] = jnp.sum(si.astype(F32), 0, keepdims=True)


def slope_inner(s, sl, wo, dg):
    t, d = sl.shape
    ff = wo.shape[0]
    w = 512
    return call(
        slope_inner_body,
        (ff // w,),
        [full((t, d)), rows_of(w, d), cols(t, w)],
        [cols(t, w), cols(1, w)],
        [shape((t, ff), BF), shape((1, ff), F32)],
        [],
        "slope_inner",
        2_400_000_000,
        12 << 20,
    )(s, sl, wo, dg)


def slope_first_body(s, si, wi, ss, n1, rs, g1, sm_o, ml_o, vec_o, acc):
    j = pl.program_id(0)
    part = nt(si[...], wi[...])

    @pl.when(j == 0)
    def _():
        acc[...] = part

    @pl.when(j > 0)
    def _():
        acc[...] += part

    @pl.when(j == pl.num_programs(0) - 1)
    def _():
        gain = jnp.zeros((1, ss.shape[1]), F32)
        bias, mixer = gain, gain
        for i in range(4):
            at = pl.ds(i * 128, 128)
            sf = acc[at] + ss[at]
            n = n1[at]
            gain += jnp.sum(sf * n, 0, keepdims=True)
            bias += jnp.sum(sf, 0, keepdims=True)
            sm = norm_back(sf * lane(g1), n, rs[at])
            sm_o[at] = sm
            low = sm.astype(BF)
            ml_o[at] = low
            mixer += jnp.sum(low.astype(F32), 0, keepdims=True)
        vec_o[0:1] = gain
        vec_o[1:2] = bias
        vec_o[2:3] = mixer


def slope_first(s, si, wi, ss, n1, rs, g1):
    t, d = ss.shape
    ff = wi.shape[1]
    w = 1024
    return call(
        slope_first_body,
        (ff // w,),
        [cols(t, w), cols(d, w), full((t, d)), full((t, d)), full((t, 1)), whole_vec(d)],
        [full((t, d)), full((t, d)), full((3, d))],
        [shape((t, d), F32), shape((t, d), BF), shape((3, d), F32)],
        [pltpu.VMEM((t, d), F32)],
        "slope_first",
        2_400_000_000,
        14 << 20,
    )(s, si, wi, ss, n1, rs, g1)


def attn_bwd_body(s, ml, wm, q, kt, v, e, il, ctx, dq_o, dk_o, dv_o):
    t = ml.shape[0]
    dct = nt(wm[...], ml[...]).astype(BF)
    ctxt = ctx[...].T
    zero = jnp.zeros((64, t), BF)
    lanes = lax.broadcasted_iota(jnp.int32, (t, 128), 1)
    dqs = []
    for pair in range(2):
        dkp = jnp.zeros((t, 128), F32)
        dvp = dkp
        at = slice(pair * 128, pair * 128 + 128)
        vp, qp = v[:, at], q[:, at]
        for one in range(2):
            h = pair * 2 + one
            sub = slice(h * 64, h * 64 + 64)
            dc = (dct[sub].astype(F32) * il[h]).astype(BF)
            da = jnp.concatenate([dc, zero] if one == 0 else [zero, dc], 0)
            delta = jnp.sum(dc.astype(F32) * ctxt[sub].astype(F32), 0, keepdims=True)
            low = e[h]
            ds = (low.astype(F32) * (nn(vp, da) - delta)).astype(BF)
            keep = (lanes < 64) if one == 0 else (lanes >= 64)
            dkp += nn(ds, jnp.where(keep, qp, BF(0)))
            dvp += nn(low, da.T)
            dqs.append(nn(kt[sub], ds) * 0.125)
        dk_o[:, at] = dkp.astype(BF)
        dv_o[:, at] = dvp.astype(BF)
    dq_o[...] = jnp.concatenate(dqs, 0).astype(BF).T


def attn_bwd(g, s, ml, wm, q, kt, v, e, il, ctx):
    t, d = ml.shape

    def at_col(rows):
        return pl.BlockSpec((rows, 256), lambda i, s: (0, g))

    return call(
        attn_bwd_body,
        (1,),
        [
            full((t, d)),
            pl.BlockSpec((256, d), lambda i, s: (g, 0)),
            at_col(t),
            pl.BlockSpec((256, t), lambda i, s: (g, 0)),
            at_col(t),
            pl.BlockSpec((4, t, t), lambda i, s: (g, 0, 0)),
            pl.BlockSpec((4, 1, t), lambda i, s: (g, 0, 0)),
            at_col(t),
        ],
        [full((t, 256))] * 3,
        [shape((t, 256), BF)] * 3,
        [],
        "attn_bwd",
        1_200_000_000,
        5 << 20,
    )(s, ml, wm, q, kt, v, e, il, ctx)


def input_grad_body(s, dq0, dk0, dv0, dq1, dk1, dv1, dq2, dk2, dv2, wq, wk, wv, sm, own_o, rem_o):
    half = sm.shape[0] // 2
    w = dq0.shape[1]
    total = sm[...]
    for g, (dq, dk, dv) in enumerate(((dq0, dk0, dv0), (dq1, dk1, dv1), (dq2, dk2, dv2))):
        at = slice(g * w, g * w + w)
        total += nt(dq[...], wq[:, at]) + nt(dk[...], wk[:, at]) + nt(dv[...], wv[:, at])
    own_o[0] = total[:half]
    rem_o[...] = total[half:].astype(BF)


def input_grad(s, slopes, wq, wk, wv, sm):
    t, d = sm.shape
    half = t // 2
    return call(
        input_grad_body,
        (1,),
        [full((t, 256))] * 9 + [full((d, d))] * 3 + [full((t, d))],
        [own_slot(half, d), full((half, d))],
        [shape((2, half, d), F32), shape((half, d), BF)],
        [],
        "input_grad",
        1_800_000_000,
        8 << 20,
    )(s, *slopes, wq, wk, wv, sm)


XY = (("x", "y", "z1", "z2"), ("y", "x", "z1", "z2"))
XZY = (("x", "z1", "y", "z2"), ("y", "z1", "x", "z2"))


def place(s, core, order, x, y, z1, z2):
    far = {"x": x ^ s[3], "y": y ^ s[0], "z1": z1 ^ s[4], "z2": z2 ^ s[5]}
    return [far[p] if p == q else jnp.where(core == 0, far[p], far[q]) for p, q in zip(*order)]


def outer_jobs(s, core, j):
    for x in range(2):
        for y in range(2):
            yield place(s, core, XZY, x, y, j & 1, j >> 1), (2 * x + core) * 192, 192, y * 384, 0


def thin_jobs(s, core, ys, ats):
    for r in range(8):
        for p in range(2):
            where = place(s, core, XY, r & 1, ys[p], (r >> 1) & 1, r >> 2)
            yield where, (2 * r + core) * 48, 48, 384 * p, ats[p]


def flush(s, tile, outs, sems, jobs_of):
    copies = []
    for away, out in enumerate(outs):
        for where, row, height, col, at in jobs_of(s[2] ^ away):
            copies.append(
                pltpu.make_async_copy(
                    tile.at[pl.ds(pl.multiple_of(row, 16), height), pl.ds(col, 384)],
                    out.at[*where, pl.ds(at, height)],
                    sems.at[len(copies)],
                )
            )
    return copies


def run_tiles(s, steps, tiles, sems, outs, fill, jobs_of):
    j = pl.program_id(0)

    def go(step, slot, wait):
        for copy in flush(s, tiles.at[slot], outs, sems.at[slot], lambda core: jobs_of(core, step)):
            copy.wait() if wait else copy.start()

    slot = lax.rem(j, 2)

    @pl.when(j >= 2)
    def _():
        go(j - 2, slot, True)

    fill(j, tiles.at[slot])
    go(j, slot, False)

    @pl.when(j == steps - 1)
    def _():
        if steps > 1:
            go(j - 1, 1 - slot, True)
        go(j, slot, True)


def outer_body(s, act, sl, keep, send, tiles, sems):
    def fill(_, tile):
        tile[...] = tn(act[...], sl[...]).astype(BF)

    run_tiles(s, 4, tiles, sems, (keep, send), fill, lambda core, step: outer_jobs(s, core, step))


def inner_body(s, nl, si, keep, send, tiles, sems):
    def jobs_of(core, step):
        base = pl.multiple_of((step & 1) * 96, 16)
        return thin_jobs(s, core, (step >> 1, step >> 1), (base, pl.multiple_of(base + 48, 16)))

    def fill(_, tile):
        tile[...] = tn(nl[...], si[...]).astype(BF)

    run_tiles(s, 4, tiles, sems, (keep, send), fill, jobs_of)


def last_body(s, own, rem, dq0, dk0, dv0, dq1, dk1, dv1, dq2, dk2, dv2, ctx, ml, v2, v1, bi,
              keep, send, vec_o, tiles, sems, xs):
    half, d = rem.shape

    def put(row, value):
        vec_o[row : row + 1] = value[:, :384]
        vec_o[12 + row : 13 + row] = value[:, 384:]

    @pl.when(pl.program_id(0) == 0)
    def _():
        xs[:half] = own[0]
        xs[half:] = rem[...]
        for i in range(3):
            put(2 + i, v2[i : i + 1])
            put(5 + i, v1[i : i + 1])
        for i in range(4):
            put(8 + i, bi[:, i * d : i * d + d])
        vec_o[24:] = jnp.zeros((8, 384), F32)

    def jobs_of(core, step):
        at = pl.multiple_of(step * 48, 16)
        return thin_jobs(s, core, (0, 1), (at, at))

    def fill(j, tile):
        for one, parts in enumerate(((dq0, dq1, dq2), (dk0, dk1, dk2), (dv0, dv1, dv2))):

            @pl.when(j == one)
            def _():
                for g, part in enumerate(parts):
                    tile[:, g * 256 : g * 256 + 256] = tn(xs[...], part[...]).astype(BF)
                if one != 1:
                    ones = jnp.ones((8, 2 * half), BF)
                    put(one // 2, jnp.concatenate([nn(ones, part[...])[:1] for part in parts], 1))

        @pl.when(j == 3)
        def _():
            tile[...] = tn(ctx[...], ml[...]).astype(BF)

    run_tiles(s, 4, tiles, sems, (keep, send), fill, jobs_of)


def weight_call(body, in_specs, jobs, name, flops, scratch=(), extra=()):
    block = (2, 2, 2, 2, 192, 384)
    hbm = pl.BlockSpec(memory_space=pl.ANY)
    return call(
        body,
        (4,),
        in_specs,
        [hbm] * 2 + [full(dims) for dims in extra],
        [shape(block, BF)] * 2 + [shape(dims, F32) for dims in extra],
        [pltpu.VMEM((2, 768, 768), BF), pltpu.SemaphoreType.DMA((2, 2 * jobs))] + list(scratch),
        name,
        flops,
        10 << 20,
    )


def vec_terms(vec, vec_in):
    got = vec_in[...].astype(F32)
    return vec[...] + (got if got.shape[0] == 32 else got[:32] + got[32:])


def combine_body(counts, last, s, *refs):
    ins, vec, vec_in = refs[: sum(counts)], refs[sum(counts)], refs[sum(counts) + 1]
    outs = refs[sum(counts) + 2 :]
    at = 0
    for i, count in enumerate(counts):
        total = sum(ref[...].astype(F32) for ref in ins[at : at + count])
        at += count
        if last:
            for j in range(4):
                outs[j][...] = total[j * 48 : j * 48 + 48]
        else:
            outs[i][: total.shape[0]] = total.astype(BF)
    new = vec_terms(vec, vec_in)
    if last:
        outs[-1][:, :384] = new[:12]
        outs[-1][:, 384:] = new[12:24]
    else:
        outs[-1][...] = new
        height = outs[0].shape[0]
        high = new.astype(BF)
        outs[0][height - 64 : height - 32] = high
        outs[0][height - 32 :] = (new - high.astype(F32)).astype(BF)


def combine(s, groups, vec, vec_in, last=False):
    specs, args, outs = [], [], []
    for parts, height, at in groups:
        specs += [pl.BlockSpec((height, 384), lambda g, s, at=at: (at, 0))] * len(parts)
        args += [part.reshape(-1, 384) for part in parts]
        outs.append(shape((height, 384), BF))
    if last:
        outs = [shape((48, 384), F32)] * 4 + [shape((12, 768), F32)]
    else:
        outs[0] = shape((groups[0][1] + 64, 384), BF)
        outs.append(shape((32, 384), F32))
    rows = vec_in.shape[0]
    tail = full((32, 384)) if rows == 32 else pl.BlockSpec((64, 384), lambda g, s: (rows // 64 - 1, 0))
    return call(
        functools.partial(combine_body, [len(parts) for parts, *_ in groups], last),
        (1,),
        specs + [full((32, 384)), tail],
        [full(o.shape) for o in outs],
        outs,
        [],
        "combine",
        0,
        4 << 20,
    )(s, *args, vec, vec_in)


def finish_body(s, *refs):
    *recv, _, out = refs
    at = 0
    for part in recv:
        out[0, at : at + part.shape[0]] = part[...].astype(F32)
        at += part.shape[0]


def finish(s, recv, whole):
    half, d = whole.shape[1:]
    return call(
        finish_body,
        (1,),
        [full(part.shape) for part in recv] + [pl.BlockSpec(memory_space=pl.ANY)],
        pl.BlockSpec((1, half, d), lambda g, s: (1 - s[0], 0, 0)),
        shape(whole.shape, F32),
        [],
        "finish",
        0,
        1 << 20,
        aliases={len(recv) + 1: 0},
    )(s, *recv, whole)


def local(n, tokens, cotangent, lengths, query_weight, query_bias, key_weight, value_weight, value_bias,
          mixer_weight, mixer_bias, first_gain, first_bias, inner_weight, inner_bias, outer_weight,
          outer_bias, second_gain, second_bias):
    d = tokens.shape[2]
    low_n = n // 16
    y = lax.axis_index("seq")
    dp = lax.axis_index("dp")
    hi = dp // low_n
    mine = lax.dynamic_index_in_dim(lengths, y, 0, keepdims=False)
    s = jnp.stack([y, mine, hi & 1, (hi >> 1) & 1, (hi >> 2) & 1, (hi >> 3) & 1]).astype(jnp.int32)

    def trade(value, bit):
        if bit == "y":
            return lax.ppermute(value, "seq", [(0, 1), (1, 0)])
        return lax.ppermute(value, "dp", [(i, i ^ (bit * low_n)) for i in range(n)])

    steps = {"x": 2 * low_n, "z1": 4 * low_n, "z2": 8 * low_n}

    def trade_stage(value, orders, stage):
        pairs = []
        for i in range(n):
            bit = orders[(i // low_n) % 2][stage]
            for r in range(2):
                pairs.append((2 * i + r, 2 * i + 1 - r if bit == "y" else 2 * (i ^ steps[bit]) + r))
        return lax.ppermute(value, ("dp", "seq"), pairs)

    rem = trade(lax.dynamic_index_in_dim(tokens, 1 - y, 0, keepdims=False), "y")
    cot_rem = trade(lax.dynamic_index_in_dim(cotangent, 1 - y, 0, keepdims=False), "y")

    def after(value, *others):
        return lax.optimization_barrier((value, others))[0]

    (tokens, cotangent, query_weight, query_bias, key_weight, value_weight, value_bias, mixer_weight,
     mixer_bias, first_gain, first_bias, inner_weight, inner_bias, outer_weight, outer_bias, second_gain,
     second_bias) = [
        pltpu.with_memory_space_constraint(v, pltpu.HBM)
        for v in (tokens, cotangent, query_weight, query_bias, key_weight, value_weight, value_bias,
                  mixer_weight, mixer_bias, first_gain, first_bias, inner_weight, inner_bias, outer_weight,
                  outer_bias, second_gain, second_bias)
    ]
    g1, b1, g2, b2 = first_gain, first_bias, second_gain, second_bias
    q, kt, v, e, il, ctx, n1, rs, nl = attn_fwd(
        s, tokens, rem, query_weight, key_weight, value_weight, query_bias, value_bias,
        mixer_weight, mixer_bias, g1, b1)
    act, dg, out, out0, out1, ss, sl, v2 = mlp_fwd(
        s, nl, inner_weight, inner_bias, outer_weight, outer_bias, n1, g1, b1, g2, b2,
        cotangent, cot_rem)
    t = sl.shape[0]
    half = t // 2
    piece = cols(t, 768)
    hold = full((t, d))

    def together(*values):
        return lax.optimization_barrier(values)

    class Reduce:
        def __init__(self, made, orders):
            self.keep, self.going = made
            self.orders = orders
            self.got = [self.keep]

        def total(self, index):
            return sum(a[index[max(i - 1, 0):]].astype(F32) for i, a in enumerate(self.got))

        def add(self):
            self.going = self.total((0,) * (len(self.got) - 2) + (1,)).astype(BF)

        def away(self, value):
            stage = len(self.got) - 2
            return trade(value, 1) if stage < 0 else trade_stage(value, self.orders, stage)

        def send(self):
            self.got.append(self.away(self.going))

        def done(self):
            return self.total((0, 0, 0, 0))

    got0 = trade(out0, "y")
    r1 = Reduce(weight_call(outer_body, [piece, hold], 4, "weight_outer", 2_400_000_000)(s, act, sl), XZY)
    r1.going, got0, out1 = together(r1.going, got0, out1)
    r1.send()
    got1 = trade(out1, "y")
    si, bi = slope_inner(after(s, r1.going), sl, outer_weight, dg)

    r1.got[-1], got1, bi = together(r1.got[-1], got1, bi)
    r1.add()
    early = r1.away(r1.going[1])
    r2 = Reduce(weight_call(inner_body, [hold, piece], 16, "weight_inner", 2_400_000_000)(
        after(s, r1.going), nl, si), XY)

    early, r2.going, rest = together(early, r2.going, r1.going[0])
    late = r1.away(rest)
    r2.send()
    sm, ml, v1 = slope_first(after(s, r2.going), si, inner_weight, ss, n1, rs, g1)

    early, late, r2.got[-1], v1 = together(early, late, r2.got[-1], v1)
    r1.got.append([late, early])
    r1.total = lambda index: sum(
        (a[index[1]][index[2:]] if i == 2 else a[index[max(i - 1, 0):]]).astype(F32) for i, a in enumerate(r1.got))
    r1.add()
    r1.send()
    r2.add()
    r2.send()
    back = (mixer_weight, q, kt, v, e, il, ctx)
    first = attn_bwd(0, after(s, r1.going, r2.going), ml, *back)
    second = attn_bwd(1, after(s, first[0]), ml, *back)
    third = attn_bwd(2, after(s, second[0]), ml, *back)

    r1.got[-1], r2.got[-1], *third = together(r1.got[-1], r2.got[-1], *third)
    slopes = (*first, *second, *third)
    r1.add()
    r1.send()
    r2.add()
    r2.send()
    quarter = [full((t, 256))] * 9
    *made, vec = weight_call(
        last_body, [own_slot(half, d), full((half, d))] + quarter + [hold] * 2 + [full((3, d))] * 2 + [full((1, 4 * d))],
        16, "weight_last", 2_400_000_000, [pltpu.VMEM((t, d), BF)], [(32, 384)])(
            after(s, r1.going, r2.going), tokens, rem, *slopes, ctx, ml, v2, v1, bi)
    r3 = Reduce(made, XY)

    r1.got[-1], r2.got[-1], r3.going, vec = together(r1.got[-1], r2.got[-1], r3.going, vec)
    r1.add()
    r1.send()
    r3.send()
    vec_got = trade(vec, 1)
    grad, grad_rem = input_grad(
        after(s, r1.going, r3.going), slopes, query_weight, key_weight, value_weight, sm)

    r1.got[-1], r3.got[-1], vec_got, grad_rem, r2.got[-1] = together(
        r1.got[-1], r3.got[-1], vec_got, grad_rem, r2.got[-1])
    rows = r3.going.size // 384 // 2
    going, r2.going, vec = combine(
        s, [(r3.got, rows, 1), (r2.got, rows // 4, 1)], vec, vec_got)
    r3.got.append(r3.away(going))
    r2.send()
    outer = r1.done()
    out = finish(after(s, going), (got0, got1), out)

    r3.got[-1], r2.got[-1], out, outer = together(r3.got[-1], r2.got[-1], out, outer)
    going, r2.going, vec = combine(
        s, [(r3.got, rows // 2, 1), (r2.got, rows // 8, 1)], vec, r3.got[-1])
    r3.got.append(r3.away(going))
    r2.send()

    r3.got[-1], r2.got[-1], grad_rem = together(r3.got[-1], r2.got[-1], grad_rem)
    going, vec = combine(s, [(r3.got, rows // 4, 1)], vec, r3.got[-1])
    r3.got.append(r3.away(going))
    grad_got = trade(after(grad_rem, going), "y")
    inner = sum(u.reshape(-1, 384)[: rows // 8].astype(F32) for u in r2.got)

    r3.got[-1], inner = together(r3.got[-1], inner)
    going, vec = combine(s, [(r3.got, rows // 8, 1)], vec, r3.got[-1])
    r3.got.append(r3.away(going))
    grad = finish(after(s, going), (grad_got,), grad)

    r3.got[-1], grad = together(r3.got[-1], grad)
    *weights, vec = combine(s, [(r3.got, rows // 8, 0)], vec, r3.got[-1], last=True)

    inner_own = jnp.concatenate([inner[i * 48 : i * 48 + 48] for i in range(4)], 1)
    weights += [inner_own, outer]
    step = low_n // 2
    while step >= 1:
        bit = (dp // step) % 2
        rest = []
        for w in weights:
            two = w.reshape(2, w.shape[0] // 2, w.shape[1])
            away = lax.dynamic_index_in_dim(two, 1 - bit, 0, keepdims=False)
            near = lax.dynamic_index_in_dim(two, bit, 0, keepdims=False)
            rest.append(near + lax.ppermute(away, "dp", [(i, i ^ step) for i in range(n)]))
        weights = rest
        vec = vec + lax.ppermute(vec, "dp", [(i, i ^ step) for i in range(n)])
        step //= 2
    return (out, grad, *weights, vec[0], vec[1], vec[7], vec[8:].reshape(-1), vec[4], vec[5], vec[6], vec[2], vec[3])


def solution(mesh):
    split = P("dp", "seq", None)
    block = P("dp", "seq")
    n = mesh.shape["dp"]

    def run(*args):
        return local(n, *args)

    return jax.shard_map(
        run,
        mesh=mesh,
        in_specs=(split, split, P("dp")) + (P(),) * 15,
        out_specs=(split, split) + (block,) * 6 + (P(),) * 9,
        check_vma=False,
    )
```

```python
import functools
import math

import jax
import jax.numpy as jnp
from jax import lax
from jax.experimental import pallas as pl
from jax.experimental.pallas import tpu as pltpu
from jax.sharding import PartitionSpec as P

HEADS = 12
F32, BF = jnp.float32, jnp.bfloat16
NEG = -1000000000.0
GELU = math.sqrt(2.0 / math.pi)
VMEM_LIMIT = 20 << 20


def nn(a, b):
    return lax.dot_general(a, b, (((1,), (0,)), ((), ())), preferred_element_type=F32)


def nt(a, b):
    return lax.dot_general(a, b, (((1,), (1,)), ((), ())), preferred_element_type=F32)


def tn(a, b):
    return lax.dot_general(a, b, (((0,), (0,)), ((), ())), preferred_element_type=F32)


def shape(dims, dtype):
    return jax.ShapeDtypeStruct(dims, dtype)


def full(dims):
    return pl.BlockSpec(dims, lambda g, s: (0,) * len(dims))


def cols(rows, width):
    return pl.BlockSpec((rows, width), lambda g, s: (0, g))


def vec(width):
    return pl.BlockSpec((width,), lambda g, s: (g,))


def whole_vec(width):
    return pl.BlockSpec((width,), lambda g, s: (0,))


def lane(ref):
    return ref[...].reshape(1, -1)


def rows_of(height, width):
    return pl.BlockSpec((height, width), lambda g, s: (g, 0))


def own_slot(rows, width):
    return pl.BlockSpec((1, rows, width), lambda g, s: (s[0], 0, 0))


def call(body, grid, in_specs, out_specs, out_shape, scratch, name, flops, nbytes, trans=0, aliases=None, vmem=VMEM_LIMIT):
    return pl.pallas_call(
        body,
        grid_spec=pltpu.PrefetchScalarGridSpec(
            num_scalar_prefetch=1,
            grid=grid,
            in_specs=in_specs,
            out_specs=out_specs,
            scratch_shapes=scratch,
        ),
        out_shape=out_shape,
        input_output_aliases=aliases or {},
        compiler_params=pltpu.CompilerParams(vmem_limit_bytes=vmem),
        cost_estimate=pl.CostEstimate(flops=flops // 1000, bytes_accessed=nbytes // 1000, transcendentals=0),
        name=name,
    )


def attn_fwd_body(s, own, rem, wq, wk, wv, bq, bv, wm, mb, g1, b1,
                  q_o, kt_o, v_o, e_o, il_o, ctx_o, n1_o, rs_o, nl_o, xs, mask, acc):
    g = pl.program_id(0)
    half = own.shape[1]
    length = 2 * half

    @pl.when(g == 0)
    def _():
        xs[:half] = own[0]
        xs[half:] = rem[...]
        at = lax.broadcasted_iota(jnp.int32, (length, 128), 0) + s[0] * half
        at = jnp.where(at >= length, at - length, at)
        mask[...] = jnp.where(at < s[1], 0.0, NEG)

    x = xs[...]
    q = (nn(x, wq[...]) + lane(bq)).astype(BF) * BF(0.125)
    k = nn(x, wk[...]).astype(BF)
    v = (nn(x, wv[...]) + lane(bv)).astype(BF)
    q_o[...] = q
    v_o[...] = v
    qt = q.T
    kt_o[...] = k.T
    vt = v.T
    zero = jnp.zeros((64, length), BF)
    outs = []
    for h in range(4):
        pair = (h // 2) * 128
        qh = qt[h * 64 : h * 64 + 64]
        qa = jnp.concatenate([qh, zero] if h % 2 == 0 else [zero, qh], 0)
        sc = nn(k[:, pair : pair + 128], qa) + mask[:, :1]
        e = jnp.exp(sc - jnp.max(sc, 0, keepdims=True))
        il = 1.0 / jnp.sum(e, 0, keepdims=True)
        low = e.astype(BF)
        e_o[h] = low
        il_o[h] = il
        outs.append(nn(vt[h * 64 : h * 64 + 64], low) * il)
    ctx = jnp.concatenate(outs, 0).astype(BF).T
    ctx_o[...] = ctx
    part = nn(ctx, wm[...])

    @pl.when(g == 0)
    def _():
        acc[...] = part

    @pl.when(g > 0)
    def _():
        acc[...] += part

    @pl.when(g == pl.num_programs(0) - 1)
    def _():
        for i in range(4):
            at = pl.ds(i * 128, 128)
            r = acc[at] + lane(mb) + xs[at].astype(F32)
            c = r - jnp.mean(r, -1, keepdims=True)
            rs = lax.rsqrt(jnp.mean(c * c, -1, keepdims=True) + 1e-05)
            n = c * rs
            n1_o[at] = n
            rs_o[at] = rs
            nl_o[at] = (n * lane(g1) + lane(b1)).astype(BF)


def attn_fwd(s, tokens, rem, wq, wk, wv, bq, bv, wm, mb, g1, b1):
    half, d = rem.shape
    t = 2 * half
    return call(
        attn_fwd_body,
        (d // 256,),
        [own_slot(half, d), full((half, d))]
        + [cols(d, 256)] * 3
        + [vec(256)] * 2
        + [rows_of(256, d)]
        + [whole_vec(d)] * 3,
        [
            cols(t, 256),
            rows_of(256, t),
            cols(t, 256),
            pl.BlockSpec((4, t, t), lambda g, s: (g, 0, 0)),
            pl.BlockSpec((4, 1, t), lambda g, s: (g, 0, 0)),
            cols(t, 256),
            full((t, d)),
            full((t, 1)),
            full((t, d)),
        ],
        [
            shape((t, d), BF),
            shape((d, t), BF),
            shape((t, d), BF),
            shape((HEADS, t, t), BF),
            shape((HEADS, 1, t), F32),
            shape((t, d), BF),
            shape((t, d), F32),
            shape((t, 1), F32),
            shape((t, d), BF),
        ],
        [pltpu.VMEM((t, d), BF), pltpu.VMEM((t, 128), F32), pltpu.VMEM((t, d), F32)],
        "attn_fwd",
        3_200_000_000,
        18 << 20,
        3 << 20,
    )(s, tokens, rem, wq, wk, wv, bq, bv, wm, mb, g1, b1)


def gelu_both(u):
    u2 = u * u
    a = 0.5 + 0.5 * jnp.tanh(u * (GELU + (GELU * 0.044715) * u2))
    return u * a, a + (2.0 * u) * (a * (1.0 - a)) * (GELU + (3.0 * GELU * 0.044715) * u2)


def norm_back(c, n, rs):
    return rs * (c - jnp.mean(c, -1, keepdims=True) - n * jnp.mean(c * n, -1, keepdims=True))


def mlp_fwd_body(s, nl, wi, bi, wo, bo, n1, g1, b1, g2, b2, cot_own, cot_rem,
                 act_o, dg_o, out_own, rem0, rem1, ss_o, sl_o, vec_o, acc):
    j = pl.program_id(0)
    half = cot_rem.shape[0]
    u = nn(nl[...], wi[...]) + lane(bi)
    act, slope = gelu_both(u)
    act = act.astype(BF)
    act_o[...] = act
    dg_o[...] = slope.astype(BF)
    part = nn(act, wo[...])

    @pl.when(j == 0)
    def _():
        acc[...] = part

    @pl.when(j > 0)
    def _():
        acc[...] += part

    @pl.when(j == pl.num_programs(0) - 1)
    def _():
        gain = jnp.zeros((1, nl.shape[1]), F32)
        bias, outer = gain, gain
        for i in range(4):
            at = pl.ds(i * 128, 128)
            r = acc[at] + lane(bo) + (n1[at] * lane(g1) + lane(b1))
            c = r - jnp.mean(r, -1, keepdims=True)
            rs = lax.rsqrt(jnp.mean(c * c, -1, keepdims=True) + 1e-05)
            n = c * rs
            o = n * lane(g2) + lane(b2)
            if i * 128 < half:
                out_own[0, at] = o
                ct = cot_own[0, at].astype(F32)
            else:
                back = pl.ds(i * 128 - half, 128)
                (rem1 if i * 128 - half >= half // 2 else rem0)[...] = o.astype(BF)
                ct = cot_rem[back].astype(F32)
            gain += jnp.sum(ct * n, 0, keepdims=True)
            bias += jnp.sum(ct, 0, keepdims=True)
            slope2 = norm_back(ct * lane(g2), n, rs)
            ss_o[at] = slope2
            low = slope2.astype(BF)
            sl_o[at] = low
            outer += jnp.sum(low.astype(F32), 0, keepdims=True)
        vec_o[0:1] = gain
        vec_o[1:2] = bias
        vec_o[2:3] = outer


def mlp_fwd(s, nl, wi, bi, wo, bo, n1, g1, b1, g2, b2, cot, cot_rem):
    t, d = nl.shape
    ff = wi.shape[1]
    half = t // 2
    w = 1024
    return call(
        mlp_fwd_body,
        (ff // w,),
        [full((t, d)), cols(d, w), vec(w), rows_of(w, d), whole_vec(d), full((t, d))]
        + [whole_vec(d)] * 4
        + [own_slot(half, d), full((half, d))],
        [cols(t, w), cols(t, w), own_slot(half, d)] + [full((half // 2, d))] * 2 + [full((t, d)), full((t, d)), full((3, d))],
        [
            shape((t, ff), BF),
            shape((t, ff), BF),
            shape((2, half, d), F32),
            shape((half // 2, d), BF),
            shape((half // 2, d), BF),
            shape((t, d), F32),
            shape((t, d), BF),
            shape((3, d), F32),
        ],
        [pltpu.VMEM((t, d), F32)],
        "mlp_fwd",
        4_800_000_000,
        24 << 20,
        2 << 20,
        vmem=30 << 20,
    )(s, nl, wi, bi, wo, bo, n1, g1, b1, g2, b2, cot, cot_rem)


def slope_inner_body(s, sl, wo, dg, si_o, bi_o):
    si = (nt(sl[...], wo[...]) * dg[...].astype(F32)).astype(BF)
    si_o[...] = si
    bi_o[...] = jnp.sum(si.astype(F32), 0, keepdims=True)


def slope_inner(s, sl, wo, dg):
    t, d = sl.shape
    ff = wo.shape[0]
    w = 512
    return call(
        slope_inner_body,
        (ff // w,),
        [full((t, d)), rows_of(w, d), cols(t, w)],
        [cols(t, w), cols(1, w)],
        [shape((t, ff), BF), shape((1, ff), F32)],
        [],
        "slope_inner",
        2_400_000_000,
        12 << 20,
    )(s, sl, wo, dg)


def slope_first_body(s, si, wi, ss, n1, rs, g1, sm_o, ml_o, vec_o, acc):
    j = pl.program_id(0)
    part = nt(si[...], wi[...])

    @pl.when(j == 0)
    def _():
        acc[...] = part

    @pl.when(j > 0)
    def _():
        acc[...] += part

    @pl.when(j == pl.num_programs(0) - 1)
    def _():
        gain = jnp.zeros((1, ss.shape[1]), F32)
        bias, mixer = gain, gain
        for i in range(4):
            at = pl.ds(i * 128, 128)
            sf = acc[at] + ss[at]
            n = n1[at]
            gain += jnp.sum(sf * n, 0, keepdims=True)
            bias += jnp.sum(sf, 0, keepdims=True)
            sm = norm_back(sf * lane(g1), n, rs[at])
            sm_o[at] = sm
            low = sm.astype(BF)
            ml_o[at] = low
            mixer += jnp.sum(low.astype(F32), 0, keepdims=True)
        vec_o[0:1] = gain
        vec_o[1:2] = bias
        vec_o[2:3] = mixer


def slope_first(s, si, wi, ss, n1, rs, g1):
    t, d = ss.shape
    ff = wi.shape[1]
    w = 1024
    return call(
        slope_first_body,
        (ff // w,),
        [cols(t, w), cols(d, w), full((t, d)), full((t, d)), full((t, 1)), whole_vec(d)],
        [full((t, d)), full((t, d)), full((3, d))],
        [shape((t, d), F32), shape((t, d), BF), shape((3, d), F32)],
        [pltpu.VMEM((t, d), F32)],
        "slope_first",
        2_400_000_000,
        14 << 20,
    )(s, si, wi, ss, n1, rs, g1)


def attn_bwd_body(s, ml, wm, q, kt, v, e, il, ctx, dq_o, dk_o, dv_o):
    t = ml.shape[0]
    dct = nt(wm[...], ml[...]).astype(BF)
    ctxt = ctx[...].T
    zero = jnp.zeros((64, t), BF)
    lanes = lax.broadcasted_iota(jnp.int32, (t, 128), 1)
    dqs = []
    for pair in range(2):
        dkp = jnp.zeros((t, 128), F32)
        dvp = dkp
        at = slice(pair * 128, pair * 128 + 128)
        vp, qp = v[:, at], q[:, at]
        for one in range(2):
            h = pair * 2 + one
            sub = slice(h * 64, h * 64 + 64)
            dc = (dct[sub].astype(F32) * il[h]).astype(BF)
            da = jnp.concatenate([dc, zero] if one == 0 else [zero, dc], 0)
            delta = jnp.sum(dc.astype(F32) * ctxt[sub].astype(F32), 0, keepdims=True)
            low = e[h]
            ds = (low.astype(F32) * (nn(vp, da) - delta)).astype(BF)
            keep = (lanes < 64) if one == 0 else (lanes >= 64)
            dkp += nn(ds, jnp.where(keep, qp, BF(0)))
            dvp += nn(low, da.T)
            dqs.append(nn(kt[sub], ds) * 0.125)
        dk_o[:, at] = dkp.astype(BF)
        dv_o[:, at] = dvp.astype(BF)
    dq_o[...] = jnp.concatenate(dqs, 0).astype(BF).T


def attn_bwd(s, ml, wm, q, kt, v, e, il, ctx):
    t, d = ml.shape
    return call(
        attn_bwd_body,
        (d // 256,),
        [
            full((t, d)),
            rows_of(256, d),
            cols(t, 256),
            rows_of(256, t),
            cols(t, 256),
            pl.BlockSpec((4, t, t), lambda g, s: (g, 0, 0)),
            pl.BlockSpec((4, 1, t), lambda g, s: (g, 0, 0)),
            cols(t, 256),
        ],
        [cols(t, 256)] * 3,
        [shape((t, d), BF)] * 3,
        [],
        "attn_bwd",
        3_600_000_000,
        15 << 20,
    )(s, ml, wm, q, kt, v, e, il, ctx)


def input_grad_body(s, dq, dk, dv, wq, wk, wv, sm, own_o, rem_o):
    half = sm.shape[0] // 2
    total = sm[...] + nt(dq[...], wq[...]) + nt(dk[...], wk[...]) + nt(dv[...], wv[...])
    own_o[0] = total[:half]
    rem_o[...] = total[half:].astype(BF)


def input_grad(s, slopes, wq, wk, wv, sm):
    t, d = sm.shape
    half = t // 2
    return call(
        input_grad_body,
        (1,),
        [full((t, d))] * 3 + [full((d, d))] * 3 + [full((t, d))],
        [own_slot(half, d), full((half, d))],
        [shape((2, half, d), F32), shape((half, d), BF)],
        [],
        "input_grad",
        1_800_000_000,
        8 << 20,
    )(s, *slopes, wq, wk, wv, sm)


XY = (("x", "y", "z1", "z2"), ("y", "x", "z1", "z2"))
XZY = (("x", "z1", "y", "z2"), ("y", "z1", "x", "z2"))


def meets(s, core, a, f):
    return jnp.where(core == 0, a, f) ^ s[3], jnp.where(core == 0, f, a) ^ s[0]


def outer_jobs(s, core, j):
    for a in range(2):
        for f in range(2):
            x, y = meets(s, core, a, f)
            yield a, ((j & 1) ^ s[4], f, (j >> 1) ^ s[5]), (2 * x + core) * 192, 192, y * 384, 0


def thin_jobs(s, core, j):
    at = pl.multiple_of(j * 48, 16)
    for a in range(2):
        for f in range(2):
            x, y = meets(s, core, a, f)
            for e in range(2):
                for g in range(2):
                    row = (8 * (g ^ s[5]) + 4 * (e ^ s[4]) + 2 * x + core) * 48
                    yield a, (f, e, g), row, 48, y * 384, at


def flush(s, tile, outs, sems, jobs_of):
    copies = []
    keep, *send = outs
    for away in range(2):
        for a, rest, row, height, col, at in jobs_of(s[2] ^ away):
            where = (a, *rest)
            out = keep.at[*where]
            if away:
                split = {1: 0, 2: 1, 4: 2}[len(send)]
                index = sum(i << (split - 1 - n) for n, i in enumerate(where[:split]))
                out = send[index].at[*where[split:]]
            copies.append(
                pltpu.make_async_copy(
                    tile.at[pl.ds(pl.multiple_of(row, 16), height), pl.ds(pl.multiple_of(col, 128), 384)],
                    out.at[pl.ds(at, height)],
                    sems.at[len(copies)],
                )
            )
    return copies


def run_tiles(s, steps, tiles, sems, outs, fill, jobs_of):
    j = pl.program_id(0)

    def go(step, slot, wait):
        for copy in flush(s, tiles.at[slot], outs, sems.at[slot], lambda core: jobs_of(core, step)):
            copy.wait() if wait else copy.start()

    slot = lax.rem(j, 2)

    @pl.when(j >= 2)
    def _():
        go(j - 2, slot, True)

    fill(j, tiles.at[slot])
    go(j, slot, False)

    @pl.when(j == steps - 1)
    def _():
        if steps > 1:
            go(j - 1, 1 - slot, True)
        go(j, slot, True)


def outer_body(s, act, sl, keep, send, tiles, sems):
    def fill(_, tile):
        tile[...] = tn(act[...], sl[...]).astype(BF)

    run_tiles(s, 4, tiles, sems, (keep, send), fill, lambda core, step: outer_jobs(s, core, step))


def inner_body(s, nl, si0, si1, keep, send0, send1, tiles, sems):
    def fill(_, tile):
        tile[...] = tn(nl[...], jnp.concatenate([si0[...], si1[...]], 1)).astype(BF)

    run_tiles(s, 4, tiles, sems, (keep, send0, send1), fill, lambda core, step: thin_jobs(s, core, step))


def last_body(s, own, rem, dq, dk, dv, ctx, ml, v2, v1, bi,
              keep, send0, send1, send2, send3, vec_o, tiles, sems, xs):
    half, d = rem.shape

    def put(row, value):
        vec_o[row : row + 1] = value[:, :384]
        vec_o[12 + row : 13 + row] = value[:, 384:]

    @pl.when(pl.program_id(0) == 0)
    def _():
        xs[:half] = own[0]
        xs[half:] = rem[...]
        for i in range(3):
            put(2 + i, v2[i : i + 1])
            put(5 + i, v1[i : i + 1])
        for i in range(4):
            put(8 + i, bi[:, i * d : i * d + d])
        vec_o[24:] = jnp.zeros((8, 384), F32)

    def fill(j, tile):
        for one, part in enumerate((dq, dk, dv)):

            @pl.when(j == one)
            def _():
                tile[...] = tn(xs[...], part[...]).astype(BF)
                if one != 1:
                    put(one // 2, nn(jnp.ones((8, 2 * half), BF), part[...])[:1])

        @pl.when(j == 3)
        def _():
            tile[...] = tn(ctx[...], ml[...]).astype(BF)

    sends = (send0, send1, send2, send3)
    run_tiles(s, 4, tiles, sems, (keep, *sends), fill, lambda core, step: thin_jobs(s, core, step))


def weight_call(body, in_specs, jobs, name, flops, scratch=(), extra=(), sends=1):
    block = (2, 2, 2, 2, 192, 384)
    hbm = pl.BlockSpec(memory_space=pl.ANY)
    return call(
        body,
        (4,),
        in_specs,
        [hbm] * (1 + sends) + [full(dims) for dims in extra],
        [shape(block, BF)] + [shape(block[sends.bit_length() - 1 :], BF)] * sends + [shape(dims, F32) for dims in extra],
        [pltpu.VMEM((2, 768, 768), BF), pltpu.SemaphoreType.DMA((2, 2 * jobs))] + list(scratch),
        name,
        flops,
        10 << 20,
    )


VECTORS = (0, 1, 7, 8, 4, 5, 6, 2, 3)


def combine_body(counts, last, s, *refs):
    ins, vec, vec_in = refs[: sum(counts)], refs[sum(counts)], refs[sum(counts) + 1]
    outs = refs[sum(counts) + 2 :]
    new = vec[...] + vec_in[...].astype(F32)
    at = 0
    for i, count in enumerate(counts):
        parts = ins[at : at + count]
        at += count
        step = min(part.shape[0] for part in parts)
        for n in range(parts[0].shape[0] // step):
            rows = slice(n * step, n * step + step)
            pieces = [part for part in parts if part.shape[0] < parts[0].shape[0]]
            terms = [part[rows] for part in parts if part.shape[0] == parts[0].shape[0]]
            terms += [pieces[n][...]] if pieces else []
            total = sum(u.astype(F32) for u in terms)
            if last:
                for j in range(4):
                    outs[j][...] = total[j * 48 : j * 48 + 48]
            else:
                outs[i][rows] = total.astype(BF)
    if last and len(outs) == 5:
        outs[4][:, :384] = new[:12]
        outs[4][:, 384:] = new[12:24]
    elif last:
        for out, first in zip(outs[4:], VECTORS):
            for i in range(out.shape[0] // 768):
                out[i * 768 : i * 768 + 384] = new[first + i]
                out[i * 768 + 384 : i * 768 + 768] = new[12 + first + i]
    else:
        outs[0][outs[0].shape[0] - 32 :] = new.astype(BF)
        outs[-1][...] = new


def combine(s, groups, vec, vec_in, last=False, apart=False):
    specs, args, outs = [], [], []
    for height, parts in groups:
        for part, at in parts:
            rows = part.size // 384
            size = min(rows, height)
            specs.append(pl.BlockSpec((size, 384), lambda g, s, at=at: (at, 0)))
            args.append(part.reshape(rows, 384))
        outs.append(shape((height, 384), BF))
    if last:
        outs = [shape((48, 384), F32)] * 4
        outs += [shape((3072 if i == 8 else 768,), F32) for i in VECTORS] if apart else [shape((12, 768), F32)]
    else:
        outs[0] = shape((groups[0][0] + 32, 384), BF)
        outs.append(shape((32, 384), F32))
    rows = vec_in.shape[0]
    return call(
        functools.partial(combine_body, [len(parts) for _, parts in groups], last),
        (1,),
        specs + [full((32, 384)), pl.BlockSpec((32, 384), lambda g, s: (rows // 32 - 1, 0))],
        [whole_vec(*o.shape) if len(o.shape) == 1 else full(o.shape) for o in outs],
        outs,
        [],
        "combine",
        0,
        4 << 20,
    )(s, *args, vec, vec_in)


def finish_body(s, *refs):
    *recv, _, out = refs
    at = 0
    for part in recv:
        out[0, at : at + part.shape[0]] = part[...].astype(F32)
        at += part.shape[0]


def finish(s, recv, whole):
    half, d = whole.shape[1:]
    return call(
        finish_body,
        (1,),
        [full(part.shape) for part in recv] + [pl.BlockSpec(memory_space=pl.ANY)],
        pl.BlockSpec((1, half, d), lambda g, s: (1 - s[0], 0, 0)),
        shape(whole.shape, F32),
        [],
        "finish",
        0,
        1 << 20,
        aliases={len(recv) + 1: 0},
    )(s, *recv, whole)


def local(n, tokens, cotangent, lengths, query_weight, query_bias, key_weight, value_weight, value_bias,
          mixer_weight, mixer_bias, first_gain, first_bias, inner_weight, inner_bias, outer_weight,
          outer_bias, second_gain, second_bias):
    d = tokens.shape[2]
    low_n = n // 16
    y = lax.axis_index("seq")
    dp = lax.axis_index("dp")
    hi = dp // low_n
    mine = lax.dynamic_index_in_dim(lengths, y, 0, keepdims=False)
    s = jnp.stack([y, mine, hi & 1, (hi >> 1) & 1, (hi >> 2) & 1, (hi >> 3) & 1]).astype(jnp.int32)

    def trade(value, bit):
        if bit == "y":
            return lax.ppermute(value, "seq", [(0, 1), (1, 0)])
        return lax.ppermute(value, "dp", [(i, i ^ (bit * low_n)) for i in range(n)])

    steps = {"x": 2 * low_n, "z1": 4 * low_n, "z2": 8 * low_n}

    def trade_stage(value, orders, stage):
        pairs = []
        for i in range(n):
            bit = orders[(i // low_n) % 2][stage]
            for r in range(2):
                pairs.append((2 * i + r, 2 * i + 1 - r if bit == "y" else 2 * (i ^ steps[bit]) + r))
        return lax.ppermute(value, ("dp", "seq"), pairs)

    rem = trade(lax.dynamic_index_in_dim(tokens, 1 - y, 0, keepdims=False), "y")
    cot_rem = trade(lax.dynamic_index_in_dim(cotangent, 1 - y, 0, keepdims=False), "y")

    def after(value, *others):
        return lax.optimization_barrier((value, others))[0]

    (tokens, cotangent, query_weight, query_bias, key_weight, value_weight, value_bias, mixer_weight,
     mixer_bias, first_gain, first_bias, inner_weight, inner_bias, outer_weight, outer_bias, second_gain,
     second_bias) = [
        pltpu.with_memory_space_constraint(v, pltpu.HBM)
        for v in (tokens, cotangent, query_weight, query_bias, key_weight, value_weight, value_bias,
                  mixer_weight, mixer_bias, first_gain, first_bias, inner_weight, inner_bias, outer_weight,
                  outer_bias, second_gain, second_bias)
    ]
    g1, b1, g2, b2 = first_gain, first_bias, second_gain, second_bias
    q, kt, v, e, il, ctx, n1, rs, nl = attn_fwd(
        s, tokens, rem, query_weight, key_weight, value_weight, query_bias, value_bias,
        mixer_weight, mixer_bias, g1, b1)
    act, dg, out, out0, out1, ss, sl, v2 = mlp_fwd(
        s, nl, inner_weight, inner_bias, outer_weight, outer_bias, n1, g1, b1, g2, b2,
        cotangent, cot_rem)
    t = sl.shape[0]
    half = t // 2
    piece = cols(t, 768)
    hold = full((t, d))

    def together(*values):
        return lax.optimization_barrier(values)

    class Reduce:
        def __init__(self, made, orders):
            self.keep, self.going = made
            self.orders = orders
            self.got = [self.keep]

        def total(self, index):
            return sum(a[index[max(i - 1, 0):]].astype(F32) for i, a in enumerate(self.got))

        def add(self):
            self.going = self.total((0,) * (len(self.got) - 2) + (1,)).astype(BF)

        def away(self, value):
            stage = len(self.got) - 2
            return trade(value, 1) if stage < 0 else trade_stage(value, self.orders, stage)

        def send(self):
            self.got.append(self.away(self.going))

    got0 = trade(out0, "y")
    r1 = Reduce(weight_call(outer_body, [piece, hold], 4, "weight_outer", 2_400_000_000)(s, act, sl), XZY)
    r1.going, got0, out1 = together(r1.going, got0, out1)
    r1.send()
    got1 = trade(out1, "y")
    si, bi = slope_inner(after(s, r1.going), sl, outer_weight, dg)

    r1.got[-1], got1, bi = together(r1.got[-1], got1, bi)
    r1.add()
    r1.send()
    pieces = [pl.BlockSpec((t, 384), lambda g, s, y=y: (0, 4 * y + g)) for y in range(2)]
    keep, *parts = weight_call(inner_body, [hold] + pieces, 16, "weight_inner", 2_400_000_000, sends=2)(
        after(s, r1.going), nl, si, si)
    core = [trade(part, 1) for part in parts]
    sm, ml, v1 = slope_first(after(s, *parts), si, inner_weight, ss, n1, rs, g1)

    r1.got[-1], core[0], core[1], v1 = together(r1.got[-1], *core, v1)
    r1.add()
    r1.send()
    r2 = Reduce((keep, None), XY)
    r2.got.append(core[1])
    r2.going = (keep[1].astype(F32) + core[1].astype(F32)).astype(BF)
    r2.got[1] = core[0][None]
    r2.send()
    back = (mixer_weight, q, kt, v, e, il, ctx)
    slopes = attn_bwd(after(s, r1.going, r2.going), ml, *back)

    r1.got[-1], r2.got[-1], *slopes = together(r1.got[-1], r2.got[-1], *slopes)
    r1.add()
    r1.send()
    r2.add()
    r2.send()
    keep, *parts, vec = weight_call(
        last_body, [own_slot(half, d), full((half, d))] + [hold] * 5 + [full((3, d))] * 2 + [full((1, 4 * d))],
        16, "weight_last", 2_400_000_000, [pltpu.VMEM((t, d), BF)], [(32, 384)], sends=4)(
            after(s, r1.going, r2.going), tokens, rem, *slopes, ctx, ml, v2, v1, bi)

    def at(index, *values):
        return [(value, index) for value in values]

    r1.got[-1], parts[2], parts[3], vec = together(r1.got[-1], parts[2], parts[3], vec)
    core = [None, None, trade(parts[2], 1), trade(parts[3], 1)]
    vec_got = trade(vec, 1)

    r1.got[-1], r2.got[-1], core[2], core[3], vec_got = together(
        r1.got[-1], r2.got[-1], core[2], core[3], vec_got)
    rows = keep.size // 384 // 2
    r3 = Reduce((keep, None), XY)
    r3.got.append(None)
    going, r2.going, r1.going, vec = combine(
        s,
        [(rows, at(1, keep) + at(0, core[2], core[3])), (rows // 4, at(1, *r2.got)), (rows // 8, at(1, *r1.got))],
        vec, vec_got)
    r3.got.append(r3.away(going))
    core[:2] = [trade(after(part, going), 1) for part in parts[:2]]
    r2.send()
    r1.send()
    grad, grad_rem = input_grad(after(s, going, *parts[:2]), slopes, query_weight, key_weight, value_weight, sm)

    r3.got[-1], core[0], core[1], r2.got[-1], r1.got[-1], grad_rem = together(
        r3.got[-1], core[0], core[1], r2.got[-1], r1.got[-1], grad_rem)
    going, r2.going, vec = combine(
        s, [(rows // 2, at(1, keep, r3.got[-1]) + at(0, core[1])), (rows // 8, at(1, *r2.got))], vec, r3.got[-1])
    r3.got[1] = core[0]
    r3.got.append(r3.away(going))
    r2.send()
    outer = sum(u.reshape(-1, 384)[: rows // 8].astype(F32) for u in r1.got)
    out = finish(after(s, going, r2.going), (got0, got1), out)

    r3.got[-1], r2.got[-1], out, outer = together(r3.got[-1], r2.got[-1], out, outer)
    going, vec = combine(s, [(rows // 4, at(1, *r3.got))], vec, r3.got[-1])
    r3.got.append(r3.away(going))
    grad_got = trade(after(grad_rem, going), "y")

    going, vec = combine(s, [(rows // 8, at(1, *r3.got))], vec, r3.got[-1])
    r3.got.append(r3.away(going))
    inner = sum(after(u, going).reshape(-1, 384)[: rows // 8].astype(F32) for u in r2.got)
    grad = finish(after(s, going), (grad_got,), grad)

    inner = jnp.concatenate([inner[i * 48 : i * 48 + 48] for i in range(4)], 1)
    r3.got[-1], grad, inner = together(r3.got[-1], grad, inner)
    apart = low_n == 1
    sums = combine(s, [(rows // 8, at(0, *r3.got))], vec, r3.got[-1], last=True, apart=apart)
    weights = [*sums[:4], inner, outer]
    if apart:
        return (out, grad, *weights, *sums[4:])
    vec = sums[4]
    step = low_n // 2
    while step >= 1:
        bit = (dp // step) % 2
        rest = []
        for w in weights:
            two = w.reshape(2, w.shape[0] // 2, w.shape[1])
            away = lax.dynamic_index_in_dim(two, 1 - bit, 0, keepdims=False)
            near = lax.dynamic_index_in_dim(two, bit, 0, keepdims=False)
            rest.append(near + lax.ppermute(away, "dp", [(i, i ^ step) for i in range(n)]))
        weights = rest
        vec = vec + lax.ppermute(vec, "dp", [(i, i ^ step) for i in range(n)])
        step //= 2
    return (out, grad, *weights, *(vec[8:].reshape(-1) if i == 8 else vec[i] for i in VECTORS))


def solution(mesh):
    split = P("dp", "seq", None)
    block = P("dp", "seq")
    n = mesh.shape["dp"]

    def run(*args):
        return local(n, *args)

    return jax.shard_map(
        run,
        mesh=mesh,
        in_specs=(split, split, P("dp")) + (P(),) * 15,
        out_specs=(split, split) + (block,) * 6 + (P(),) * 9,
        check_vma=False,
    )
```

```python
import functools
import math

import jax
import jax.numpy as jnp
from jax import lax
from jax.experimental import pallas as pl
from jax.experimental.pallas import tpu as pltpu
from jax.sharding import PartitionSpec as P

HEADS = 12
F32, BF = jnp.float32, jnp.bfloat16
NEG = -1000000000.0
GELU = math.sqrt(2.0 / math.pi)
VMEM_LIMIT = 20 << 20


def nn(a, b):
    return lax.dot_general(a, b, (((1,), (0,)), ((), ())), preferred_element_type=F32)


def nt(a, b):
    return lax.dot_general(a, b, (((1,), (1,)), ((), ())), preferred_element_type=F32)


def tn(a, b):
    return lax.dot_general(a, b, (((0,), (0,)), ((), ())), preferred_element_type=F32)


def shape(dims, dtype):
    return jax.ShapeDtypeStruct(dims, dtype)


def full(dims):
    return pl.BlockSpec(dims, lambda g, s: (0,) * len(dims))


def cols(rows, width):
    return pl.BlockSpec((rows, width), lambda g, s: (0, g))


def vec(width):
    return pl.BlockSpec((width,), lambda g, s: (g,))


def whole_vec(width):
    return pl.BlockSpec((width,), lambda g, s: (0,))


def lane(ref):
    return ref[...].reshape(1, -1)


def rows_of(height, width):
    return pl.BlockSpec((height, width), lambda g, s: (g, 0))


def own_slot(rows, width):
    return pl.BlockSpec((1, rows, width), lambda g, s: (s[0], 0, 0))


def call(body, grid, in_specs, out_specs, out_shape, scratch, name, flops, nbytes, trans=0, aliases=None, vmem=VMEM_LIMIT):
    return pl.pallas_call(
        body,
        grid_spec=pltpu.PrefetchScalarGridSpec(
            num_scalar_prefetch=1,
            grid=grid,
            in_specs=in_specs,
            out_specs=out_specs,
            scratch_shapes=scratch,
        ),
        out_shape=out_shape,
        input_output_aliases=aliases or {},
        compiler_params=pltpu.CompilerParams(vmem_limit_bytes=vmem),
        cost_estimate=pl.CostEstimate(flops=flops // 1000, bytes_accessed=nbytes // 1000, transcendentals=0),
        name=name,
    )


def attn_fwd_body(s, own, rem, wq, wk, wv, bq, bv, wm, mb, g1, b1,
                  q_o, kt_o, v_o, e_o, il_o, ctx_o, n1_o, rs_o, nl_o, xs, mask, acc):
    g = pl.program_id(0)
    half = own.shape[1]
    length = 2 * half

    @pl.when(g == 0)
    def _():
        xs[:half] = own[0]
        xs[half:] = rem[...]
        at = lax.broadcasted_iota(jnp.int32, (length, 128), 0) + s[0] * half
        at = jnp.where(at >= length, at - length, at)
        mask[...] = jnp.where(at < s[1], 0.0, NEG)

    x = xs[...]
    q = (nn(x, wq[...]) + lane(bq)).astype(BF) * BF(0.125)
    k = nn(x, wk[...]).astype(BF)
    v = (nn(x, wv[...]) + lane(bv)).astype(BF)
    q_o[...] = q
    v_o[...] = v
    qt = q.T
    kt_o[...] = k.T
    vt = v.T
    zero = jnp.zeros((64, length), BF)
    outs = []
    for h in range(4):
        pair = (h // 2) * 128
        qh = qt[h * 64 : h * 64 + 64]
        qa = jnp.concatenate([qh, zero] if h % 2 == 0 else [zero, qh], 0)
        sc = nn(k[:, pair : pair + 128], qa) + mask[:, :1]
        e = jnp.exp(sc - jnp.max(sc, 0, keepdims=True))
        il = 1.0 / jnp.sum(e, 0, keepdims=True)
        low = e.astype(BF)
        e_o[h] = low
        il_o[h] = il
        outs.append(nn(vt[h * 64 : h * 64 + 64], low) * il)
    ctx = jnp.concatenate(outs, 0).astype(BF).T
    ctx_o[...] = ctx
    part = nn(ctx, wm[...])

    @pl.when(g == 0)
    def _():
        acc[...] = part

    @pl.when(g > 0)
    def _():
        acc[...] += part

    @pl.when(g == pl.num_programs(0) - 1)
    def _():
        for i in range(4):
            at = pl.ds(i * 128, 128)
            r = acc[at] + lane(mb) + xs[at].astype(F32)
            c = r - jnp.mean(r, -1, keepdims=True)
            rs = lax.rsqrt(jnp.mean(c * c, -1, keepdims=True) + 1e-05)
            n = c * rs
            n1_o[at] = n
            rs_o[at] = rs
            nl_o[at] = (n * lane(g1) + lane(b1)).astype(BF)


def attn_fwd(s, tokens, rem, wq, wk, wv, bq, bv, wm, mb, g1, b1):
    half, d = rem.shape
    t = 2 * half
    return call(
        attn_fwd_body,
        (d // 256,),
        [own_slot(half, d), full((half, d))]
        + [cols(d, 256)] * 3
        + [vec(256)] * 2
        + [rows_of(256, d)]
        + [whole_vec(d)] * 3,
        [
            cols(t, 256),
            rows_of(256, t),
            cols(t, 256),
            pl.BlockSpec((4, t, t), lambda g, s: (g, 0, 0)),
            pl.BlockSpec((4, 1, t), lambda g, s: (g, 0, 0)),
            cols(t, 256),
            full((t, d)),
            full((t, 1)),
            full((t, d)),
        ],
        [
            shape((t, d), BF),
            shape((d, t), BF),
            shape((t, d), BF),
            shape((HEADS, t, t), BF),
            shape((HEADS, 1, t), F32),
            shape((t, d), BF),
            shape((t, d), F32),
            shape((t, 1), F32),
            shape((t, d), BF),
        ],
        [pltpu.VMEM((t, d), BF), pltpu.VMEM((t, 128), F32), pltpu.VMEM((t, d), F32)],
        "attn_fwd",
        3_200_000_000,
        18 << 20,
        3 << 20,
    )(s, tokens, rem, wq, wk, wv, bq, bv, wm, mb, g1, b1)


def gelu_both(u):
    u2 = u * u
    a = 0.5 + 0.5 * jnp.tanh(u * (GELU + (GELU * 0.044715) * u2))
    return u * a, a + (2.0 * u) * (a * (1.0 - a)) * (GELU + (3.0 * GELU * 0.044715) * u2)


def norm_back(c, n, rs):
    return rs * (c - jnp.mean(c, -1, keepdims=True) - n * jnp.mean(c * n, -1, keepdims=True))


def mlp_fwd_body(s, nl, wi, bi, wo, bo, n1, g1, b1, g2, b2, cot_own, cot_rem,
                 act_o, dg_o, out_own, rem0, rem1, ss_o, sl_o, vec_o, acc):
    j = pl.program_id(0)
    half = cot_rem.shape[0]
    u = nn(nl[...], wi[...]) + lane(bi)
    act, slope = gelu_both(u)
    act = act.astype(BF)
    act_o[...] = act
    dg_o[...] = slope.astype(BF)
    part = nn(act, wo[...])

    @pl.when(j == 0)
    def _():
        acc[...] = part

    @pl.when(j > 0)
    def _():
        acc[...] += part

    @pl.when(j == pl.num_programs(0) - 1)
    def _():
        gain = jnp.zeros((1, nl.shape[1]), F32)
        bias, outer = gain, gain
        for i in range(4):
            at = pl.ds(i * 128, 128)
            r = acc[at] + lane(bo) + (n1[at] * lane(g1) + lane(b1))
            c = r - jnp.mean(r, -1, keepdims=True)
            rs = lax.rsqrt(jnp.mean(c * c, -1, keepdims=True) + 1e-05)
            n = c * rs
            o = n * lane(g2) + lane(b2)
            if i * 128 < half:
                out_own[0, at] = o
                ct = cot_own[0, at].astype(F32)
            else:
                back = pl.ds(i * 128 - half, 128)
                (rem1 if i * 128 - half >= half // 2 else rem0)[...] = o.astype(BF)
                ct = cot_rem[back].astype(F32)
            gain += jnp.sum(ct * n, 0, keepdims=True)
            bias += jnp.sum(ct, 0, keepdims=True)
            slope2 = norm_back(ct * lane(g2), n, rs)
            ss_o[at] = slope2
            low = slope2.astype(BF)
            sl_o[at] = low
            outer += jnp.sum(low.astype(F32), 0, keepdims=True)
        vec_o[0:1] = gain
        vec_o[1:2] = bias
        vec_o[2:3] = outer


def mlp_fwd(s, nl, wi, bi, wo, bo, n1, g1, b1, g2, b2, cot, cot_rem):
    t, d = nl.shape
    ff = wi.shape[1]
    half = t // 2
    w = 1024
    return call(
        mlp_fwd_body,
        (ff // w,),
        [full((t, d)), cols(d, w), vec(w), rows_of(w, d), whole_vec(d), full((t, d))]
        + [whole_vec(d)] * 4
        + [own_slot(half, d), full((half, d))],
        [cols(t, w), cols(t, w), own_slot(half, d)] + [full((half // 2, d))] * 2 + [full((t, d)), full((t, d)), full((3, d))],
        [
            shape((t, ff), BF),
            shape((t, ff), BF),
            shape((2, half, d), F32),
            shape((half // 2, d), BF),
            shape((half // 2, d), BF),
            shape((t, d), F32),
            shape((t, d), BF),
            shape((3, d), F32),
        ],
        [pltpu.VMEM((t, d), F32)],
        "mlp_fwd",
        4_800_000_000,
        24 << 20,
        2 << 20,
        vmem=30 << 20,
    )(s, nl, wi, bi, wo, bo, n1, g1, b1, g2, b2, cot, cot_rem)


def slope_inner_body(s, sl, wo, dg, si_o, bi_o):
    si = (nt(sl[...], wo[...]) * dg[...].astype(F32)).astype(BF)
    si_o[...] = si
    bi_o[...] = jnp.sum(si.astype(F32), 0, keepdims=True)


def slope_inner(s, sl, wo, dg):
    t, d = sl.shape
    ff = wo.shape[0]
    w = 512
    return call(
        slope_inner_body,
        (ff // w,),
        [full((t, d)), rows_of(w, d), cols(t, w)],
        [cols(t, w), cols(1, w)],
        [shape((t, ff), BF), shape((1, ff), F32)],
        [],
        "slope_inner",
        2_400_000_000,
        12 << 20,
    )(s, sl, wo, dg)


def slope_first_body(s, si, wi, ss, n1, rs, g1, sm_o, ml_o, vec_o, acc):
    j = pl.program_id(0)
    part = nt(si[...], wi[...])

    @pl.when(j == 0)
    def _():
        acc[...] = part

    @pl.when(j > 0)
    def _():
        acc[...] += part

    @pl.when(j == pl.num_programs(0) - 1)
    def _():
        gain = jnp.zeros((1, ss.shape[1]), F32)
        bias, mixer = gain, gain
        for i in range(4):
            at = pl.ds(i * 128, 128)
            sf = acc[at] + ss[at]
            n = n1[at]
            gain += jnp.sum(sf * n, 0, keepdims=True)
            bias += jnp.sum(sf, 0, keepdims=True)
            sm = norm_back(sf * lane(g1), n, rs[at])
            sm_o[at] = sm
            low = sm.astype(BF)
            ml_o[at] = low
            mixer += jnp.sum(low.astype(F32), 0, keepdims=True)
        vec_o[0:1] = gain
        vec_o[1:2] = bias
        vec_o[2:3] = mixer


def slope_first(s, si, wi, ss, n1, rs, g1):
    t, d = ss.shape
    ff = wi.shape[1]
    w = 1024
    return call(
        slope_first_body,
        (ff // w,),
        [cols(t, w), cols(d, w), full((t, d)), full((t, d)), full((t, 1)), whole_vec(d)],
        [full((t, d)), full((t, d)), full((3, d))],
        [shape((t, d), F32), shape((t, d), BF), shape((3, d), F32)],
        [pltpu.VMEM((t, d), F32)],
        "slope_first",
        2_400_000_000,
        14 << 20,
    )(s, si, wi, ss, n1, rs, g1)


def attn_bwd_body(s, ml, wm, q, kt, v, e, il, ctx, dq_o, dk_o, dv_o):
    t = ml.shape[0]
    dct = nt(wm[...], ml[...]).astype(BF)
    ctxt = ctx[...].T
    zero = jnp.zeros((64, t), BF)
    lanes = lax.broadcasted_iota(jnp.int32, (t, 128), 1)
    dqs = []
    for pair in range(2):
        dkp = jnp.zeros((t, 128), F32)
        dvp = dkp
        at = slice(pair * 128, pair * 128 + 128)
        vp, qp = v[:, at], q[:, at]
        for one in range(2):
            h = pair * 2 + one
            sub = slice(h * 64, h * 64 + 64)
            dc = (dct[sub].astype(F32) * il[h]).astype(BF)
            da = jnp.concatenate([dc, zero] if one == 0 else [zero, dc], 0)
            delta = jnp.sum(dc.astype(F32) * ctxt[sub].astype(F32), 0, keepdims=True)
            low = e[h]
            ds = (low.astype(F32) * (nn(vp, da) - delta)).astype(BF)
            keep = (lanes < 64) if one == 0 else (lanes >= 64)
            dkp += nn(ds, jnp.where(keep, qp, BF(0)))
            dvp += nn(low, da.T)
            dqs.append(nn(kt[sub], ds) * 0.125)
        dk_o[:, at] = dkp.astype(BF)
        dv_o[:, at] = dvp.astype(BF)
    dq_o[...] = jnp.concatenate(dqs, 0).astype(BF).T


def attn_bwd(s, ml, wm, q, kt, v, e, il, ctx):
    t, d = ml.shape
    return call(
        attn_bwd_body,
        (d // 256,),
        [
            full((t, d)),
            rows_of(256, d),
            cols(t, 256),
            rows_of(256, t),
            cols(t, 256),
            pl.BlockSpec((4, t, t), lambda g, s: (g, 0, 0)),
            pl.BlockSpec((4, 1, t), lambda g, s: (g, 0, 0)),
            cols(t, 256),
        ],
        [cols(t, 256)] * 3,
        [shape((t, d), BF)] * 3,
        [],
        "attn_bwd",
        3_600_000_000,
        15 << 20,
    )(s, ml, wm, q, kt, v, e, il, ctx)


def input_grad_body(s, dq, dk, dv, wq, wk, wv, sm, own_o, rem_o):
    half = sm.shape[0] // 2
    total = sm[...] + nt(dq[...], wq[...]) + nt(dk[...], wk[...]) + nt(dv[...], wv[...])
    own_o[0] = total[:half]
    rem_o[...] = total[half:].astype(BF)


def input_grad(s, slopes, wq, wk, wv, sm):
    t, d = sm.shape
    half = t // 2
    return call(
        input_grad_body,
        (1,),
        [full((t, d))] * 3 + [full((d, d))] * 3 + [full((t, d))],
        [own_slot(half, d), full((half, d))],
        [shape((2, half, d), F32), shape((half, d), BF)],
        [],
        "input_grad",
        1_800_000_000,
        8 << 20,
    )(s, *slopes, wq, wk, wv, sm)


XY = (("x", "y", "z1", "z2"), ("y", "x", "z1", "z2"))
XZY = (("x", "z1", "y", "z2"), ("y", "z1", "x", "z2"))


def meets(s, core, a, f):
    return jnp.where(core == 0, a, f) ^ s[3], jnp.where(core == 0, f, a) ^ s[0]


def cols_of(y):
    return pl.ds(pl.multiple_of(y * 384, 128), 384)


def outer_jobs(s, core, j, tile):
    for a in range(2):
        for f in range(2):
            x, y = meets(s, core, a, f)
            where = (a, (j & 1) ^ s[4], f, (j >> 1) ^ s[5])
            yield where, tile.at[2 * x + core, :, cols_of(y)], slice(None)


def thin_jobs(s, core, j, tile):
    for a in range(2):
        for f in range(2):
            x, y = meets(s, core, a, f)
            rows = pl.ds(pl.multiple_of((2 * x + core) * 48, 16), 48)
            yield (a, f), tile.at[:, rows, cols_of(y)], pl.ds(pl.multiple_of(j * 48, 16), 48)


def flush(s, step, tile, outs, sems, jobs_of):
    copies = []
    keep, *send = outs
    split = len(send).bit_length() - 1
    for away in range(2):
        for where, part, rows in jobs_of(s, s[2] ^ away, step, tile):
            out = keep.at[*where]
            if away:
                index = sum(i << (split - 1 - n) for n, i in enumerate(where[:split]))
                out = send[index].at[*where[split:]] if where[split:] else send[index]
            out = out.at[rows] if len(where) == 4 else out.at[:, rows]
            copies.append(pltpu.make_async_copy(part, out, sems.at[len(copies)]))
    return copies


def run_tiles(s, steps, tiles, sems, outs, fill, jobs_of):
    j = pl.program_id(0)

    def go(step, slot, wait):
        for copy in flush(s, step, tiles.at[slot], outs, sems.at[slot], jobs_of):
            copy.wait() if wait else copy.start()

    slot = lax.rem(j, 2)

    @pl.when(j >= 2)
    def _():
        go(j - 2, slot, True)

    fill(j, tiles.at[slot])
    go(j, slot, False)

    @pl.when(j == steps - 1)
    def _():
        if steps > 1:
            go(j - 1, 1 - slot, True)
        go(j, slot, True)


def outer_body(s, act, sl, keep, send, tiles, sems):
    def fill(_, tile):
        tile[...] = tn(act[...], sl[...]).astype(BF).reshape(tile.shape)

    run_tiles(s, 4, tiles, sems, (keep, send), fill, outer_jobs)


def inner_body(s, nl, si0, si1, keep, send0, send1, tiles, sems):
    def fill(_, tile):
        tile[...] = tn(nl[...], jnp.concatenate([si0[...], si1[...]], 1)).astype(BF).reshape(tile.shape)

    run_tiles(s, 4, tiles, sems, (keep, send0, send1), fill, thin_jobs)


def last_body(s, own, rem, dq, dk, dv, ctx, ml, v2, v1, bi,
              keep, send0, send1, send2, send3, vec_o, tiles, sems, xs):
    half, d = rem.shape

    def put(row, value):
        vec_o[row : row + 1] = value[:, :384]
        vec_o[12 + row : 13 + row] = value[:, 384:]

    @pl.when(pl.program_id(0) == 0)
    def _():
        xs[:half] = own[0]
        xs[half:] = rem[...]
        for i in range(3):
            put(2 + i, v2[i : i + 1])
            put(5 + i, v1[i : i + 1])
        for i in range(4):
            put(8 + i, bi[:, i * d : i * d + d])
        vec_o[24:] = jnp.zeros((8, 384), F32)

    def fill(j, tile):
        for one, part in enumerate((dq, dk, dv)):

            @pl.when(j == one)
            def _():
                tile[...] = tn(xs[...], part[...]).astype(BF).reshape(tile.shape)
                if one != 1:
                    put(one // 2, nn(jnp.ones((8, 2 * half), BF), part[...])[:1])

        @pl.when(j == 3)
        def _():
            tile[...] = tn(ctx[...], ml[...]).astype(BF).reshape(tile.shape)

    sends = (send0, send1, send2, send3)
    run_tiles(s, 4, tiles, sems, (keep, *sends), fill, thin_jobs)


def weight_call(body, in_specs, block, name, flops, scratch=(), extra=(), sends=1):
    hbm = pl.BlockSpec(memory_space=pl.ANY)
    return call(
        body,
        (4,),
        in_specs,
        [hbm] * (1 + sends) + [full(dims) for dims in extra],
        [shape(block, BF)] + [shape(block[sends.bit_length() - 1 :], BF)] * sends + [shape(dims, F32) for dims in extra],
        [pltpu.VMEM((2, 4, 192, 768), BF), pltpu.SemaphoreType.DMA((2, 8))] + list(scratch),
        name,
        flops,
        10 << 20,
    )


VECTORS = (0, 1, 7, 8, 4, 5, 6, 2, 3)


def combine_body(counts, last, s, *refs):
    n = sum(sum(chunks) for chunks in counts)
    ins, vec, vec_in, outs = list(refs[:n]), refs[n], refs[n + 1], refs[n + 2 :]
    new = vec[...] + vec_in[...].astype(F32)
    for out, chunks in zip(outs, counts):
        at = 0
        for count in chunks:
            total = sum(ins.pop(0)[...].astype(F32) for _ in range(count))
            if last:
                for j in range(4):
                    outs[j][...] = total[j * 48 : j * 48 + 48]
            else:
                out[at : at + total.shape[0]] = total.astype(BF)
            at += total.shape[0]
    if last and len(outs) == 5:
        outs[4][:, :384] = new[:12]
        outs[4][:, 384:] = new[12:24]
    elif last:
        for out, first in zip(outs[4:], VECTORS):
            for i in range(out.shape[0] // 768):
                out[i * 768 : i * 768 + 384] = new[first + i]
                out[i * 768 + 384 : i * 768 + 768] = new[12 + first + i]
    else:
        outs[0][outs[0].shape[0] - 32 :] = new.astype(BF)
        outs[-1][...] = new


def block_of(height, part, at):
    index = at if callable(at) else lambda s: at
    return part.reshape(-1, 384), pl.BlockSpec((height, 384), lambda g, s: (index(s), 0))


def total_body(s, *refs):
    *ins, out = refs
    total = sum(ref[...].astype(F32) for ref in ins)
    for i in range(4):
        out[:, i * 384 : i * 384 + 384] = total[i * 48 : i * 48 + 48]


def total_inner(s, parts):
    args, specs = zip(*(block_of(192, *part) for part in parts))
    return call(
        total_body,
        (1,),
        list(specs),
        full((48, 1536)),
        shape((48, 1536), F32),
        [],
        "total_inner",
        0,
        1 << 20,
    )(s, *args)


def combine(s, groups, vec, vec_in, last=False, apart=False):
    specs, args, outs = [], [], []
    for group in groups:
        for height, parts in group:
            for part in parts:
                value, spec = block_of(height, *part)
                args.append(value)
                specs.append(spec)
        outs.append(shape((sum(height for height, _ in group), 384), BF))
    if last:
        outs = [shape((48, 384), F32)] * 4
        outs += [shape((3072 if i == 8 else 768,), F32) for i in VECTORS] if apart else [shape((12, 768), F32)]
    else:
        outs[0] = shape((outs[0].shape[0] + 32, 384), BF)
        outs.append(shape((32, 384), F32))
    rows = vec_in.shape[0]
    return call(
        functools.partial(combine_body, [[len(parts) for _, parts in group] for group in groups], last),
        (1,),
        specs + [full((32, 384)), pl.BlockSpec((32, 384), lambda g, s: (rows // 32 - 1, 0))],
        [whole_vec(*o.shape) if len(o.shape) == 1 else full(o.shape) for o in outs],
        outs,
        [],
        "combine",
        0,
        4 << 20,
    )(s, *args, vec, vec_in)


def finish_body(s, *refs):
    *recv, _, out = refs
    at = 0
    for part in recv:
        out[0, at : at + part.shape[0]] = part[...].astype(F32)
        at += part.shape[0]


def finish(s, recv, whole):
    half, d = whole.shape[1:]
    return call(
        finish_body,
        (1,),
        [full(part.shape) for part in recv] + [pl.BlockSpec(memory_space=pl.ANY)],
        pl.BlockSpec((1, half, d), lambda g, s: (1 - s[0], 0, 0)),
        shape(whole.shape, F32),
        [],
        "finish",
        0,
        1 << 20,
        aliases={len(recv) + 1: 0},
    )(s, *recv, whole)


def local(n, tokens, cotangent, lengths, query_weight, query_bias, key_weight, value_weight, value_bias,
          mixer_weight, mixer_bias, first_gain, first_bias, inner_weight, inner_bias, outer_weight,
          outer_bias, second_gain, second_bias):
    d = tokens.shape[2]
    low_n = n // 16
    y = lax.axis_index("seq")
    dp = lax.axis_index("dp")
    hi = dp // low_n
    mine = lax.dynamic_index_in_dim(lengths, y, 0, keepdims=False)
    s = jnp.stack([y, mine, hi & 1, (hi >> 1) & 1, (hi >> 2) & 1, (hi >> 3) & 1]).astype(jnp.int32)

    def trade(value, bit):
        if bit == "y":
            return lax.ppermute(value, "seq", [(0, 1), (1, 0)])
        return lax.ppermute(value, "dp", [(i, i ^ (bit * low_n)) for i in range(n)])

    steps = {"x": 2 * low_n, "z1": 4 * low_n, "z2": 8 * low_n}

    def trade_stage(value, orders, stage):
        pairs = []
        for i in range(n):
            bit = orders[(i // low_n) % 2][stage]
            for r in range(2):
                pairs.append((2 * i + r, 2 * i + 1 - r if bit == "y" else 2 * (i ^ steps[bit]) + r))
        return lax.ppermute(value, ("dp", "seq"), pairs)

    rem = trade(lax.dynamic_index_in_dim(tokens, 1 - y, 0, keepdims=False), "y")
    cot_rem = trade(lax.dynamic_index_in_dim(cotangent, 1 - y, 0, keepdims=False), "y")

    def after(value, *others):
        return lax.optimization_barrier((value, others))[0]

    (tokens, cotangent, query_weight, query_bias, key_weight, value_weight, value_bias, mixer_weight,
     mixer_bias, first_gain, first_bias, inner_weight, inner_bias, outer_weight, outer_bias, second_gain,
     second_bias) = [
        pltpu.with_memory_space_constraint(v, pltpu.HBM)
        for v in (tokens, cotangent, query_weight, query_bias, key_weight, value_weight, value_bias,
                  mixer_weight, mixer_bias, first_gain, first_bias, inner_weight, inner_bias, outer_weight,
                  outer_bias, second_gain, second_bias)
    ]
    g1, b1, g2, b2 = first_gain, first_bias, second_gain, second_bias
    q, kt, v, e, il, ctx, n1, rs, nl = attn_fwd(
        s, tokens, rem, query_weight, key_weight, value_weight, query_bias, value_bias,
        mixer_weight, mixer_bias, g1, b1)
    act, dg, out, out0, out1, ss, sl, v2 = mlp_fwd(
        s, nl, inner_weight, inner_bias, outer_weight, outer_bias, n1, g1, b1, g2, b2,
        cotangent, cot_rem)
    t = sl.shape[0]
    half = t // 2
    piece = cols(t, 768)
    hold = full((t, d))

    def together(*values):
        return lax.optimization_barrier(values)

    class Reduce:
        def __init__(self, made, orders):
            self.keep, self.going = made
            self.orders = orders
            self.got = [self.keep]

        def total(self, index):
            return sum(a[index[max(i - 1, 0):]].astype(F32) for i, a in enumerate(self.got))

        def add(self):
            self.going = self.total((0,) * (len(self.got) - 2) + (1,)).astype(BF)

        def away(self, value):
            stage = len(self.got) - 2
            return trade(value, 1) if stage < 0 else trade_stage(value, self.orders, stage)

        def send(self):
            self.got.append(self.away(self.going))

    got0 = trade(out0, "y")
    r1 = Reduce(weight_call(outer_body, [piece, hold], (2, 2, 2, 2, 192, 384), "weight_outer", 2_400_000_000)(s, act, sl), XZY)
    r1.going, got0, out1 = together(r1.going, got0, out1)
    r1.send()
    got1 = trade(out1, "y")
    si, bi = slope_inner(after(s, r1.going), sl, outer_weight, dg)

    r1.got[-1], got1, bi = together(r1.got[-1], got1, bi)
    r1.add()
    r1.send()
    pieces = [pl.BlockSpec((t, 384), lambda g, s, y=y: (0, 4 * y + g)) for y in range(2)]
    keep, *parts = weight_call(inner_body, [hold] + pieces, (2, 2, 4, 192, 384), "weight_inner", 2_400_000_000, sends=2)(
        after(s, r1.going), nl, si, si)
    core = [trade(part, 1) for part in parts]
    sm, ml, v1 = slope_first(after(s, *parts), si, inner_weight, ss, n1, rs, g1)

    r1.got[-1], core[0], core[1], v1 = together(r1.got[-1], *core, v1)
    r1.add()
    r1.send()
    r2 = Reduce((keep, None), XY)
    r2.got.append(core[1])
    r2.going = (keep[1].astype(F32) + core[1].astype(F32)).astype(BF)
    r2.got[1] = core[0][None]
    r2.send()
    back = (mixer_weight, q, kt, v, e, il, ctx)
    slopes = attn_bwd(after(s, r1.going, r2.going), ml, *back)

    r1.got[-1], r2.got[-1], *slopes = together(r1.got[-1], r2.got[-1], *slopes)
    r1.add()
    r1.send()
    r2.add()
    r2.send()
    keep, *parts, vec = weight_call(
        last_body, [own_slot(half, d), full((half, d))] + [hold] * 5 + [full((3, d))] * 2 + [full((1, 4 * d))],
        (2, 2, 4, 192, 384), "weight_last", 2_400_000_000, [pltpu.VMEM((t, d), BF)], [(32, 384)], sends=4)(
            after(s, r1.going, r2.going), tokens, rem, *slopes, ctx, ml, v2, v1, bi)

    def at(index, *values):
        return [(value, index) for value in values]

    def of_z(far1, far2):
        return lambda s: 2 * (s[5] ^ far2) + (s[4] ^ far1)

    def far_z1(*values):
        return [(192, at(lambda s, z2=z2: 2 * z2 + (1 - s[4]), *values)) for z2 in range(2)]

    def of_z2(far2):
        return lambda s: s[5] ^ far2

    r1.got[-1], parts[2], parts[3], vec = together(r1.got[-1], parts[2], parts[3], vec)
    core = [None, None, trade(parts[2], 1), trade(parts[3], 1)]
    vec_got = trade(vec, 1)

    r1.got[-1], r2.got[-1], core[2], core[3], vec_got = together(
        r1.got[-1], r2.got[-1], core[2], core[3], vec_got)
    r3 = Reduce((keep, None), XY)
    r3.got.append(None)
    going, r2.going, r1.going, vec = combine(
        s,
        [[(768, at(2, keep) + at(0, core[2])), (768, at(3, keep) + at(0, core[3]))],
         far_z1(*r2.got), [(192, at(1, *r1.got))]],
        vec, vec_got)
    r3.got.append(r3.away(going))
    core[:2] = [trade(after(part, going), 1) for part in parts[:2]]
    r2.send()
    r1.send()
    grad, grad_rem = input_grad(after(s, going, *parts[:2]), slopes, query_weight, key_weight, value_weight, sm)

    r3.got[-1], core[0], core[1], r2.got[-1], r1.got[-1], grad_rem = together(
        r3.got[-1], core[0], core[1], r2.got[-1], r1.got[-1], grad_rem)
    going, r2.going, vec = combine(
        s,
        [[(768, at(1, keep, r3.got[-1]) + at(0, core[1]))],
         [(192, at(of_z(0, 1), *r2.got[:4]) + at(of_z2(1), r2.got[4]))]],
        vec, r3.got[-1])
    r3.got[1] = core[0]
    r3.got.append(r3.away(going))
    r2.send()
    outer = sum(u.reshape(-1, 384)[:192].astype(F32) for u in r1.got)
    out = finish(after(s, going, r2.going), (got0, got1), out)

    r3.got[-1], r2.got[-1], out, outer = together(r3.got[-1], r2.got[-1], out, outer)
    going, vec = combine(s, [far_z1(*r3.got)], vec, r3.got[-1])
    r3.got.append(r3.away(going))
    grad_got = trade(after(grad_rem, going), "y")

    going, vec = combine(
        s, [[(192, at(of_z(0, 1), *r3.got[:4]) + at(of_z2(1), r3.got[4]))]], vec, r3.got[-1])
    r3.got.append(r3.away(going))
    grad = finish(after(s, going), (grad_got,), grad)
    inner = total_inner(
        after(s, going, grad), at(of_z(0, 0), *r2.got[:4]) + at(of_z2(0), r2.got[4]) + at(0, r2.got[5]))

    r3.got[-1], grad, inner = together(r3.got[-1], grad, inner)
    apart = low_n == 1
    sums = combine(
        s, [[(192, at(of_z(0, 0), *r3.got[:4]) + at(of_z2(0), r3.got[4]) + at(0, r3.got[5]))]],
        vec, r3.got[-1], last=True, apart=apart)
    weights = [*sums[:4], inner, outer]
    if apart:
        return (out, grad, *weights, *sums[4:])
    vec = sums[4]
    step = low_n // 2
    while step >= 1:
        bit = (dp // step) % 2
        rest = []
        for w in weights:
            two = w.reshape(2, w.shape[0] // 2, w.shape[1])
            away = lax.dynamic_index_in_dim(two, 1 - bit, 0, keepdims=False)
            near = lax.dynamic_index_in_dim(two, bit, 0, keepdims=False)
            rest.append(near + lax.ppermute(away, "dp", [(i, i ^ step) for i in range(n)]))
        weights = rest
        vec = vec + lax.ppermute(vec, "dp", [(i, i ^ step) for i in range(n)])
        step //= 2
    return (out, grad, *weights, *(vec[8:].reshape(-1) if i == 8 else vec[i] for i in VECTORS))


def solution(mesh):
    split = P("dp", "seq", None)
    block = P("dp", "seq")
    n = mesh.shape["dp"]

    def run(*args):
        return local(n, *args)

    return jax.shard_map(
        run,
        mesh=mesh,
        in_specs=(split, split, P("dp")) + (P(),) * 15,
        out_specs=(split, split) + (block,) * 6 + (P(),) * 9,
        check_vma=False,
    )
```

```python
import functools
import math

import jax
import jax.numpy as jnp
from jax import lax
from jax.experimental import pallas as pl
from jax.experimental.pallas import tpu as pltpu
from jax.sharding import PartitionSpec as P

HEADS = 12
F32, BF = jnp.float32, jnp.bfloat16
NEG = -1000000000.0
GELU = math.sqrt(2.0 / math.pi)
VMEM_LIMIT = 20 << 20


def nn(a, b):
    return lax.dot_general(a, b, (((1,), (0,)), ((), ())), preferred_element_type=F32)


def nt(a, b):
    return lax.dot_general(a, b, (((1,), (1,)), ((), ())), preferred_element_type=F32)


def tn(a, b):
    return lax.dot_general(a, b, (((0,), (0,)), ((), ())), preferred_element_type=F32)


def shape(dims, dtype):
    return jax.ShapeDtypeStruct(dims, dtype)


def full(dims):
    return pl.BlockSpec(dims, lambda g, s: (0,) * len(dims))


def cols(rows, width):
    return pl.BlockSpec((rows, width), lambda g, s: (0, g))


def vec(width):
    return pl.BlockSpec((width,), lambda g, s: (g,))


def whole_vec(width):
    return pl.BlockSpec((width,), lambda g, s: (0,))


def lane(ref):
    return ref[...].reshape(1, -1)


def rows_of(height, width):
    return pl.BlockSpec((height, width), lambda g, s: (g, 0))


def own_slot(rows, width):
    return pl.BlockSpec((1, rows, width), lambda g, s: (s[0], 0, 0))


def call(body, grid, in_specs, out_specs, out_shape, scratch, name, flops, nbytes, trans=0, aliases=None, vmem=VMEM_LIMIT):
    return pl.pallas_call(
        body,
        grid_spec=pltpu.PrefetchScalarGridSpec(
            num_scalar_prefetch=1,
            grid=grid,
            in_specs=in_specs,
            out_specs=out_specs,
            scratch_shapes=scratch,
        ),
        out_shape=out_shape,
        input_output_aliases=aliases or {},
        compiler_params=pltpu.CompilerParams(vmem_limit_bytes=vmem),
        cost_estimate=pl.CostEstimate(flops=flops // 1000, bytes_accessed=nbytes // 1000, transcendentals=0),
        name=name,
    )


def attn_fwd_body(s, own, rem, wq, wk, wv, bq, bv, wm, mb, g1, b1,
                  q_o, kt_o, v_o, e_o, il_o, ctx_o, n1_o, rs_o, nl_o, xs, mask, acc):
    g = pl.program_id(0)
    half = own.shape[1]
    length = 2 * half

    @pl.when(g == 0)
    def _():
        xs[:half] = own[0]
        xs[half:] = rem[...]
        at = lax.broadcasted_iota(jnp.int32, (length, 128), 0) + s[0] * half
        at = jnp.where(at >= length, at - length, at)
        mask[...] = jnp.where(at < s[1], 0.0, NEG)

    x = xs[...]
    q = (nn(x, wq[...]) + lane(bq)).astype(BF) * BF(0.125)
    k = nn(x, wk[...]).astype(BF)
    v = (nn(x, wv[...]) + lane(bv)).astype(BF)
    q_o[...] = q
    v_o[...] = v
    qt = q.T
    kt_o[...] = k.T
    vt = v.T
    zero = jnp.zeros((64, length), BF)
    outs = []
    for h in range(4):
        pair = (h // 2) * 128
        qh = qt[h * 64 : h * 64 + 64]
        qa = jnp.concatenate([qh, zero] if h % 2 == 0 else [zero, qh], 0)
        sc = nn(k[:, pair : pair + 128], qa) + mask[:, :1]
        e = jnp.exp(sc - jnp.max(sc, 0, keepdims=True))
        il = 1.0 / jnp.sum(e, 0, keepdims=True)
        low = e.astype(BF)
        e_o[h] = low
        il_o[h] = il
        outs.append(nn(vt[h * 64 : h * 64 + 64], low) * il)
    ctx = jnp.concatenate(outs, 0).astype(BF).T
    ctx_o[...] = ctx
    part = nn(ctx, wm[...])

    @pl.when(g == 0)
    def _():
        acc[...] = part

    @pl.when(g > 0)
    def _():
        acc[...] += part

    @pl.when(g == pl.num_programs(0) - 1)
    def _():
        for i in range(4):
            at = pl.ds(i * 128, 128)
            r = acc[at] + lane(mb) + xs[at].astype(F32)
            c = r - jnp.mean(r, -1, keepdims=True)
            rs = lax.rsqrt(jnp.mean(c * c, -1, keepdims=True) + 1e-05)
            n = c * rs
            n1_o[at] = n
            rs_o[at] = rs
            nl_o[at] = (n * lane(g1) + lane(b1)).astype(BF)


def attn_fwd(s, tokens, rem, wq, wk, wv, bq, bv, wm, mb, g1, b1):
    half, d = rem.shape
    t = 2 * half
    return call(
        attn_fwd_body,
        (d // 256,),
        [own_slot(half, d), full((half, d))]
        + [cols(d, 256)] * 3
        + [vec(256)] * 2
        + [rows_of(256, d)]
        + [whole_vec(d)] * 3,
        [
            cols(t, 256),
            rows_of(256, t),
            cols(t, 256),
            pl.BlockSpec((4, t, t), lambda g, s: (g, 0, 0)),
            pl.BlockSpec((4, 1, t), lambda g, s: (g, 0, 0)),
            cols(t, 256),
            full((t, d)),
            full((t, 1)),
            full((t, d)),
        ],
        [
            shape((t, d), BF),
            shape((d, t), BF),
            shape((t, d), BF),
            shape((HEADS, t, t), BF),
            shape((HEADS, 1, t), F32),
            shape((t, d), BF),
            shape((t, d), F32),
            shape((t, 1), F32),
            shape((t, d), BF),
        ],
        [pltpu.VMEM((t, d), BF), pltpu.VMEM((t, 128), F32), pltpu.VMEM((t, d), F32)],
        "attn_fwd",
        3_200_000_000,
        18 << 20,
        3 << 20,
    )(s, tokens, rem, wq, wk, wv, bq, bv, wm, mb, g1, b1)


def gelu_both(u):
    u2 = u * u
    a = 0.5 + 0.5 * jnp.tanh(u * (GELU + (GELU * 0.044715) * u2))
    return u * a, a + (2.0 * u) * (a * (1.0 - a)) * (GELU + (3.0 * GELU * 0.044715) * u2)


def norm_back(c, n, rs):
    return rs * (c - jnp.mean(c, -1, keepdims=True) - n * jnp.mean(c * n, -1, keepdims=True))


def mlp_fwd_body(s, nl, wi, bi, wo, bo, n1, g1, b1, g2, b2, cot_own, cot_rem,
                 act_o, dg_o, out_own, rem0, rem1, ss_o, sl_o, vec_o, acc):
    j = pl.program_id(0)
    half = cot_rem.shape[0]
    u = nn(nl[...], wi[...]) + lane(bi)
    act, slope = gelu_both(u)
    act = act.astype(BF)
    act_o[...] = act
    dg_o[...] = slope.astype(BF)
    part = nn(act, wo[...])

    @pl.when(j == 0)
    def _():
        acc[...] = part

    @pl.when(j > 0)
    def _():
        acc[...] += part

    @pl.when(j == pl.num_programs(0) - 1)
    def _():
        gain = jnp.zeros((1, nl.shape[1]), F32)
        bias, outer = gain, gain
        for i in range(4):
            at = pl.ds(i * 128, 128)
            r = acc[at] + lane(bo) + (n1[at] * lane(g1) + lane(b1))
            c = r - jnp.mean(r, -1, keepdims=True)
            rs = lax.rsqrt(jnp.mean(c * c, -1, keepdims=True) + 1e-05)
            n = c * rs
            o = n * lane(g2) + lane(b2)
            if i * 128 < half:
                out_own[0, at] = o
                ct = cot_own[0, at].astype(F32)
            else:
                back = pl.ds(i * 128 - half, 128)
                (rem1 if i * 128 - half >= half // 2 else rem0)[...] = o.astype(BF)
                ct = cot_rem[back].astype(F32)
            gain += jnp.sum(ct * n, 0, keepdims=True)
            bias += jnp.sum(ct, 0, keepdims=True)
            slope2 = norm_back(ct * lane(g2), n, rs)
            ss_o[at] = slope2
            low = slope2.astype(BF)
            sl_o[at] = low
            outer += jnp.sum(low.astype(F32), 0, keepdims=True)
        vec_o[0:1] = gain
        vec_o[1:2] = bias
        vec_o[2:3] = outer


def mlp_fwd(s, nl, wi, bi, wo, bo, n1, g1, b1, g2, b2, cot, cot_rem):
    t, d = nl.shape
    ff = wi.shape[1]
    half = t // 2
    w = 1024
    return call(
        mlp_fwd_body,
        (ff // w,),
        [full((t, d)), cols(d, w), vec(w), rows_of(w, d), whole_vec(d), full((t, d))]
        + [whole_vec(d)] * 4
        + [own_slot(half, d), full((half, d))],
        [cols(t, w), cols(t, w), own_slot(half, d)] + [full((half // 2, d))] * 2 + [full((t, d)), full((t, d)), full((3, d))],
        [
            shape((t, ff), BF),
            shape((t, ff), BF),
            shape((2, half, d), F32),
            shape((half // 2, d), BF),
            shape((half // 2, d), BF),
            shape((t, d), F32),
            shape((t, d), BF),
            shape((3, d), F32),
        ],
        [pltpu.VMEM((t, d), F32)],
        "mlp_fwd",
        4_800_000_000,
        24 << 20,
        2 << 20,
        vmem=30 << 20,
    )(s, nl, wi, bi, wo, bo, n1, g1, b1, g2, b2, cot, cot_rem)


def slope_inner_body(s, sl, wo, dg, si_o, bi_o):
    si = (nt(sl[...], wo[...]) * dg[...].astype(F32)).astype(BF)
    si_o[...] = si
    bi_o[...] = jnp.sum(si.astype(F32), 0, keepdims=True)


def slope_inner(s, sl, wo, dg):
    t, d = sl.shape
    ff = wo.shape[0]
    w = 1536
    return call(
        slope_inner_body,
        (ff // w,),
        [full((t, d)), rows_of(w, d), cols(t, w)],
        [cols(t, w), cols(1, w)],
        [shape((t, ff), BF), shape((1, ff), F32)],
        [],
        "slope_inner",
        2_400_000_000,
        12 << 20,
    )(s, sl, wo, dg)


def slope_first_body(s, si, wi, ss, n1, rs, g1, sm_o, ml_o, vec_o, acc):
    j = pl.program_id(0)
    part = nt(si[...], wi[...])

    @pl.when(j == 0)
    def _():
        acc[...] = part

    @pl.when(j > 0)
    def _():
        acc[...] += part

    @pl.when(j == pl.num_programs(0) - 1)
    def _():
        gain = jnp.zeros((1, ss.shape[1]), F32)
        bias, mixer = gain, gain
        for i in range(4):
            at = pl.ds(i * 128, 128)
            sf = acc[at] + ss[at]
            n = n1[at]
            gain += jnp.sum(sf * n, 0, keepdims=True)
            bias += jnp.sum(sf, 0, keepdims=True)
            sm = norm_back(sf * lane(g1), n, rs[at])
            sm_o[at] = sm
            low = sm.astype(BF)
            ml_o[at] = low
            mixer += jnp.sum(low.astype(F32), 0, keepdims=True)
        vec_o[0:1] = gain
        vec_o[1:2] = bias
        vec_o[2:3] = mixer


def slope_first(s, si, wi, ss, n1, rs, g1):
    t, d = ss.shape
    ff = wi.shape[1]
    w = 1024
    return call(
        slope_first_body,
        (ff // w,),
        [cols(t, w), cols(d, w), full((t, d)), full((t, d)), full((t, 1)), whole_vec(d)],
        [full((t, d)), full((t, d)), full((3, d))],
        [shape((t, d), F32), shape((t, d), BF), shape((3, d), F32)],
        [pltpu.VMEM((t, d), F32)],
        "slope_first",
        2_400_000_000,
        14 << 20,
    )(s, si, wi, ss, n1, rs, g1)


def attn_bwd_body(s, ml, wm, q, kt, v, e, il, ctx, dq_o, dk_o, dv_o):
    t = ml.shape[0]
    dct = nt(wm[...], ml[...]).astype(BF)
    ctxt = ctx[...].T
    zero = jnp.zeros((64, t), BF)
    lanes = lax.broadcasted_iota(jnp.int32, (t, 128), 1)
    dqs = []
    for pair in range(2):
        dkp = jnp.zeros((t, 128), F32)
        dvp = dkp
        at = slice(pair * 128, pair * 128 + 128)
        vp, qp = v[:, at], q[:, at]
        for one in range(2):
            h = pair * 2 + one
            sub = slice(h * 64, h * 64 + 64)
            dc = (dct[sub].astype(F32) * il[h]).astype(BF)
            da = jnp.concatenate([dc, zero] if one == 0 else [zero, dc], 0)
            delta = jnp.sum(dc.astype(F32) * ctxt[sub].astype(F32), 0, keepdims=True)
            low = e[h]
            ds = (low.astype(F32) * (nn(vp, da) - delta)).astype(BF)
            keep = (lanes < 64) if one == 0 else (lanes >= 64)
            dkp += nn(ds, jnp.where(keep, qp, BF(0)))
            dvp += nn(low, da.T)
            dqs.append(nn(kt[sub], ds) * 0.125)
        dk_o[:, at] = dkp.astype(BF)
        dv_o[:, at] = dvp.astype(BF)
    dq_o[...] = jnp.concatenate(dqs, 0).astype(BF).T


def attn_bwd(s, ml, wm, q, kt, v, e, il, ctx):
    t, d = ml.shape
    return call(
        attn_bwd_body,
        (d // 256,),
        [
            full((t, d)),
            rows_of(256, d),
            cols(t, 256),
            rows_of(256, t),
            cols(t, 256),
            pl.BlockSpec((4, t, t), lambda g, s: (g, 0, 0)),
            pl.BlockSpec((4, 1, t), lambda g, s: (g, 0, 0)),
            cols(t, 256),
        ],
        [cols(t, 256)] * 3,
        [shape((t, d), BF)] * 3,
        [],
        "attn_bwd",
        3_600_000_000,
        15 << 20,
    )(s, ml, wm, q, kt, v, e, il, ctx)


def input_grad_body(s, dq, dk, dv, wq, wk, wv, sm, own_o, rem_o):
    half = sm.shape[0] // 2
    total = sm[...] + nt(dq[...], wq[...]) + nt(dk[...], wk[...]) + nt(dv[...], wv[...])
    own_o[0] = total[:half]
    rem_o[...] = total[half:].astype(BF)


def input_grad(s, slopes, wq, wk, wv, sm):
    t, d = sm.shape
    half = t // 2
    return call(
        input_grad_body,
        (1,),
        [full((t, d))] * 3 + [full((d, d))] * 3 + [full((t, d))],
        [own_slot(half, d), full((half, d))],
        [shape((2, half, d), F32), shape((half, d), BF)],
        [],
        "input_grad",
        1_800_000_000,
        8 << 20,
    )(s, *slopes, wq, wk, wv, sm)


XY = (("x", "y", "z1", "z2"), ("y", "x", "z1", "z2"))
XZY = (("x", "z1", "y", "z2"), ("y", "z1", "x", "z2"))


def meets(s, core, a, f):
    return jnp.where(core == 0, a, f) ^ s[3], jnp.where(core == 0, f, a) ^ s[0]


def cols_of(y):
    return pl.ds(pl.multiple_of(y * 384, 128), 384)


def outer_jobs(s, core, j, tile):
    for a in range(2):
        for f in range(2):
            x, y = meets(s, core, a, f)
            where = (a, (j & 1) ^ s[4], f, (j >> 1) ^ s[5])
            yield where, tile.at[2 * x + core, :, cols_of(y)], slice(None)


def thin_jobs(s, core, j, tile):
    for a in range(2):
        for f in range(2):
            x, y = meets(s, core, a, f)
            rows = pl.ds(pl.multiple_of((2 * x + core) * 48, 16), 48)
            yield (a, f), tile.at[:, rows, cols_of(y)], pl.ds(pl.multiple_of(j * 48, 16), 48)


def flush(s, step, tile, outs, sems, jobs_of):
    copies = []
    keep, *send = outs
    split = len(send).bit_length() - 1
    for away in range(2):
        for where, part, rows in jobs_of(s, s[2] ^ away, step, tile):
            out = keep.at[*where]
            if away:
                index = sum(i << (split - 1 - n) for n, i in enumerate(where[:split]))
                out = send[index].at[*where[split:]] if where[split:] else send[index]
            out = out.at[rows] if len(where) == 4 else out.at[:, rows]
            copies.append(pltpu.make_async_copy(part, out, sems.at[len(copies)]))
    return copies


def run_tiles(s, steps, tiles, sems, outs, fill, jobs_of):
    j = pl.program_id(0)

    def go(step, slot, wait):
        for copy in flush(s, step, tiles.at[slot], outs, sems.at[slot], jobs_of):
            copy.wait() if wait else copy.start()

    slot = lax.rem(j, 2)

    @pl.when(j >= 2)
    def _():
        go(j - 2, slot, True)

    fill(j, tiles.at[slot])
    go(j, slot, False)

    @pl.when(j == steps - 1)
    def _():
        if steps > 1:
            go(j - 1, 1 - slot, True)
        go(j, slot, True)


def outer_body(s, act, sl, keep, send, tiles, sems):
    def fill(_, tile):
        tile[...] = tn(act[...], sl[...]).astype(BF).reshape(tile.shape)

    run_tiles(s, 4, tiles, sems, (keep, send), fill, outer_jobs)


def inner_body(s, nl, si0, si1, keep, send0, send1, tiles, sems):
    def fill(_, tile):
        tile[...] = tn(nl[...], jnp.concatenate([si0[...], si1[...]], 1)).astype(BF).reshape(tile.shape)

    run_tiles(s, 4, tiles, sems, (keep, send0, send1), fill, thin_jobs)


def last_body(s, own, rem, dq, dk, dv, ctx, ml, v2, v1, bi,
              keep, send0, send1, send2, send3, vec_o, tiles, sems, xs):
    half, d = rem.shape

    def put(row, value):
        vec_o[row : row + 1] = value[:, :384]
        vec_o[12 + row : 13 + row] = value[:, 384:]

    @pl.when(pl.program_id(0) == 0)
    def _():
        xs[:half] = own[0]
        xs[half:] = rem[...]
        for i in range(3):
            put(2 + i, v2[i : i + 1])
            put(5 + i, v1[i : i + 1])
        for i in range(4):
            put(8 + i, bi[:, i * d : i * d + d])
        vec_o[24:] = jnp.zeros((8, 384), F32)

    def fill(j, tile):
        for one, part in enumerate((dq, dk, dv)):

            @pl.when(j == one)
            def _():
                tile[...] = tn(xs[...], part[...]).astype(BF).reshape(tile.shape)
                if one != 1:
                    put(one // 2, nn(jnp.ones((8, 2 * half), BF), part[...])[:1])

        @pl.when(j == 3)
        def _():
            tile[...] = tn(ctx[...], ml[...]).astype(BF).reshape(tile.shape)

    sends = (send0, send1, send2, send3)
    run_tiles(s, 4, tiles, sems, (keep, *sends), fill, thin_jobs)


def weight_call(body, in_specs, block, name, flops, scratch=(), extra=(), sends=1):
    hbm = pl.BlockSpec(memory_space=pl.ANY)
    return call(
        body,
        (4,),
        in_specs,
        [hbm] * (1 + sends) + [full(dims) for dims in extra],
        [shape(block, BF)] + [shape(block[sends.bit_length() - 1 :], BF)] * sends + [shape(dims, F32) for dims in extra],
        [pltpu.VMEM((2, 4, 192, 768), BF), pltpu.SemaphoreType.DMA((2, 8))] + list(scratch),
        name,
        flops,
        10 << 20,
    )


VECTORS = (0, 1, 7, 8, 4, 5, 6, 2, 3)


def combine_body(counts, last, s, *refs):
    n = sum(sum(chunks) for chunks in counts)
    ins, vec, vec_in, outs = list(refs[:n]), refs[n], refs[n + 1], refs[n + 2 :]
    new = vec[...] + vec_in[...].astype(F32)
    for out, chunks in zip(outs, counts):
        at = 0
        for count in chunks:
            total = sum(ins.pop(0)[...].astype(F32) for _ in range(count))
            if last:
                for j in range(4):
                    outs[j][...] = total[j * 48 : j * 48 + 48]
            else:
                out[at : at + total.shape[0]] = total.astype(BF)
            at += total.shape[0]
    if last and len(outs) == 5:
        outs[4][:, :384] = new[:12]
        outs[4][:, 384:] = new[12:24]
    elif last:
        for out, first in zip(outs[4:], VECTORS):
            for i in range(out.shape[0] // 768):
                out[i * 768 : i * 768 + 384] = new[first + i]
                out[i * 768 + 384 : i * 768 + 768] = new[12 + first + i]
    else:
        outs[0][outs[0].shape[0] - 32 :] = new.astype(BF)
        outs[-1][...] = new


def block_of(height, part, at):
    index = at if callable(at) else lambda s: at
    return part.reshape(-1, 384), pl.BlockSpec((height, 384), lambda g, s: (index(s), 0))


def total_body(s, *refs):
    *ins, out = refs
    total = sum(ref[...].astype(F32) for ref in ins)
    for i in range(4):
        out[:, i * 384 : i * 384 + 384] = total[i * 48 : i * 48 + 48]


def total_inner(s, parts):
    args, specs = zip(*(block_of(192, *part) for part in parts))
    return call(
        total_body,
        (1,),
        list(specs),
        full((48, 1536)),
        shape((48, 1536), F32),
        [],
        "total_inner",
        0,
        1 << 20,
    )(s, *args)


def combine(s, groups, vec, vec_in, last=False, apart=False):
    specs, args, outs = [], [], []
    for group in groups:
        for height, parts in group:
            for part in parts:
                value, spec = block_of(height, *part)
                args.append(value)
                specs.append(spec)
        outs.append(shape((sum(height for height, _ in group), 384), BF))
    if last:
        outs = [shape((48, 384), F32)] * 4
        outs += [shape((3072 if i == 8 else 768,), F32) for i in VECTORS] if apart else [shape((12, 768), F32)]
    else:
        outs[0] = shape((outs[0].shape[0] + 32, 384), BF)
        outs.append(shape((32, 384), F32))
    rows = vec_in.shape[0]
    return call(
        functools.partial(combine_body, [[len(parts) for _, parts in group] for group in groups], last),
        (1,),
        specs + [full((32, 384)), pl.BlockSpec((32, 384), lambda g, s: (rows // 32 - 1, 0))],
        [whole_vec(*o.shape) if len(o.shape) == 1 else full(o.shape) for o in outs],
        outs,
        [],
        "combine",
        0,
        4 << 20,
    )(s, *args, vec, vec_in)


def finish_body(s, recv, whole, out):
    out[0] = recv[...].astype(F32)


def finish(s, recv, whole, part=0):
    rows, d = recv.shape
    return call(
        finish_body,
        (1,),
        [full(recv.shape), pl.BlockSpec(memory_space=pl.ANY)],
        pl.BlockSpec((1, rows, d), lambda g, s: (1 - s[0], part, 0)),
        shape(whole.shape, F32),
        [],
        "finish",
        0,
        1 << 20,
        aliases={2: 0},
    )(s, recv, whole)


def local(n, tokens, cotangent, lengths, query_weight, query_bias, key_weight, value_weight, value_bias,
          mixer_weight, mixer_bias, first_gain, first_bias, inner_weight, inner_bias, outer_weight,
          outer_bias, second_gain, second_bias):
    d = tokens.shape[2]
    low_n = n // 16
    y = lax.axis_index("seq")
    dp = lax.axis_index("dp")
    hi = dp // low_n
    mine = lax.dynamic_index_in_dim(lengths, y, 0, keepdims=False)
    s = jnp.stack([y, mine, hi & 1, (hi >> 1) & 1, (hi >> 2) & 1, (hi >> 3) & 1]).astype(jnp.int32)

    def trade(value, bit):
        if bit == "y":
            return lax.ppermute(value, "seq", [(0, 1), (1, 0)])
        return lax.ppermute(value, "dp", [(i, i ^ (bit * low_n)) for i in range(n)])

    steps = {"x": 2 * low_n, "z1": 4 * low_n, "z2": 8 * low_n}

    def trade_stage(value, orders, stage):
        pairs = []
        for i in range(n):
            bit = orders[(i // low_n) % 2][stage]
            for r in range(2):
                pairs.append((2 * i + r, 2 * i + 1 - r if bit == "y" else 2 * (i ^ steps[bit]) + r))
        return lax.ppermute(value, ("dp", "seq"), pairs)

    rem = trade(lax.dynamic_index_in_dim(tokens, 1 - y, 0, keepdims=False), "y")
    cot_rem = trade(lax.dynamic_index_in_dim(cotangent, 1 - y, 0, keepdims=False), "y")

    def after(value, *others):
        return lax.optimization_barrier((value, others))[0]

    (tokens, cotangent, query_weight, query_bias, key_weight, value_weight, value_bias, mixer_weight,
     mixer_bias, first_gain, first_bias, inner_weight, inner_bias, outer_weight, outer_bias, second_gain,
     second_bias) = [
        pltpu.with_memory_space_constraint(v, pltpu.HBM)
        for v in (tokens, cotangent, query_weight, query_bias, key_weight, value_weight, value_bias,
                  mixer_weight, mixer_bias, first_gain, first_bias, inner_weight, inner_bias, outer_weight,
                  outer_bias, second_gain, second_bias)
    ]
    g1, b1, g2, b2 = first_gain, first_bias, second_gain, second_bias
    q, kt, v, e, il, ctx, n1, rs, nl = attn_fwd(
        s, tokens, rem, query_weight, key_weight, value_weight, query_bias, value_bias,
        mixer_weight, mixer_bias, g1, b1)
    act, dg, out, out0, out1, ss, sl, v2 = mlp_fwd(
        s, nl, inner_weight, inner_bias, outer_weight, outer_bias, n1, g1, b1, g2, b2,
        cotangent, cot_rem)
    t = sl.shape[0]
    half = t // 2
    piece = cols(t, 768)
    hold = full((t, d))

    def together(*values):
        return lax.optimization_barrier(values)

    class Reduce:
        def __init__(self, made, orders):
            self.keep, self.going = made
            self.orders = orders
            self.got = [self.keep]

        def total(self, index):
            return sum(a[index[max(i - 1, 0):]].astype(F32) for i, a in enumerate(self.got))

        def add(self):
            self.going = self.total((0,) * (len(self.got) - 2) + (1,)).astype(BF)

        def away(self, value):
            stage = len(self.got) - 2
            return trade(value, 1) if stage < 0 else trade_stage(value, self.orders, stage)

        def send(self):
            self.got.append(self.away(self.going))

    got0 = trade(out0, "y")
    r1 = Reduce(weight_call(outer_body, [piece, hold], (2, 2, 2, 2, 192, 384), "weight_outer", 2_400_000_000)(s, act, sl), XZY)
    r1.going, got0 = together(r1.going, got0)
    r1.send()
    si, bi = slope_inner(after(s, r1.going), sl, outer_weight, dg)

    r1.got[-1], bi = together(r1.got[-1], bi)
    r1.add()
    r1.send()
    pieces = [pl.BlockSpec((t, 384), lambda g, s, y=y: (0, 4 * y + g)) for y in range(2)]
    keep, *parts = weight_call(inner_body, [hold] + pieces, (2, 2, 4, 192, 384), "weight_inner", 2_400_000_000, sends=2)(
        after(s, r1.going), nl, si, si)
    core = [trade(part, 1) for part in parts]
    sm, ml, v1 = slope_first(after(s, *parts), si, inner_weight, ss, n1, rs, g1)

    r1.got[-1], core[0], core[1], v1 = together(r1.got[-1], *core, v1)
    r1.add()
    r1.send()
    r2 = Reduce((keep, None), XY)
    r2.got.append(core[1])
    r2.going = (keep[1].astype(F32) + core[1].astype(F32)).astype(BF)
    r2.got[1] = core[0][None]
    r2.send()
    back = (mixer_weight, q, kt, v, e, il, ctx)
    slopes = attn_bwd(after(s, r1.going, r2.going), ml, *back)

    r1.got[-1], r2.got[-1], *slopes = together(r1.got[-1], r2.got[-1], *slopes)
    r1.add()
    r1.send()
    r2.add()
    r2.send()
    keep, *parts, vec = weight_call(
        last_body, [own_slot(half, d), full((half, d))] + [hold] * 5 + [full((3, d))] * 2 + [full((1, 4 * d))],
        (2, 2, 4, 192, 384), "weight_last", 2_400_000_000, [pltpu.VMEM((t, d), BF)], [(32, 384)], sends=4)(
            after(s, r1.going, r2.going), tokens, rem, *slopes, ctx, ml, v2, v1, bi)

    def at(index, *values):
        return [(value, index) for value in values]

    def of_z(far1, far2):
        return lambda s: 2 * (s[5] ^ far2) + (s[4] ^ far1)

    def far_z1(*values):
        return [(192, at(lambda s, z2=z2: 2 * z2 + (1 - s[4]), *values)) for z2 in range(2)]

    def of_z2(far2):
        return lambda s: s[5] ^ far2

    r1.got[-1], parts[2], parts[3], vec = together(r1.got[-1], parts[2], parts[3], vec)
    core = [None, None, trade(parts[2], 1), trade(parts[3], 1)]
    vec_got = trade(vec, 1)

    r1.got[-1], r2.got[-1], core[2], core[3], vec_got = together(
        r1.got[-1], r2.got[-1], core[2], core[3], vec_got)
    r3 = Reduce((keep, None), XY)
    r3.got.append(None)
    going, r2.going, r1.going, vec = combine(
        s,
        [[(768, at(2, keep) + at(0, core[2])), (768, at(3, keep) + at(0, core[3]))],
         far_z1(*r2.got), [(192, at(1, *r1.got))]],
        vec, vec_got)
    r3.got.append(r3.away(going))
    core[:2] = [trade(after(part, going), 1) for part in parts[:2]]
    r2.send()
    r1.send()
    grad, grad_rem = input_grad(after(s, going, *parts[:2]), slopes, query_weight, key_weight, value_weight, sm)

    r3.got[-1], core[0], core[1], r2.got[-1], r1.got[-1], grad_rem = together(
        r3.got[-1], core[0], core[1], r2.got[-1], r1.got[-1], grad_rem)
    going, r2.going, vec = combine(
        s,
        [[(768, at(1, keep, r3.got[-1]) + at(0, core[1]))],
         [(192, at(of_z(0, 1), *r2.got[:4]) + at(of_z2(1), r2.got[4]))]],
        vec, r3.got[-1])
    r3.got[1] = core[0]
    r3.got.append(r3.away(going))
    r2.send()
    outer = sum(u.reshape(-1, 384)[:192].astype(F32) for u in r1.got)
    out = finish(after(s, going, r2.going), got0, out)

    r3.got[-1], r2.got[-1], out, outer = together(r3.got[-1], r2.got[-1], out, outer)
    going, vec = combine(s, [far_z1(*r3.got)], vec, r3.got[-1])
    r3.got.append(r3.away(going))
    grad_got = trade(after(grad_rem, going), "y")
    got1 = trade(after(out1, going), "y")

    going, vec = combine(
        s, [[(192, at(of_z(0, 1), *r3.got[:4]) + at(of_z2(1), r3.got[4]))]], vec, r3.got[-1])
    r3.got.append(r3.away(going))
    grad = finish(after(s, going), grad_got, grad)
    inner = total_inner(
        after(s, going, grad), at(of_z(0, 0), *r2.got[:4]) + at(of_z2(0), r2.got[4]) + at(0, r2.got[5]))

    out = finish(after(s, inner), got1, out, 1)

    r3.got[-1], grad, inner, out = together(r3.got[-1], grad, inner, out)
    apart = low_n == 1
    sums = combine(
        s, [[(192, at(of_z(0, 0), *r3.got[:4]) + at(of_z2(0), r3.got[4]) + at(0, r3.got[5]))]],
        vec, r3.got[-1], last=True, apart=apart)
    weights = [*sums[:4], inner, outer]
    if apart:
        return (out, grad, *weights, *sums[4:])
    vec = sums[4]
    step = low_n // 2
    while step >= 1:
        bit = (dp // step) % 2
        rest = []
        for w in weights:
            two = w.reshape(2, w.shape[0] // 2, w.shape[1])
            away = lax.dynamic_index_in_dim(two, 1 - bit, 0, keepdims=False)
            near = lax.dynamic_index_in_dim(two, bit, 0, keepdims=False)
            rest.append(near + lax.ppermute(away, "dp", [(i, i ^ step) for i in range(n)]))
        weights = rest
        vec = vec + lax.ppermute(vec, "dp", [(i, i ^ step) for i in range(n)])
        step //= 2
    return (out, grad, *weights, *(vec[8:].reshape(-1) if i == 8 else vec[i] for i in VECTORS))


def solution(mesh):
    split = P("dp", "seq", None)
    block = P("dp", "seq")
    n = mesh.shape["dp"]

    def run(*args):
        return local(n, *args)

    return jax.shard_map(
        run,
        mesh=mesh,
        in_specs=(split, split, P("dp")) + (P(),) * 15,
        out_specs=(split, split) + (block,) * 6 + (P(),) * 9,
        check_vma=False,
    )
```

```python
import functools
import math

import jax
import jax.numpy as jnp
from jax import lax
from jax.experimental import pallas as pl
from jax.experimental.pallas import tpu as pltpu
from jax.sharding import PartitionSpec as P

HEADS = 12
F32, BF = jnp.float32, jnp.bfloat16
NEG = -1000000000.0
GELU = math.sqrt(2.0 / math.pi)
VMEM_LIMIT = 20 << 20


def nn(a, b):
    return lax.dot_general(a, b, (((1,), (0,)), ((), ())), preferred_element_type=F32)


def nt(a, b):
    return lax.dot_general(a, b, (((1,), (1,)), ((), ())), preferred_element_type=F32)


def tn(a, b):
    return lax.dot_general(a, b, (((0,), (0,)), ((), ())), preferred_element_type=F32)


def shape(dims, dtype):
    return jax.ShapeDtypeStruct(dims, dtype)


def full(dims):
    return pl.BlockSpec(dims, lambda g, s: (0,) * len(dims))


def cols(rows, width):
    return pl.BlockSpec((rows, width), lambda g, s: (0, g))


def vec(width):
    return pl.BlockSpec((width,), lambda g, s: (g,))


def whole_vec(width):
    return pl.BlockSpec((width,), lambda g, s: (0,))


def lane(ref):
    return ref[...].reshape(1, -1)


def rows_of(height, width):
    return pl.BlockSpec((height, width), lambda g, s: (g, 0))


def own_slot(rows, width):
    return pl.BlockSpec((1, rows, width), lambda g, s: (s[0], 0, 0))


def call(body, grid, in_specs, out_specs, out_shape, scratch, name, flops, nbytes, trans=0, aliases=None, vmem=VMEM_LIMIT):
    return pl.pallas_call(
        body,
        grid_spec=pltpu.PrefetchScalarGridSpec(
            num_scalar_prefetch=1,
            grid=grid,
            in_specs=in_specs,
            out_specs=out_specs,
            scratch_shapes=scratch,
        ),
        out_shape=out_shape,
        input_output_aliases=aliases or {},
        compiler_params=pltpu.CompilerParams(vmem_limit_bytes=vmem),
        cost_estimate=pl.CostEstimate(flops=flops // 1000, bytes_accessed=nbytes // 1000, transcendentals=0),
        name=name,
    )


def attn_fwd_body(s, own, rem, wq, wk, wv, bq, bv, wm, mb, g1, b1,
                  q_o, kt_o, v_o, e_o, il_o, ctx_o, n1_o, rs_o, nl_o, xs, mask, cs, acc):
    g = pl.program_id(0)
    half = own.shape[1]
    length = 2 * half

    @pl.when(g == 0)
    def _():
        xs[:half] = own[0]
        xs[half:] = rem[...]
        at = lax.broadcasted_iota(jnp.int32, (length, 128), 0) + s[0] * half
        at = jnp.where(at >= length, at - length, at)
        mask[...] = jnp.where(at < s[1], 0.0, NEG)

    x = xs[...]
    q = (nn(x, wq[...]) + lane(bq)).astype(BF) * BF(0.125)
    k = nn(x, wk[...]).astype(BF)
    v = (nn(x, wv[...]) + lane(bv)).astype(BF)
    q_o[...] = q
    v_o[...] = v
    qt = q.T
    kt_o[...] = k.T
    vt = v.T
    zero = jnp.zeros((64, length), BF)
    outs = []
    for h in range(4):
        pair = (h // 2) * 128
        qh = qt[h * 64 : h * 64 + 64]
        qa = jnp.concatenate([qh, zero] if h % 2 == 0 else [zero, qh], 0)
        sc = nn(k[:, pair : pair + 128], qa) + mask[:, :1]
        e = jnp.exp(sc - jnp.max(sc, 0, keepdims=True))
        il = 1.0 / jnp.sum(e, 0, keepdims=True)
        low = e.astype(BF)
        e_o[h] = low
        il_o[h] = il
        outs.append(nn(vt[h * 64 : h * 64 + 64], low) * il)
    ctx = jnp.concatenate(outs, 0).astype(BF).T
    ctx_o[...] = ctx
    cs[:, pl.ds(pl.multiple_of(g * 256, 256), 256)] = ctx

    @pl.when(g == pl.num_programs(0) - 1)
    def _():
        acc[...] = nn(cs[...], wm[...])
        for i in range(4):
            at = pl.ds(i * 128, 128)
            r = acc[at] + lane(mb) + xs[at].astype(F32)
            c = r - jnp.mean(r, -1, keepdims=True)
            rs = lax.rsqrt(jnp.mean(c * c, -1, keepdims=True) + 1e-05)
            n = c * rs
            n1_o[at] = n
            rs_o[at] = rs
            nl_o[at] = (n * lane(g1) + lane(b1)).astype(BF)


def attn_fwd(s, tokens, rem, wq, wk, wv, bq, bv, wm, mb, g1, b1):
    half, d = rem.shape
    t = 2 * half
    return call(
        attn_fwd_body,
        (d // 256,),
        [own_slot(half, d), full((half, d))]
        + [cols(d, 256)] * 3
        + [vec(256)] * 2
        + [full((d, d))]
        + [whole_vec(d)] * 3,
        [
            cols(t, 256),
            rows_of(256, t),
            cols(t, 256),
            pl.BlockSpec((4, t, t), lambda g, s: (g, 0, 0)),
            pl.BlockSpec((4, 1, t), lambda g, s: (g, 0, 0)),
            cols(t, 256),
            full((t, d)),
            full((t, 1)),
            full((t, d)),
        ],
        [
            shape((t, d), BF),
            shape((d, t), BF),
            shape((t, d), BF),
            shape((HEADS, t, t), BF),
            shape((HEADS, 1, t), F32),
            shape((t, d), BF),
            shape((t, d), F32),
            shape((t, 1), F32),
            shape((t, d), BF),
        ],
        [pltpu.VMEM((t, d), BF), pltpu.VMEM((t, 128), F32), pltpu.VMEM((t, d), BF), pltpu.VMEM((t, d), F32)],
        "attn_fwd",
        3_200_000_000,
        18 << 20,
        3 << 20,
    )(s, tokens, rem, wq, wk, wv, bq, bv, wm, mb, g1, b1)


def gelu_both(u):
    u2 = u * u
    a = 0.5 + 0.5 * jnp.tanh(u * (GELU + (GELU * 0.044715) * u2))
    return u * a, a + (2.0 * u) * (a * (1.0 - a)) * (GELU + (3.0 * GELU * 0.044715) * u2)


def norm_back(c, n, rs):
    return rs * (c - jnp.mean(c, -1, keepdims=True) - n * jnp.mean(c * n, -1, keepdims=True))


def mlp_fwd_body(s, nl, wi, bi, wo, bo, n1, g1, b1, g2, b2, cot_own, cot_rem,
                 act_o, dg_o, out_own, rem0, rem1, ss_o, sl_o, vec_o, acc):
    j = pl.program_id(0)
    half = cot_rem.shape[0]
    u = nn(nl[...], wi[...]) + lane(bi)
    act, slope = gelu_both(u)
    act = act.astype(BF)
    act_o[...] = act
    dg_o[...] = slope.astype(BF)
    part = nn(act, wo[...])

    @pl.when(j == 0)
    def _():
        acc[...] = part

    @pl.when(j > 0)
    def _():
        acc[...] += part

    @pl.when(j == pl.num_programs(0) - 1)
    def _():
        gain = jnp.zeros((1, nl.shape[1]), F32)
        bias, outer = gain, gain
        for i in range(4):
            at = pl.ds(i * 128, 128)
            r = acc[at] + lane(bo) + (n1[at] * lane(g1) + lane(b1))
            c = r - jnp.mean(r, -1, keepdims=True)
            rs = lax.rsqrt(jnp.mean(c * c, -1, keepdims=True) + 1e-05)
            n = c * rs
            o = n * lane(g2) + lane(b2)
            if i * 128 < half:
                out_own[0, at] = o
                ct = cot_own[0, at].astype(F32)
            else:
                back = pl.ds(i * 128 - half, 128)
                (rem1 if i * 128 - half >= half // 2 else rem0)[...] = o.astype(BF)
                ct = cot_rem[back].astype(F32)
            gain += jnp.sum(ct * n, 0, keepdims=True)
            bias += jnp.sum(ct, 0, keepdims=True)
            slope2 = norm_back(ct * lane(g2), n, rs)
            ss_o[at] = slope2
            low = slope2.astype(BF)
            sl_o[at] = low
            outer += jnp.sum(low.astype(F32), 0, keepdims=True)
        vec_o[0:1] = gain
        vec_o[1:2] = bias
        vec_o[2:3] = outer


def mlp_fwd(s, nl, wi, bi, wo, bo, n1, g1, b1, g2, b2, cot, cot_rem):
    t, d = nl.shape
    ff = wi.shape[1]
    half = t // 2
    w = 1024
    return call(
        mlp_fwd_body,
        (ff // w,),
        [full((t, d)), cols(d, w), vec(w), rows_of(w, d), whole_vec(d), full((t, d))]
        + [whole_vec(d)] * 4
        + [own_slot(half, d), full((half, d))],
        [cols(t, w), cols(t, w), own_slot(half, d)] + [full((half // 2, d))] * 2 + [full((t, d)), full((t, d)), full((3, d))],
        [
            shape((t, ff), BF),
            shape((t, ff), BF),
            shape((2, half, d), F32),
            shape((half // 2, d), BF),
            shape((half // 2, d), BF),
            shape((t, d), F32),
            shape((t, d), BF),
            shape((3, d), F32),
        ],
        [pltpu.VMEM((t, d), F32)],
        "mlp_fwd",
        4_800_000_000,
        24 << 20,
        2 << 20,
        vmem=30 << 20,
    )(s, nl, wi, bi, wo, bo, n1, g1, b1, g2, b2, cot, cot_rem)


def slope_inner_body(s, sl, wo, dg, si_o, bi_o):
    si = (nt(sl[...], wo[...]) * dg[...].astype(F32)).astype(BF)
    si_o[...] = si
    bi_o[...] = jnp.sum(si.astype(F32), 0, keepdims=True)


def slope_inner(s, sl, wo, dg):
    t, d = sl.shape
    ff = wo.shape[0]
    w = 1536
    return call(
        slope_inner_body,
        (ff // w,),
        [full((t, d)), rows_of(w, d), cols(t, w)],
        [cols(t, w), cols(1, w)],
        [shape((t, ff), BF), shape((1, ff), F32)],
        [],
        "slope_inner",
        2_400_000_000,
        12 << 20,
    )(s, sl, wo, dg)


def slope_first_body(s, si, wi, ss, n1, rs, g1, sm_o, ml_o, vec_o, acc):
    j = pl.program_id(0)
    part = nt(si[...], wi[...])

    @pl.when(j == 0)
    def _():
        acc[...] = part

    @pl.when(j > 0)
    def _():
        acc[...] += part

    @pl.when(j == pl.num_programs(0) - 1)
    def _():
        gain = jnp.zeros((1, ss.shape[1]), F32)
        bias, mixer = gain, gain
        for i in range(4):
            at = pl.ds(i * 128, 128)
            sf = acc[at] + ss[at]
            n = n1[at]
            gain += jnp.sum(sf * n, 0, keepdims=True)
            bias += jnp.sum(sf, 0, keepdims=True)
            sm = norm_back(sf * lane(g1), n, rs[at])
            sm_o[at] = sm
            low = sm.astype(BF)
            ml_o[at] = low
            mixer += jnp.sum(low.astype(F32), 0, keepdims=True)
        vec_o[0:1] = gain
        vec_o[1:2] = bias
        vec_o[2:3] = mixer


def slope_first(s, si, wi, ss, n1, rs, g1):
    t, d = ss.shape
    ff = wi.shape[1]
    w = 1024
    return call(
        slope_first_body,
        (ff // w,),
        [cols(t, w), cols(d, w), full((t, d)), full((t, d)), full((t, 1)), whole_vec(d)],
        [full((t, d)), full((t, d)), full((3, d))],
        [shape((t, d), F32), shape((t, d), BF), shape((3, d), F32)],
        [pltpu.VMEM((t, d), F32)],
        "slope_first",
        2_400_000_000,
        14 << 20,
    )(s, si, wi, ss, n1, rs, g1)


def attn_bwd_body(s, ml, wm, q, kt, v, e, il, ctx, dq_o, dk_o, dv_o):
    t = ml.shape[0]
    dct = nt(wm[...], ml[...]).astype(BF)
    ctxt = ctx[...].T
    zero = jnp.zeros((64, t), BF)
    lanes = lax.broadcasted_iota(jnp.int32, (t, 128), 1)
    dqs = []
    for pair in range(2):
        dkp = jnp.zeros((t, 128), F32)
        dvp = dkp
        at = slice(pair * 128, pair * 128 + 128)
        vp, qp = v[:, at], q[:, at]
        for one in range(2):
            h = pair * 2 + one
            sub = slice(h * 64, h * 64 + 64)
            dc = (dct[sub].astype(F32) * il[h]).astype(BF)
            da = jnp.concatenate([dc, zero] if one == 0 else [zero, dc], 0)
            delta = jnp.sum(dc.astype(F32) * ctxt[sub].astype(F32), 0, keepdims=True)
            low = e[h]
            ds = (low.astype(F32) * (nn(vp, da) - delta)).astype(BF)
            keep = (lanes < 64) if one == 0 else (lanes >= 64)
            dkp += nn(ds, jnp.where(keep, qp, BF(0)))
            dvp += nn(low, da.T)
            dqs.append(nn(kt[sub], ds) * 0.125)
        dk_o[:, at] = dkp.astype(BF)
        dv_o[:, at] = dvp.astype(BF)
    dq_o[...] = jnp.concatenate(dqs, 0).astype(BF).T


def attn_bwd(s, ml, wm, q, kt, v, e, il, ctx):
    t, d = ml.shape
    return call(
        attn_bwd_body,
        (d // 256,),
        [
            full((t, d)),
            rows_of(256, d),
            cols(t, 256),
            rows_of(256, t),
            cols(t, 256),
            pl.BlockSpec((4, t, t), lambda g, s: (g, 0, 0)),
            pl.BlockSpec((4, 1, t), lambda g, s: (g, 0, 0)),
            cols(t, 256),
        ],
        [cols(t, 256)] * 3,
        [shape((t, d), BF)] * 3,
        [],
        "attn_bwd",
        3_600_000_000,
        15 << 20,
    )(s, ml, wm, q, kt, v, e, il, ctx)


def input_grad_body(s, dq, dk, dv, wq, wk, wv, sm, own_o, rem_o):
    half = sm.shape[0] // 2
    total = sm[...] + nt(dq[...], wq[...]) + nt(dk[...], wk[...]) + nt(dv[...], wv[...])
    own_o[0] = total[:half]
    rem_o[...] = total[half:].astype(BF)


def input_grad(s, slopes, wq, wk, wv, sm):
    t, d = sm.shape
    half = t // 2
    return call(
        input_grad_body,
        (1,),
        [full((t, d))] * 3 + [full((d, d))] * 3 + [full((t, d))],
        [own_slot(half, d), full((half, d))],
        [shape((2, half, d), F32), shape((half, d), BF)],
        [],
        "input_grad",
        1_800_000_000,
        8 << 20,
    )(s, *slopes, wq, wk, wv, sm)


XY = (("x", "y", "z1", "z2"), ("y", "x", "z1", "z2"))
XZY = (("x", "z1", "y", "z2"), ("y", "z1", "x", "z2"))


def meets(s, core, a, f):
    return jnp.where(core == 0, a, f) ^ s[3], jnp.where(core == 0, f, a) ^ s[0]


def cols_of(y):
    return pl.ds(pl.multiple_of(y * 384, 128), 384)


def outer_jobs(s, core, j, tile):
    for a in range(2):
        for f in range(2):
            x, y = meets(s, core, a, f)
            where = (a, (j & 1) ^ s[4], f, (j >> 1) ^ s[5])
            yield where, tile.at[2 * x + core, :, cols_of(y)], slice(None)


def thin_jobs(s, core, j, tile):
    for a in range(2):
        for f in range(2):
            x, y = meets(s, core, a, f)
            rows = pl.ds(pl.multiple_of((2 * x + core) * 48, 16), 48)
            yield (a, f), tile.at[:, rows, cols_of(y)], pl.ds(pl.multiple_of(j * 48, 16), 48)


def flush(s, step, tile, outs, sems, jobs_of):
    copies = []
    keep, *send = outs
    split = len(send).bit_length() - 1
    for away in range(2):
        for where, part, rows in jobs_of(s, s[2] ^ away, step, tile):
            out = keep.at[*where]
            if away:
                index = sum(i << (split - 1 - n) for n, i in enumerate(where[:split]))
                out = send[index].at[*where[split:]] if where[split:] else send[index]
            out = out.at[rows] if len(where) == 4 else out.at[:, rows]
            copies.append(pltpu.make_async_copy(part, out, sems.at[len(copies)]))
    return copies


def run_tiles(s, steps, tiles, sems, outs, fill, jobs_of):
    j = pl.program_id(0)

    def go(step, slot, wait):
        for copy in flush(s, step, tiles.at[slot], outs, sems.at[slot], jobs_of):
            copy.wait() if wait else copy.start()

    slot = lax.rem(j, 2)

    @pl.when(j >= 2)
    def _():
        go(j - 2, slot, True)

    fill(j, tiles.at[slot])
    go(j, slot, False)

    @pl.when(j == steps - 1)
    def _():
        if steps > 1:
            go(j - 1, 1 - slot, True)
        go(j, slot, True)


def outer_body(s, act, sl, keep, send, tiles, sems):
    def fill(_, tile):
        tile[...] = tn(act[...], sl[...]).astype(BF).reshape(tile.shape)

    run_tiles(s, 4, tiles, sems, (keep, send), fill, outer_jobs)


def inner_body(s, nl, si0, si1, keep, send0, send1, tiles, sems):
    def fill(_, tile):
        tile[...] = tn(nl[...], jnp.concatenate([si0[...], si1[...]], 1)).astype(BF).reshape(tile.shape)

    run_tiles(s, 4, tiles, sems, (keep, send0, send1), fill, thin_jobs)


def last_body(s, own, rem, dq, dk, dv, ctx, ml, v2, v1, bi,
              keep, send0, send1, send2, send3, vec_o, tiles, sems, xs):
    half, d = rem.shape

    def put(row, value):
        vec_o[row : row + 1] = value[:, :384]
        vec_o[12 + row : 13 + row] = value[:, 384:]

    @pl.when(pl.program_id(0) == 0)
    def _():
        xs[:half] = own[0]
        xs[half:] = rem[...]
        for i in range(3):
            put(2 + i, v2[i : i + 1])
            put(5 + i, v1[i : i + 1])
        for i in range(4):
            put(8 + i, bi[:, i * d : i * d + d])
        vec_o[24:] = jnp.zeros((8, 384), F32)

    def fill(j, tile):
        for one, part in enumerate((dq, dk, dv)):

            @pl.when(j == one)
            def _():
                tile[...] = tn(xs[...], part[...]).astype(BF).reshape(tile.shape)
                if one != 1:
                    put(one // 2, nn(jnp.ones((8, 2 * half), BF), part[...])[:1])

        @pl.when(j == 3)
        def _():
            tile[...] = tn(ctx[...], ml[...]).astype(BF).reshape(tile.shape)

    sends = (send0, send1, send2, send3)
    run_tiles(s, 4, tiles, sems, (keep, *sends), fill, thin_jobs)


def weight_call(body, in_specs, block, name, flops, scratch=(), extra=(), sends=1):
    hbm = pl.BlockSpec(memory_space=pl.ANY)
    return call(
        body,
        (4,),
        in_specs,
        [hbm] * (1 + sends) + [full(dims) for dims in extra],
        [shape(block, BF)] + [shape(block[sends.bit_length() - 1 :], BF)] * sends + [shape(dims, F32) for dims in extra],
        [pltpu.VMEM((2, 4, 192, 768), BF), pltpu.SemaphoreType.DMA((2, 8))] + list(scratch),
        name,
        flops,
        10 << 20,
    )


VECTORS = (0, 1, 7, 8, 4, 5, 6, 2, 3)


def combine_body(counts, last, s, *refs):
    n = sum(sum(chunks) for chunks in counts)
    ins, vec, vec_in, outs = list(refs[:n]), refs[n], refs[n + 1], refs[n + 2 :]
    new = vec[...] + vec_in[...].astype(F32)
    for out, chunks in zip(outs, counts):
        at = 0
        for count in chunks:
            total = sum(ins.pop(0)[...].astype(F32) for _ in range(count))
            if last:
                for j in range(4):
                    outs[j][...] = total[j * 48 : j * 48 + 48]
            else:
                out[at : at + total.shape[0]] = total.astype(BF)
            at += total.shape[0]
    if last and len(outs) == 5:
        outs[4][:, :384] = new[:12]
        outs[4][:, 384:] = new[12:24]
    elif last:
        for out, first in zip(outs[4:], VECTORS):
            for i in range(out.shape[0] // 768):
                out[i * 768 : i * 768 + 384] = new[first + i]
                out[i * 768 + 384 : i * 768 + 768] = new[12 + first + i]
    else:
        outs[0][outs[0].shape[0] - 32 :] = new.astype(BF)
        outs[-1][...] = new


def block_of(height, part, at):
    index = at if callable(at) else lambda s: at
    return part.reshape(-1, 384), pl.BlockSpec((height, 384), lambda g, s: (index(s), 0))


def total_body(s, *refs):
    *ins, out = refs
    total = sum(ref[...].astype(F32) for ref in ins)
    for i in range(4):
        out[:, i * 384 : i * 384 + 384] = total[i * 48 : i * 48 + 48]


def total_inner(s, parts):
    args, specs = zip(*(block_of(192, *part) for part in parts))
    return call(
        total_body,
        (1,),
        list(specs),
        full((48, 1536)),
        shape((48, 1536), F32),
        [],
        "total_inner",
        0,
        1 << 20,
    )(s, *args)


def combine(s, groups, vec, vec_in, last=False, apart=False):
    specs, args, outs = [], [], []
    for group in groups:
        for height, parts in group:
            for part in parts:
                value, spec = block_of(height, *part)
                args.append(value)
                specs.append(spec)
        outs.append(shape((sum(height for height, _ in group), 384), BF))
    if last:
        outs = [shape((48, 384), F32)] * 4
        outs += [shape((3072 if i == 8 else 768,), F32) for i in VECTORS] if apart else [shape((12, 768), F32)]
    else:
        outs[0] = shape((outs[0].shape[0] + 32, 384), BF)
        outs.append(shape((32, 384), F32))
    rows = vec_in.shape[0]
    return call(
        functools.partial(combine_body, [[len(parts) for _, parts in group] for group in groups], last),
        (1,),
        specs + [full((32, 384)), pl.BlockSpec((32, 384), lambda g, s: (rows // 32 - 1, 0))],
        [whole_vec(*o.shape) if len(o.shape) == 1 else full(o.shape) for o in outs],
        outs,
        [],
        "combine",
        0,
        4 << 20,
    )(s, *args, vec, vec_in)


def finish_body(s, recv, whole, out):
    out[0] = recv[...].astype(F32)


def finish(s, recv, whole, part=0):
    rows, d = recv.shape
    return call(
        finish_body,
        (1,),
        [full(recv.shape), pl.BlockSpec(memory_space=pl.ANY)],
        pl.BlockSpec((1, rows, d), lambda g, s: (1 - s[0], part, 0)),
        shape(whole.shape, F32),
        [],
        "finish",
        0,
        1 << 20,
        aliases={2: 0},
    )(s, recv, whole)


def local(n, tokens, cotangent, lengths, query_weight, query_bias, key_weight, value_weight, value_bias,
          mixer_weight, mixer_bias, first_gain, first_bias, inner_weight, inner_bias, outer_weight,
          outer_bias, second_gain, second_bias):
    d = tokens.shape[2]
    low_n = n // 16
    y = lax.axis_index("seq")
    dp = lax.axis_index("dp")
    hi = dp // low_n
    mine = lax.dynamic_index_in_dim(lengths, y, 0, keepdims=False)
    s = jnp.stack([y, mine, hi & 1, (hi >> 1) & 1, (hi >> 2) & 1, (hi >> 3) & 1]).astype(jnp.int32)

    def trade(value, bit):
        if bit == "y":
            return lax.ppermute(value, "seq", [(0, 1), (1, 0)])
        return lax.ppermute(value, "dp", [(i, i ^ (bit * low_n)) for i in range(n)])

    steps = {"x": 2 * low_n, "z1": 4 * low_n, "z2": 8 * low_n}

    def trade_stage(value, orders, stage):
        pairs = []
        for i in range(n):
            bit = orders[(i // low_n) % 2][stage]
            for r in range(2):
                pairs.append((2 * i + r, 2 * i + 1 - r if bit == "y" else 2 * (i ^ steps[bit]) + r))
        return lax.ppermute(value, ("dp", "seq"), pairs)

    rem = trade(lax.dynamic_index_in_dim(tokens, 1 - y, 0, keepdims=False), "y")
    cot_rem = trade(lax.dynamic_index_in_dim(cotangent, 1 - y, 0, keepdims=False), "y")

    def after(value, *others):
        return lax.optimization_barrier((value, others))[0]

    (tokens, cotangent, query_weight, query_bias, key_weight, value_weight, value_bias, mixer_weight,
     mixer_bias, first_gain, first_bias, inner_weight, inner_bias, outer_weight, outer_bias, second_gain,
     second_bias) = [
        pltpu.with_memory_space_constraint(v, pltpu.HBM)
        for v in (tokens, cotangent, query_weight, query_bias, key_weight, value_weight, value_bias,
                  mixer_weight, mixer_bias, first_gain, first_bias, inner_weight, inner_bias, outer_weight,
                  outer_bias, second_gain, second_bias)
    ]
    g1, b1, g2, b2 = first_gain, first_bias, second_gain, second_bias
    q, kt, v, e, il, ctx, n1, rs, nl = attn_fwd(
        s, tokens, rem, query_weight, key_weight, value_weight, query_bias, value_bias,
        mixer_weight, mixer_bias, g1, b1)
    act, dg, out, out0, out1, ss, sl, v2 = mlp_fwd(
        s, nl, inner_weight, inner_bias, outer_weight, outer_bias, n1, g1, b1, g2, b2,
        cotangent, cot_rem)
    t = sl.shape[0]
    half = t // 2
    piece = cols(t, 768)
    hold = full((t, d))

    def together(*values):
        return lax.optimization_barrier(values)

    class Reduce:
        def __init__(self, made, orders):
            self.keep, self.going = made
            self.orders = orders
            self.got = [self.keep]

        def total(self, index):
            return sum(a[index[max(i - 1, 0):]].astype(F32) for i, a in enumerate(self.got))

        def add(self):
            self.going = self.total((0,) * (len(self.got) - 2) + (1,)).astype(BF)

        def away(self, value):
            stage = len(self.got) - 2
            return trade(value, 1) if stage < 0 else trade_stage(value, self.orders, stage)

        def send(self):
            self.got.append(self.away(self.going))

    got0 = trade(out0, "y")
    r1 = Reduce(weight_call(outer_body, [piece, hold], (2, 2, 2, 2, 192, 384), "weight_outer", 2_400_000_000)(s, act, sl), XZY)
    r1.going, got0 = together(r1.going, got0)
    r1.send()
    si, bi = slope_inner(after(s, r1.going), sl, outer_weight, dg)

    r1.got[-1], bi = together(r1.got[-1], bi)
    r1.add()
    r1.send()
    pieces = [pl.BlockSpec((t, 384), lambda g, s, y=y: (0, 4 * y + g)) for y in range(2)]
    keep, *parts = weight_call(inner_body, [hold] + pieces, (2, 2, 4, 192, 384), "weight_inner", 2_400_000_000, sends=2)(
        after(s, r1.going), nl, si, si)
    core = [trade(part, 1) for part in parts]
    sm, ml, v1 = slope_first(after(s, *parts), si, inner_weight, ss, n1, rs, g1)

    r1.got[-1], core[0], core[1], v1 = together(r1.got[-1], *core, v1)
    r1.add()
    r1.send()
    r2 = Reduce((keep, None), XY)
    r2.got.append(core[1])
    r2.going = (keep[1].astype(F32) + core[1].astype(F32)).astype(BF)
    r2.got[1] = core[0][None]
    r2.send()
    back = (mixer_weight, q, kt, v, e, il, ctx)
    slopes = attn_bwd(after(s, r1.going, r2.going), ml, *back)

    r1.got[-1], r2.got[-1], *slopes = together(r1.got[-1], r2.got[-1], *slopes)
    r1.add()
    r1.send()
    r2.add()
    r2.send()
    keep, *parts, vec = weight_call(
        last_body, [own_slot(half, d), full((half, d))] + [hold] * 5 + [full((3, d))] * 2 + [full((1, 4 * d))],
        (2, 2, 4, 192, 384), "weight_last", 2_400_000_000, [pltpu.VMEM((t, d), BF)], [(32, 384)], sends=4)(
            after(s, r1.going, r2.going), tokens, rem, *slopes, ctx, ml, v2, v1, bi)

    def at(index, *values):
        return [(value, index) for value in values]

    def of_z(far1, far2):
        return lambda s: 2 * (s[5] ^ far2) + (s[4] ^ far1)

    def far_z1(*values):
        return [(192, at(lambda s, z2=z2: 2 * z2 + (1 - s[4]), *values)) for z2 in range(2)]

    def of_z2(far2):
        return lambda s: s[5] ^ far2

    r1.got[-1], parts[2], parts[3], vec = together(r1.got[-1], parts[2], parts[3], vec)
    core = [None, None, trade(parts[2], 1), trade(parts[3], 1)]
    vec_got = trade(vec, 1)

    r1.got[-1], r2.got[-1], core[2], core[3], vec_got = together(
        r1.got[-1], r2.got[-1], core[2], core[3], vec_got)
    r3 = Reduce((keep, None), XY)
    r3.got.append(None)
    going, r2.going, r1.going, vec = combine(
        s,
        [[(768, at(2, keep) + at(0, core[2])), (768, at(3, keep) + at(0, core[3]))],
         far_z1(*r2.got), [(192, at(1, *r1.got))]],
        vec, vec_got)
    r3.got.append(r3.away(going))
    core[:2] = [trade(after(part, going), 1) for part in parts[:2]]
    r2.send()
    r1.send()
    grad, grad_rem = input_grad(after(s, going, *parts[:2]), slopes, query_weight, key_weight, value_weight, sm)

    r3.got[-1], core[0], core[1], r2.got[-1], r1.got[-1], grad_rem = together(
        r3.got[-1], core[0], core[1], r2.got[-1], r1.got[-1], grad_rem)
    going, r2.going, vec = combine(
        s,
        [[(768, at(1, keep, r3.got[-1]) + at(0, core[1]))],
         [(192, at(of_z(0, 1), *r2.got[:4]) + at(of_z2(1), r2.got[4]))]],
        vec, r3.got[-1])
    r3.got[1] = core[0]
    r3.got.append(r3.away(going))
    r2.send()
    outer = sum(u.reshape(-1, 384)[:192].astype(F32) for u in r1.got)
    out = finish(after(s, going, r2.going), got0, out)

    r3.got[-1], r2.got[-1], out, outer = together(r3.got[-1], r2.got[-1], out, outer)
    going, vec = combine(s, [far_z1(*r3.got)], vec, r3.got[-1])
    r3.got.append(r3.away(going))
    grad_got = trade(after(grad_rem, going), "y")
    got1 = trade(after(out1, going), "y")

    going, vec = combine(
        s, [[(192, at(of_z(0, 1), *r3.got[:4]) + at(of_z2(1), r3.got[4]))]], vec, r3.got[-1])
    r3.got.append(r3.away(going))
    grad = finish(after(s, going), grad_got, grad)
    inner = total_inner(
        after(s, going, grad), at(of_z(0, 0), *r2.got[:4]) + at(of_z2(0), r2.got[4]) + at(0, r2.got[5]))

    out = finish(after(s, inner), got1, out, 1)

    r3.got[-1], grad, inner, out = together(r3.got[-1], grad, inner, out)
    apart = low_n == 1
    sums = combine(
        s, [[(192, at(of_z(0, 0), *r3.got[:4]) + at(of_z2(0), r3.got[4]) + at(0, r3.got[5]))]],
        vec, r3.got[-1], last=True, apart=apart)
    weights = [*sums[:4], inner, outer]
    if apart:
        return (out, grad, *weights, *sums[4:])
    vec = sums[4]
    step = low_n // 2
    while step >= 1:
        bit = (dp // step) % 2
        rest = []
        for w in weights:
            two = w.reshape(2, w.shape[0] // 2, w.shape[1])
            away = lax.dynamic_index_in_dim(two, 1 - bit, 0, keepdims=False)
            near = lax.dynamic_index_in_dim(two, bit, 0, keepdims=False)
            rest.append(near + lax.ppermute(away, "dp", [(i, i ^ step) for i in range(n)]))
        weights = rest
        vec = vec + lax.ppermute(vec, "dp", [(i, i ^ step) for i in range(n)])
        step //= 2
    return (out, grad, *weights, *(vec[8:].reshape(-1) if i == 8 else vec[i] for i in VECTORS))


def solution(mesh):
    split = P("dp", "seq", None)
    block = P("dp", "seq")
    n = mesh.shape["dp"]

    def run(*args):
        return local(n, *args)

    return jax.shard_map(
        run,
        mesh=mesh,
        in_specs=(split, split, P("dp")) + (P(),) * 15,
        out_specs=(split, split) + (block,) * 6 + (P(),) * 9,
        check_vma=False,
    )
```

```python
import functools
import math

import jax
import jax.numpy as jnp
from jax import lax
from jax.experimental import pallas as pl
from jax.experimental.pallas import tpu as pltpu
from jax.sharding import PartitionSpec as P

HEADS = 12
F32, BF = jnp.float32, jnp.bfloat16
NEG = -1000000000.0
GELU = math.sqrt(2.0 / math.pi)
VMEM_LIMIT = 20 << 20


def nn(a, b):
    return lax.dot_general(a, b, (((1,), (0,)), ((), ())), preferred_element_type=F32)


def nt(a, b):
    return lax.dot_general(a, b, (((1,), (1,)), ((), ())), preferred_element_type=F32)


def tn(a, b):
    return lax.dot_general(a, b, (((0,), (0,)), ((), ())), preferred_element_type=F32)


def shape(dims, dtype):
    return jax.ShapeDtypeStruct(dims, dtype)


def full(dims):
    return pl.BlockSpec(dims, lambda g, s: (0,) * len(dims))


def cols(rows, width):
    return pl.BlockSpec((rows, width), lambda g, s: (0, g))


def vec(width):
    return pl.BlockSpec((width,), lambda g, s: (g,))


def whole_vec(width):
    return pl.BlockSpec((width,), lambda g, s: (0,))


def lane(ref):
    return ref[...].reshape(1, -1)


def rows_of(height, width):
    return pl.BlockSpec((height, width), lambda g, s: (g, 0))


def own_slot(rows, width):
    return pl.BlockSpec((1, rows, width), lambda g, s: (s[0], 0, 0))


def call(body, grid, in_specs, out_specs, out_shape, scratch, name, flops, nbytes, trans=0, aliases=None, vmem=VMEM_LIMIT):
    return pl.pallas_call(
        body,
        grid_spec=pltpu.PrefetchScalarGridSpec(
            num_scalar_prefetch=1,
            grid=grid,
            in_specs=in_specs,
            out_specs=out_specs,
            scratch_shapes=scratch,
        ),
        out_shape=out_shape,
        input_output_aliases=aliases or {},
        compiler_params=pltpu.CompilerParams(vmem_limit_bytes=vmem),
        cost_estimate=pl.CostEstimate(flops=flops // 1000, bytes_accessed=nbytes // 1000, transcendentals=0),
        name=name,
    )


def attn_fwd_body(s, own, rem, wq, wk, wv, bq, bv, wm, mb, g1, b1,
                  q_o, kt_o, v_o, e_o, il_o, ctx_o, n1_o, rs_o, nl_o, xs, mask, cs, acc):
    g = pl.program_id(0)
    half = own.shape[1]
    length = 2 * half

    @pl.when(g == 0)
    def _():
        xs[:half] = own[0]
        xs[half:] = rem[...]
        at = lax.broadcasted_iota(jnp.int32, (length, 128), 0) + s[0] * half
        at = jnp.where(at >= length, at - length, at)
        mask[...] = jnp.where(at < s[1], 0.0, NEG)

    x = xs[...]
    q = (nn(x, wq[...]) + lane(bq)).astype(BF) * BF(0.125)
    k = nn(x, wk[...]).astype(BF)
    v = (nn(x, wv[...]) + lane(bv)).astype(BF)
    q_o[...] = q
    v_o[...] = v
    qt = q.T
    kt_o[...] = k.T
    vt = v.T
    zero = jnp.zeros((64, length), BF)
    outs = []
    for h in range(4):
        pair = (h // 2) * 128
        qh = qt[h * 64 : h * 64 + 64]
        qa = jnp.concatenate([qh, zero] if h % 2 == 0 else [zero, qh], 0)
        sc = nn(k[:, pair : pair + 128], qa) + mask[:, :1]
        e = jnp.exp(sc - jnp.max(sc, 0, keepdims=True))
        il = 1.0 / jnp.sum(e, 0, keepdims=True)
        low = e.astype(BF)
        e_o[h] = low
        il_o[h] = il
        outs.append(nn(vt[h * 64 : h * 64 + 64], low) * il)
    ctx = jnp.concatenate(outs, 0).astype(BF).T
    ctx_o[...] = ctx
    cs[:, pl.ds(pl.multiple_of(g * 256, 256), 256)] = ctx

    @pl.when(g == pl.num_programs(0) - 1)
    def _():
        acc[...] = nn(cs[...], wm[...])
        for i in range(4):
            at = pl.ds(i * 128, 128)
            r = acc[at] + lane(mb) + xs[at].astype(F32)
            c = r - jnp.mean(r, -1, keepdims=True)
            rs = lax.rsqrt(jnp.mean(c * c, -1, keepdims=True) + 1e-05)
            n = c * rs
            n1_o[at] = n
            rs_o[at] = rs
            nl_o[at] = (n * lane(g1) + lane(b1)).astype(BF)


def attn_fwd(s, tokens, rem, wq, wk, wv, bq, bv, wm, mb, g1, b1):
    half, d = rem.shape
    t = 2 * half
    return call(
        attn_fwd_body,
        (d // 256,),
        [own_slot(half, d), full((half, d))]
        + [cols(d, 256)] * 3
        + [vec(256)] * 2
        + [full((d, d))]
        + [whole_vec(d)] * 3,
        [
            cols(t, 256),
            rows_of(256, t),
            cols(t, 256),
            pl.BlockSpec((4, t, t), lambda g, s: (g, 0, 0)),
            pl.BlockSpec((4, 1, t), lambda g, s: (g, 0, 0)),
            cols(t, 256),
            full((t, d)),
            full((t, 1)),
            full((t, d)),
        ],
        [
            shape((t, d), BF),
            shape((d, t), BF),
            shape((t, d), BF),
            shape((HEADS, t, t), BF),
            shape((HEADS, 1, t), F32),
            shape((t, d), BF),
            shape((t, d), F32),
            shape((t, 1), F32),
            shape((t, d), BF),
        ],
        [pltpu.VMEM((t, d), BF), pltpu.VMEM((t, 128), F32), pltpu.VMEM((t, d), BF), pltpu.VMEM((t, d), F32)],
        "attn_fwd",
        3_200_000_000,
        18 << 20,
        3 << 20,
    )(s, tokens, rem, wq, wk, wv, bq, bv, wm, mb, g1, b1)


def gelu_both(u):
    u2 = u * u
    a = 0.5 + 0.5 * jnp.tanh(u * (GELU + (GELU * 0.044715) * u2))
    return u * a, a + (2.0 * u) * (a * (1.0 - a)) * (GELU + (3.0 * GELU * 0.044715) * u2)


def norm_back(c, n, rs):
    return rs * (c - jnp.mean(c, -1, keepdims=True) - n * jnp.mean(c * n, -1, keepdims=True))


def mlp_fwd_body(s, nl, wi, bi, wo, bo, n1, g1, b1, g2, b2, cot_own, cot_rem,
                 act_o, dg_o, out_own, rem0, rem1, ss_o, sl_o, vec_o, acc):
    j = pl.program_id(0)
    half = cot_rem.shape[0]
    u = nn(nl[...], wi[...]) + lane(bi)
    act, slope = gelu_both(u)
    act = act.astype(BF)
    act_o[...] = act
    dg_o[...] = slope.astype(BF)
    part = nn(act, wo[...])

    @pl.when(j == 0)
    def _():
        acc[...] = part

    @pl.when(j > 0)
    def _():
        acc[...] += part

    @pl.when(j == pl.num_programs(0) - 1)
    def _():
        gain = jnp.zeros((1, nl.shape[1]), F32)
        bias, outer = gain, gain
        for i in range(4):
            at = pl.ds(i * 128, 128)
            r = acc[at] + lane(bo) + (n1[at] * lane(g1) + lane(b1))
            c = r - jnp.mean(r, -1, keepdims=True)
            rs = lax.rsqrt(jnp.mean(c * c, -1, keepdims=True) + 1e-05)
            n = c * rs
            o = n * lane(g2) + lane(b2)
            if i * 128 < half:
                out_own[0, at] = o
                ct = cot_own[0, at].astype(F32)
            else:
                back = pl.ds(i * 128 - half, 128)
                (rem1 if i * 128 - half >= half // 2 else rem0)[...] = o.astype(BF)
                ct = cot_rem[back].astype(F32)
            gain += jnp.sum(ct * n, 0, keepdims=True)
            bias += jnp.sum(ct, 0, keepdims=True)
            slope2 = norm_back(ct * lane(g2), n, rs)
            ss_o[at] = slope2
            low = slope2.astype(BF)
            sl_o[at] = low
            outer += jnp.sum(low.astype(F32), 0, keepdims=True)
        vec_o[0:1] = gain
        vec_o[1:2] = bias
        vec_o[2:3] = outer


def mlp_fwd(s, nl, wi, bi, wo, bo, n1, g1, b1, g2, b2, cot, cot_rem):
    t, d = nl.shape
    ff = wi.shape[1]
    half = t // 2
    w = 1024
    return call(
        mlp_fwd_body,
        (ff // w,),
        [full((t, d)), cols(d, w), vec(w), rows_of(w, d), whole_vec(d), full((t, d))]
        + [whole_vec(d)] * 4
        + [own_slot(half, d), full((half, d))],
        [cols(t, w), cols(t, w), own_slot(half, d)] + [full((half // 2, d))] * 2 + [full((t, d)), full((t, d)), full((3, d))],
        [
            shape((t, ff), BF),
            shape((t, ff), BF),
            shape((2, half, d), F32),
            shape((half // 2, d), BF),
            shape((half // 2, d), BF),
            shape((t, d), F32),
            shape((t, d), BF),
            shape((3, d), F32),
        ],
        [pltpu.VMEM((t, d), F32)],
        "mlp_fwd",
        4_800_000_000,
        24 << 20,
        2 << 20,
        vmem=30 << 20,
    )(s, nl, wi, bi, wo, bo, n1, g1, b1, g2, b2, cot, cot_rem)


def slope_inner_body(s, sl, wo, dg, si_o, bi_o):
    si = (nt(sl[...], wo[...]) * dg[...].astype(F32)).astype(BF)
    si_o[...] = si
    bi_o[...] = jnp.sum(si.astype(F32), 0, keepdims=True)


def slope_inner(s, sl, wo, dg):
    t, d = sl.shape
    ff = wo.shape[0]
    w = 1536
    return call(
        slope_inner_body,
        (ff // w,),
        [full((t, d)), rows_of(w, d), cols(t, w)],
        [cols(t, w), cols(1, w)],
        [shape((t, ff), BF), shape((1, ff), F32)],
        [],
        "slope_inner",
        2_400_000_000,
        12 << 20,
    )(s, sl, wo, dg)


def slope_first_body(s, si, wi, ss, n1, rs, g1, sm_o, ml_o, vec_o, acc):
    j = pl.program_id(0)
    part = nt(si[...], wi[...])

    @pl.when(j == 0)
    def _():
        acc[...] = part

    @pl.when(j > 0)
    def _():
        acc[...] += part

    @pl.when(j == pl.num_programs(0) - 1)
    def _():
        gain = jnp.zeros((1, ss.shape[1]), F32)
        bias, mixer = gain, gain
        for i in range(4):
            at = pl.ds(i * 128, 128)
            sf = acc[at] + ss[at]
            n = n1[at]
            gain += jnp.sum(sf * n, 0, keepdims=True)
            bias += jnp.sum(sf, 0, keepdims=True)
            sm = norm_back(sf * lane(g1), n, rs[at])
            sm_o[at] = sm
            low = sm.astype(BF)
            ml_o[at] = low
            mixer += jnp.sum(low.astype(F32), 0, keepdims=True)
        vec_o[0:1] = gain
        vec_o[1:2] = bias
        vec_o[2:3] = mixer


def slope_first(s, si, wi, ss, n1, rs, g1):
    t, d = ss.shape
    ff = wi.shape[1]
    w = 1024
    return call(
        slope_first_body,
        (ff // w,),
        [cols(t, w), cols(d, w), full((t, d)), full((t, d)), full((t, 1)), whole_vec(d)],
        [full((t, d)), full((t, d)), full((3, d))],
        [shape((t, d), F32), shape((t, d), BF), shape((3, d), F32)],
        [pltpu.VMEM((t, d), F32)],
        "slope_first",
        2_400_000_000,
        14 << 20,
    )(s, si, wi, ss, n1, rs, g1)


def attn_bwd_body(s, ml, wm, q, kt, v, e, il, ctx, dq_o, dk_o, dv_o):
    t = ml.shape[0]
    dct = nt(wm[...], ml[...]).astype(BF)
    ctxt = ctx[...].T
    zero = jnp.zeros((64, t), BF)
    lanes = lax.broadcasted_iota(jnp.int32, (t, 128), 1)
    dqs = []
    for pair in range(2):
        dkp = jnp.zeros((t, 128), F32)
        dvp = dkp
        at = slice(pair * 128, pair * 128 + 128)
        vp, qp = v[:, at], q[:, at]
        for one in range(2):
            h = pair * 2 + one
            sub = slice(h * 64, h * 64 + 64)
            dc = (dct[sub].astype(F32) * il[h]).astype(BF)
            da = jnp.concatenate([dc, zero] if one == 0 else [zero, dc], 0)
            delta = jnp.sum(dc.astype(F32) * ctxt[sub].astype(F32), 0, keepdims=True)
            low = e[h]
            ds = (low.astype(F32) * (nn(vp, da) - delta)).astype(BF)
            keep = (lanes < 64) if one == 0 else (lanes >= 64)
            dkp += nn(ds, jnp.where(keep, qp, BF(0)))
            dvp += nn(low, da.T)
            dqs.append(nn(kt[sub], ds) * 0.125)
        dk_o[:, at] = dkp.astype(BF)
        dv_o[:, at] = dvp.astype(BF)
    dq_o[...] = jnp.concatenate(dqs, 0).astype(BF).T


def attn_bwd(s, ml, wm, q, kt, v, e, il, ctx):
    t, d = ml.shape
    return call(
        attn_bwd_body,
        (d // 256,),
        [
            full((t, d)),
            rows_of(256, d),
            cols(t, 256),
            rows_of(256, t),
            cols(t, 256),
            pl.BlockSpec((4, t, t), lambda g, s: (g, 0, 0)),
            pl.BlockSpec((4, 1, t), lambda g, s: (g, 0, 0)),
            cols(t, 256),
        ],
        [cols(t, 256)] * 3,
        [shape((t, d), BF)] * 3,
        [],
        "attn_bwd",
        3_600_000_000,
        15 << 20,
    )(s, ml, wm, q, kt, v, e, il, ctx)


def input_grad_body(s, dq, dk, dv, wq, wk, wv, sm, own_o, rem_o):
    half = sm.shape[0] // 2
    total = sm[...] + nt(dq[...], wq[...]) + nt(dk[...], wk[...]) + nt(dv[...], wv[...])
    own_o[0] = total[:half]
    rem_o[...] = total[half:].astype(BF)


def input_grad(s, slopes, wq, wk, wv, sm):
    t, d = sm.shape
    half = t // 2
    return call(
        input_grad_body,
        (1,),
        [full((t, d))] * 3 + [full((d, d))] * 3 + [full((t, d))],
        [own_slot(half, d), full((half, d))],
        [shape((2, half, d), F32), shape((half, d), BF)],
        [],
        "input_grad",
        1_800_000_000,
        8 << 20,
    )(s, *slopes, wq, wk, wv, sm)


XY = (("x", "y", "z1", "z2"), ("y", "x", "z1", "z2"))
XZY = (("x", "z1", "y", "z2"), ("y", "z1", "x", "z2"))


def meets(s, core, a, f):
    return jnp.where(core == 0, a, f) ^ s[3], jnp.where(core == 0, f, a) ^ s[0]


def cols_of(y):
    return pl.ds(pl.multiple_of(y * 384, 128), 384)


def outer_jobs(s, core, j, tile):
    for a in range(2):
        for f in range(2):
            x, y = meets(s, core, a, f)
            where = (a, (j & 1) ^ s[4], f, (j >> 1) ^ s[5])
            yield where, tile.at[2 * x + core, :, cols_of(y)], slice(None)


def thin_jobs(s, core, j, tile):
    for a in range(2):
        for f in range(2):
            x, y = meets(s, core, a, f)
            rows = pl.ds(pl.multiple_of((2 * x + core) * 48, 16), 48)
            yield (a, f), tile.at[:, rows, cols_of(y)], pl.ds(pl.multiple_of(j * 48, 16), 48)


def flush(s, step, tile, outs, sems, jobs_of):
    copies = []
    keep, *send = outs
    split = len(send).bit_length() - 1
    for away in range(2):
        for where, part, rows in jobs_of(s, s[2] ^ away, step, tile):
            out = keep.at[*where]
            if away:
                index = sum(i << (split - 1 - n) for n, i in enumerate(where[:split]))
                out = send[index].at[*where[split:]] if where[split:] else send[index]
            out = out.at[rows] if len(where) == 4 else out.at[:, rows]
            copies.append(pltpu.make_async_copy(part, out, sems.at[len(copies)]))
    return copies


def run_tiles(s, steps, tiles, sems, outs, fill, jobs_of):
    j = pl.program_id(0)

    def go(step, slot, wait):
        for copy in flush(s, step, tiles.at[slot], outs, sems.at[slot], jobs_of):
            copy.wait() if wait else copy.start()

    slot = lax.rem(j, 2)

    @pl.when(j >= 2)
    def _():
        go(j - 2, slot, True)

    fill(j, tiles.at[slot])
    go(j, slot, False)

    @pl.when(j == steps - 1)
    def _():
        if steps > 1:
            go(j - 1, 1 - slot, True)
        go(j, slot, True)


def outer_body(s, act, sl, keep, send, tiles, sems):
    def fill(_, tile):
        tile[...] = tn(act[...], sl[...]).astype(BF).reshape(tile.shape)

    run_tiles(s, 4, tiles, sems, (keep, send), fill, outer_jobs)


def inner_body(s, nl, si0, si1, keep, send0, send1, tiles, sems):
    def fill(_, tile):
        tile[...] = tn(nl[...], jnp.concatenate([si0[...], si1[...]], 1)).astype(BF).reshape(tile.shape)

    run_tiles(s, 4, tiles, sems, (keep, send0, send1), fill, thin_jobs)


def last_body(s, own, rem, dq, dk, dv, ctx, ml, v2, v1, bi,
              keep, send0, send1, send2, send3, vec_o, tiles, sems, xs):
    half, d = rem.shape

    def put(row, value):
        vec_o[row : row + 1] = value[:, :384]
        vec_o[12 + row : 13 + row] = value[:, 384:]

    @pl.when(pl.program_id(0) == 0)
    def _():
        xs[:half] = own[0]
        xs[half:] = rem[...]
        for i in range(3):
            put(2 + i, v2[i : i + 1])
            put(5 + i, v1[i : i + 1])
        for i in range(4):
            put(8 + i, bi[:, i * d : i * d + d])
        vec_o[24:] = jnp.zeros((8, 384), F32)

    def fill(j, tile):
        for one, part in enumerate((dq, dk, dv)):

            @pl.when(j == one)
            def _():
                tile[...] = tn(xs[...], part[...]).astype(BF).reshape(tile.shape)
                if one != 1:
                    put(one // 2, nn(jnp.ones((8, 2 * half), BF), part[...])[:1])

        @pl.when(j == 3)
        def _():
            tile[...] = tn(ctx[...], ml[...]).astype(BF).reshape(tile.shape)

    sends = (send0, send1, send2, send3)
    run_tiles(s, 4, tiles, sems, (keep, *sends), fill, thin_jobs)


def weight_call(body, in_specs, block, name, flops, scratch=(), extra=(), sends=1):
    hbm = pl.BlockSpec(memory_space=pl.ANY)
    return call(
        body,
        (4,),
        in_specs,
        [hbm] * (1 + sends) + [full(dims) for dims in extra],
        [shape(block, BF)] + [shape(block[sends.bit_length() - 1 :], BF)] * sends + [shape(dims, F32) for dims in extra],
        [pltpu.VMEM((2, 4, 192, 768), BF), pltpu.SemaphoreType.DMA((2, 8))] + list(scratch),
        name,
        flops,
        10 << 20,
    )


VECTORS = (0, 1, 7, 8, 4, 5, 6, 2, 3)


def combine_body(counts, last, s, *refs):
    n = sum(sum(chunks) for chunks in counts)
    ins, vec, vec_in, outs = list(refs[:n]), refs[n], refs[n + 1], refs[n + 2 :]
    new = vec[...] + vec_in[...].astype(F32)
    for out, chunks in zip(outs, counts):
        at = 0
        for count in chunks:
            total = sum(ins.pop(0)[...].astype(F32) for _ in range(count))
            if last:
                for j in range(4):
                    outs[j][...] = total[j * 48 : j * 48 + 48]
            else:
                out[at : at + total.shape[0]] = total.astype(BF)
            at += total.shape[0]
    if last and len(outs) == 5:
        outs[4][:, :384] = new[:12]
        outs[4][:, 384:] = new[12:24]
    elif last:
        for out, first in zip(outs[4:], VECTORS):
            for i in range(out.shape[0] // 768):
                out[i * 768 : i * 768 + 384] = new[first + i]
                out[i * 768 + 384 : i * 768 + 768] = new[12 + first + i]
    else:
        outs[0][outs[0].shape[0] - 32 :] = new.astype(BF)
        outs[-1][...] = new


def block_of(height, part, at):
    index = at if callable(at) else lambda s: at
    return part.reshape(-1, 384), pl.BlockSpec((height, 384), lambda g, s: (index(s), 0))


def total_body(s, *refs):
    *ins, out = refs
    total = sum(ref[...].astype(F32) for ref in ins)
    for i in range(4):
        out[:, i * 384 : i * 384 + 384] = total[i * 48 : i * 48 + 48]


def total_inner(s, parts):
    args, specs = zip(*(block_of(192, *part) for part in parts))
    return call(
        total_body,
        (1,),
        list(specs),
        full((48, 1536)),
        shape((48, 1536), F32),
        [],
        "total_inner",
        0,
        1 << 20,
    )(s, *args)


def combine(s, groups, vec, vec_in, last=False, apart=False):
    specs, args, outs = [], [], []
    for group in groups:
        for height, parts in group:
            for part in parts:
                value, spec = block_of(height, *part)
                args.append(value)
                specs.append(spec)
        outs.append(shape((sum(height for height, _ in group), 384), BF))
    if last:
        outs = [shape((48, 384), F32)] * 4
        outs += [shape((3072 if i == 8 else 768,), F32) for i in VECTORS] if apart else [shape((12, 768), F32)]
    else:
        outs[0] = shape((outs[0].shape[0] + 32, 384), BF)
        outs.append(shape((32, 384), F32))
    rows = vec_in.shape[0]
    return call(
        functools.partial(combine_body, [[len(parts) for _, parts in group] for group in groups], last),
        (1,),
        specs + [full((32, 384)), pl.BlockSpec((32, 384), lambda g, s: (rows // 32 - 1, 0))],
        [whole_vec(*o.shape) if len(o.shape) == 1 else full(o.shape) for o in outs],
        outs,
        [],
        "combine",
        0,
        4 << 20,
    )(s, *args, vec, vec_in)


def finish_body(s, recv, whole, out):
    out[0] = recv[...].astype(F32)


def finish(s, recv, whole, part=0):
    rows, d = recv.shape
    return call(
        finish_body,
        (1,),
        [full(recv.shape), pl.BlockSpec(memory_space=pl.ANY)],
        pl.BlockSpec((1, rows, d), lambda g, s: (1 - s[0], part, 0)),
        shape(whole.shape, F32),
        [],
        "finish",
        0,
        1 << 20,
        aliases={2: 0},
    )(s, recv, whole)


def local(n, tokens, cotangent, lengths, query_weight, query_bias, key_weight, value_weight, value_bias,
          mixer_weight, mixer_bias, first_gain, first_bias, inner_weight, inner_bias, outer_weight,
          outer_bias, second_gain, second_bias):
    d = tokens.shape[2]
    low_n = n // 16
    y = lax.axis_index("seq")
    dp = lax.axis_index("dp")
    hi = dp // low_n
    mine = lax.dynamic_index_in_dim(lengths, y, 0, keepdims=False)
    s = jnp.stack([y, mine, hi & 1, (hi >> 1) & 1, (hi >> 2) & 1, (hi >> 3) & 1]).astype(jnp.int32)

    def trade(value, bit):
        if bit == "y":
            return lax.ppermute(value, "seq", [(0, 1), (1, 0)])
        return lax.ppermute(value, "dp", [(i, i ^ (bit * low_n)) for i in range(n)])

    steps = {"x": 2 * low_n, "z1": 4 * low_n, "z2": 8 * low_n}

    def trade_stage(value, orders, stage):
        pairs = []
        for i in range(n):
            bit = orders[(i // low_n) % 2][stage]
            for r in range(2):
                pairs.append((2 * i + r, 2 * i + 1 - r if bit == "y" else 2 * (i ^ steps[bit]) + r))
        return lax.ppermute(value, ("dp", "seq"), pairs)

    rem = trade(lax.dynamic_index_in_dim(tokens, 1 - y, 0, keepdims=False), "y")
    cot_rem = trade(lax.dynamic_index_in_dim(cotangent, 1 - y, 0, keepdims=False), "y")

    def after(value, *others):
        return lax.optimization_barrier((value, others))[0]

    (tokens, cotangent, query_weight, query_bias, key_weight, value_weight, value_bias, mixer_weight,
     mixer_bias, first_gain, first_bias, inner_weight, inner_bias, outer_weight, outer_bias, second_gain,
     second_bias) = [
        pltpu.with_memory_space_constraint(v, pltpu.HBM)
        for v in (tokens, cotangent, query_weight, query_bias, key_weight, value_weight, value_bias,
                  mixer_weight, mixer_bias, first_gain, first_bias, inner_weight, inner_bias, outer_weight,
                  outer_bias, second_gain, second_bias)
    ]
    g1, b1, g2, b2 = first_gain, first_bias, second_gain, second_bias
    q, kt, v, e, il, ctx, n1, rs, nl = attn_fwd(
        s, tokens, rem, query_weight, key_weight, value_weight, query_bias, value_bias,
        mixer_weight, mixer_bias, g1, b1)
    act, dg, out, out0, out1, ss, sl, v2 = mlp_fwd(
        s, nl, inner_weight, inner_bias, outer_weight, outer_bias, n1, g1, b1, g2, b2,
        cotangent, cot_rem)
    t = sl.shape[0]
    half = t // 2
    piece = cols(t, 768)
    hold = full((t, d))

    def together(*values):
        return lax.optimization_barrier(values)

    class Reduce:
        def __init__(self, made, orders):
            self.keep, self.going = made
            self.orders = orders
            self.got = [self.keep]

        def total(self, index):
            return sum(a[index[max(i - 1, 0):]].astype(F32) for i, a in enumerate(self.got))

        def add(self):
            self.going = self.total((0,) * (len(self.got) - 2) + (1,)).astype(BF)

        def away(self, value):
            stage = len(self.got) - 2
            return trade(value, 1) if stage < 0 else trade_stage(value, self.orders, stage)

        def send(self):
            self.got.append(self.away(self.going))

    got0 = trade(out0, "y")
    r1 = Reduce(weight_call(outer_body, [piece, hold], (2, 2, 2, 2, 192, 384), "weight_outer", 2_400_000_000)(s, act, sl), XZY)
    r1.going, got0 = together(r1.going, got0)
    r1.send()
    si, bi = slope_inner(after(s, r1.going), sl, outer_weight, dg)

    r1.got[-1], bi = together(r1.got[-1], bi)
    r1.add()
    r1.send()
    pieces = [pl.BlockSpec((t, 384), lambda g, s, y=y: (0, 4 * y + g)) for y in range(2)]
    keep, *parts = weight_call(inner_body, [hold] + pieces, (2, 2, 4, 192, 384), "weight_inner", 2_400_000_000, sends=2)(
        after(s, r1.going), nl, si, si)
    core = [trade(part, 1) for part in parts]
    sm, ml, v1 = slope_first(after(s, *parts), si, inner_weight, ss, n1, rs, g1)

    r1.got[-1], core[0], core[1], v1 = together(r1.got[-1], *core, v1)
    r1.add()
    r1.send()
    r2 = Reduce((keep, None), XY)
    r2.got.append(core[1])
    r2.going = (keep[1].astype(F32) + core[1].astype(F32)).astype(BF)
    r2.got[1] = core[0][None]
    r2.send()
    back = (mixer_weight, q, kt, v, e, il, ctx)
    slopes = attn_bwd(after(s, r1.going, r2.going), ml, *back)

    r1.got[-1], r2.got[-1], *slopes = together(r1.got[-1], r2.got[-1], *slopes)
    r1.add()
    r1.send()
    r2.add()
    r2.send()
    keep, *parts, vec = weight_call(
        last_body, [own_slot(half, d), full((half, d))] + [hold] * 5 + [full((3, d))] * 2 + [full((1, 4 * d))],
        (2, 2, 4, 192, 384), "weight_last", 2_400_000_000, [pltpu.VMEM((t, d), BF)], [(32, 384)], sends=4)(
            after(s, r1.going, r2.going), tokens, rem, *slopes, ctx, ml, v2, v1, bi)

    def at(index, *values):
        return [(value, index) for value in values]

    def of_z(far1, far2):
        return lambda s: 2 * (s[5] ^ far2) + (s[4] ^ far1)

    def far_z1(*values):
        return [(192, at(lambda s, z2=z2: 2 * z2 + (1 - s[4]), *values)) for z2 in range(2)]

    def of_z2(far2):
        return lambda s: s[5] ^ far2

    r1.got[-1], parts[2], parts[3], vec = together(r1.got[-1], parts[2], parts[3], vec)
    core = [None, None, trade(parts[2], 1), trade(parts[3], 1)]
    vec_got = trade(vec, 1)

    r1.got[-1], r2.got[-1], core[2], core[3], vec_got = together(
        r1.got[-1], r2.got[-1], core[2], core[3], vec_got)
    r3 = Reduce((keep, None), XY)
    r3.got.append(None)
    going, r2.going, r1.going, vec = combine(
        s,
        [[(768, at(2, keep) + at(0, core[2])), (768, at(3, keep) + at(0, core[3]))],
         far_z1(*r2.got), [(192, at(1, *r1.got))]],
        vec, vec_got)
    r3.got.append(r3.away(going))
    core[:2] = [trade(after(part, going), 1) for part in parts[:2]]
    r2.send()
    r1.send()
    grad, grad_rem = input_grad(after(s, going, *parts[:2]), slopes, query_weight, key_weight, value_weight, sm)

    r3.got[-1], core[0], core[1], r2.got[-1], r1.got[-1], grad_rem = together(
        r3.got[-1], core[0], core[1], r2.got[-1], r1.got[-1], grad_rem)
    going, r2.going, vec = combine(
        s,
        [[(768, at(1, keep, r3.got[-1]) + at(0, core[1]))],
         [(192, at(of_z(0, 1), *r2.got[:4]) + at(of_z2(1), r2.got[4]))]],
        vec, r3.got[-1])
    r3.got[1] = core[0]
    r3.got.append(r3.away(going))
    r2.send()
    outer = sum(u.reshape(-1, 384)[:192].astype(F32) for u in r1.got)
    out = finish(after(s, going, r2.going), got0, out)

    r3.got[-1], r2.got[-1], out, outer = together(r3.got[-1], r2.got[-1], out, outer)
    going, vec = combine(s, [far_z1(*r3.got)], vec, r3.got[-1])
    r3.got.append(r3.away(going))
    grad_got = trade(after(grad_rem, going), "y")
    got1 = trade(after(out1, going), "y")
    inner = total_inner(
        after(s, going), at(of_z(0, 0), *r2.got[:4]) + at(of_z2(0), r2.got[4]) + at(0, r2.got[5]))

    r3.got[-1], inner = together(r3.got[-1], inner)

    going, vec = combine(
        s, [[(192, at(of_z(0, 1), *r3.got[:4]) + at(of_z2(1), r3.got[4]))]], vec, r3.got[-1])
    r3.got.append(r3.away(going))
    grad = finish(after(s, going), grad_got, grad)
    out = finish(after(s, grad), got1, out, 1)

    r3.got[-1], grad, out = together(r3.got[-1], grad, out)
    apart = low_n == 1
    sums = combine(
        s, [[(192, at(of_z(0, 0), *r3.got[:4]) + at(of_z2(0), r3.got[4]) + at(0, r3.got[5]))]],
        vec, r3.got[-1], last=True, apart=apart)
    weights = [*sums[:4], inner, outer]
    if apart:
        return (out, grad, *weights, *sums[4:])
    vec = sums[4]
    step = low_n // 2
    while step >= 1:
        bit = (dp // step) % 2
        rest = []
        for w in weights:
            two = w.reshape(2, w.shape[0] // 2, w.shape[1])
            away = lax.dynamic_index_in_dim(two, 1 - bit, 0, keepdims=False)
            near = lax.dynamic_index_in_dim(two, bit, 0, keepdims=False)
            rest.append(near + lax.ppermute(away, "dp", [(i, i ^ step) for i in range(n)]))
        weights = rest
        vec = vec + lax.ppermute(vec, "dp", [(i, i ^ step) for i in range(n)])
        step //= 2
    return (out, grad, *weights, *(vec[8:].reshape(-1) if i == 8 else vec[i] for i in VECTORS))


def solution(mesh):
    split = P("dp", "seq", None)
    block = P("dp", "seq")
    n = mesh.shape["dp"]

    def run(*args):
        return local(n, *args)

    return jax.shard_map(
        run,
        mesh=mesh,
        in_specs=(split, split, P("dp")) + (P(),) * 15,
        out_specs=(split, split) + (block,) * 6 + (P(),) * 9,
        check_vma=False,
    )
```
